32 devices in a mesh: dp: 8 (over y, x, core), tp: 4 (over z).
Axes of the slice: x: 2, y: 2, z: 4, core: 2. Of those that a mesh axis runs over, the one named last changes fastest.
Arguments:
- patches: bfloat16 [19200, 768], P(('dp', 'tp')), may hold values from -6 to 6
- page_mask: int32 [19200], P(('dp', 'tp')), may hold values 0 or 1
- pair_index: int32 [200, 200], replicated, may hold values from 0 to 731
- mask_embed: float32 [768], replicated, may hold values from -6 to 6
- first_gain: float32 [768], replicated, may hold values from 0.5 to 1.5
- first_shift: float32 [768], replicated, may hold values from -3 to 3
- project_weight: bfloat16 [768, 3, 768], P(None, None, 'tp'), may hold values from -0.21875 to 0.21875
- project_bias: bfloat16 [2, 768], P(None, 'tp'), may hold values from -3 to 3
- pair_table: bfloat16 [732, 12], P(None, 'tp'), may hold values from -6 to 6
- output_weight: bfloat16 [768, 768], P('tp'), may hold values from -1.25 to 1.25
- output_bias: float32 [768], replicated, may hold values from -3 to 3
- attention_scale: float32 [768], replicated, may hold values from 0.25 to 1.75
- second_gain: float32 [768], replicated, may hold values from 0.5 to 1.5
- second_shift: float32 [768], replicated, may hold values from -3 to 3
- up_weight: bfloat16 [768, 3072], P(None, 'tp'), may hold values from -0.21875 to 0.21875
- up_bias: bfloat16 [3072], P('tp'), may hold values from -3 to 3
- down_weight: bfloat16 [3072, 768], P('tp'), may hold values from -0.109375 to 0.109375
- down_bias: float32 [768], replicated, may hold values from -3 to 3
- feed_scale: float32 [768], replicated, may hold values from 0.25 to 1.75
- cotangent: bfloat16 [19200, 768], P(('dp', 'tp')), may hold values from -6 to 6
Outputs:
- layer_output: float32 [19200, 768], P(('dp', 'tp'))
- patch_gradient: float32 [19200, 768], P(('dp', 'tp'))
- embed_gradient: float32 [768], replicated
- first_gain_gradient: float32 [768], replicated
- first_shift_gradient: float32 [768], replicated
- project_weight_gradient: float32 [768, 3, 768], P(None, None, 'tp')
- project_bias_gradient: float32 [2, 768], P(None, 'tp')
- pair_table_gradient: float32 [732, 12], P(None, 'tp')
- output_weight_gradient: float32 [768, 768], P('tp')
- output_bias_gradient: float32 [768], replicated
- attention_scale_gradient: float32 [768], replicated
- second_gain_gradient: float32 [768], replicated
- second_shift_gradient: float32 [768], replicated
- up_weight_gradient: float32 [768, 3072], P(None, 'tp')
- up_bias_gradient: float32 [3072], P('tp')
- down_weight_gradient: float32 [3072, 768], P('tp')
- down_bias_gradient: float32 [768], replicated
- feed_scale_gradient: float32 [768], replicated
The draws below stay inside these ranges and needn't reach their ends.
Inputs may be any that keep to these rules, and one draw needn't show every extreme that they name: `page_mask`: read only for patches; the class token and padding are never hidden.
All inputs are finite; a program needn't handle non-finite values. No bound on the sum of `page_mask` on one device may be relied on, other than what follows from the above.
Results may differ from the reference program's by a relative error of at most 0.015.
Values may be sent and summed in bfloat16 or wider, within the bound.
A program may use at most 128 MiB of HBM per device.

```python
import jax
import jax.numpy as jnp
from jax import lax

D = 768
H = 12
HEAD = 64
FF = 3072
SEQ = 200
PATCHES = 196
NUM_REL = 732
PAGES = 96
TOKENS = 19200


def touch_ends(result, stream_key, least, high):
    index_at = [jax.random.randint(jax.random.fold_in(stream_key, axis), (), 0, length) for axis, length in enumerate(result.shape)]
    longest = result.shape.index(max(result.shape))
    neighbour = index_at[:longest] + [(index_at[longest] + 1) % result.shape[longest]] + index_at[longest + 1:]
    return result.at[tuple(index_at)].set(least).at[tuple(neighbour)].set(high)


def levels(stream_key, shape, pieces, low, top_value):
    loudness, own = 1.0, jax.random.fold_in(stream_key, 6)
    for axis_at, parts in pieces:
        heights = jnp.exp(jax.random.uniform(jax.random.fold_in(own, axis_at), (parts,), jnp.float32, low / len(pieces), top_value / len(pieces)))
        loudness = loudness * jnp.repeat(heights, shape[axis_at] // parts).reshape([-1 if axis == axis_at else 1 for axis in range(len(shape))])
    return loudness


def bell_draw(own_key, shape, deviation, most, cuts=(), kind=jnp.bfloat16):
    values = jax.random.normal(own_key, shape, jnp.float32) * deviation
    if len(cuts) > 0:
        values = levels(own_key, shape, cuts, -0.22, 0.18) * values
    return jnp.clip(values, min=-most, max=most).astype(kind)


def setup_inputs(seed: int = 0) -> dict:
    streams_of = jax.random.split(jax.random.key(seed), 21)
    return {
        "patches": bell_draw(streams_of[0], (TOKENS, D), 1.0, 6.0, ((0, 32),)),
        "page_mask": touch_ends((jax.random.randint(streams_of[1], (TOKENS,), 0, 5) < 2).astype(jnp.int32), jax.random.fold_in(streams_of[1], 1), 0, 1),
        "pair_index": touch_ends(jax.random.randint(streams_of[2], (SEQ, SEQ), 0, NUM_REL), jax.random.fold_in(streams_of[2], 1), 0, NUM_REL - 1).astype(jnp.int32),
        "mask_embed": bell_draw(streams_of[3], (D,), 1.0, 6.0, (), jnp.float32),
        "first_gain": jnp.clip(1.0 + 0.1 * jax.random.normal(streams_of[4], (D,), jnp.float32), 0.5, 1.5),
        "first_shift": bell_draw(streams_of[5], (D,), 0.5, 3.0, (), jnp.float32),
        "project_weight": bell_draw(streams_of[6], (D, 3, D), D ** -0.5, 0.21875, ((2, 4),)),
        "project_bias": bell_draw(streams_of[7], (2, D), 0.5, 3.0, ((1, 4),)),
        "pair_table": bell_draw(streams_of[8], (NUM_REL, H), 1.0, 6.0, ((1, 4),)),
        "output_weight": bell_draw(streams_of[9], (D, D), (D // 32) ** -0.5, 1.25, ((0, 4),)),
        "output_bias": bell_draw(streams_of[10], (D,), 0.5, 3.0, (), jnp.float32),
        "attention_scale": jnp.clip(1.0 + 0.15 * jax.random.normal(streams_of[11], (D,), jnp.float32), 0.25, 1.75),
        "second_gain": jnp.clip(1.0 + 0.1 * jax.random.normal(streams_of[12], (D,), jnp.float32), 0.5, 1.5),
        "second_shift": bell_draw(streams_of[13], (D,), 0.5, 3.0, (), jnp.float32),
        "up_weight": bell_draw(streams_of[14], (D, FF), D ** -0.5, 0.21875, ((1, 4),)),
        "up_bias": bell_draw(streams_of[15], (FF,), 0.5, 3.0, ((0, 4),)),
        "down_weight": bell_draw(streams_of[16], (FF, D), FF ** -0.5, 0.109375, ((0, 4),)),
        "down_bias": bell_draw(streams_of[17], (D,), 0.5, 3.0, (), jnp.float32),
        "feed_scale": jnp.clip(1.0 + 0.15 * jax.random.normal(streams_of[18], (D,), jnp.float32), 0.25, 1.75),
        "cotangent": bell_draw(streams_of[19], (TOKENS, D), 1.0, 6.0, ((0, 32),)),
    }


@jax.custom_vjp
def low(v):
    return lax.optimization_barrier(v.astype(jnp.bfloat16)).astype(jnp.float32)

@jax.custom_vjp
def low_back(v):
    return v

def low_keep(v):
    return (low(v), None)

def low_pass(kept, grad):
    return (grad,)

def back_keep(v):
    return (v, None)

def back_low(kept, grad):
    return (low(grad),)
low.defvjp(low_keep, low_pass)
low_back.defvjp(back_keep, back_low)

def dense(left, right):
    return jnp.dot(left, right, precision=lax.Precision.HIGHEST)

def layer_norm(features, weighting, offset):
    center = features - lax.optimization_barrier(jnp.mean(features, axis=-1, keepdims=True))
    spread = lax.optimization_barrier(jnp.mean(center * center, axis=-1, keepdims=True))
    return center * lax.rsqrt(spread + 1e-06) * weighting + offset

def page_block(page_count):
    return max((candidate for candidate in range(1, 9) if page_count % candidate == 0))

def attend_pages(block_data, pair_bias, key_live):
    query_part, key_part, value_part = block_data
    scores = jnp.einsum('pqhd,pkhd->phqk', query_part, key_part, precision=lax.Precision.HIGHEST) + pair_bias[None]
    scores = low_back(jnp.where(key_live, scores, -1000000000.0))
    probs = jax.nn.softmax(scores, axis=-1)
    return jnp.einsum('phqk,pkhd->pqhd', low(probs), value_part, precision=lax.Precision.HIGHEST)

def layer_forward(params, hidden, pair_index):
    patches, mask_embed, first_gain, first_shift, project_weight, project_bias, pair_table, output_weight, output_bias, attention_scale, second_gain, second_shift, up_weight, up_bias, down_weight, down_bias, feed_scale = params
    entered = jnp.where(hidden[:, None], mask_embed[None, :], patches)
    first_low = low(layer_norm(entered, first_gain, first_shift))
    zero_row = jnp.zeros_like(project_bias[0])
    project = dense(first_low, project_weight.reshape(D, 3 * D)).reshape(TOKENS, 3, D)
    project = low_back(project + jnp.stack([project_bias[0], zero_row, project_bias[1]])[None])
    block_pages = page_block(PAGES)

    def to_blocks(array):
        return array.reshape(PAGES // block_pages, block_pages, SEQ, H, HEAD)
    query_rows = to_blocks(low(project[:, 0] * HEAD ** (-0.5)))
    key_rows = to_blocks(low(project[:, 1]))
    value_rows = to_blocks(low(project[:, 2]))
    pair_bias = jnp.transpose(jnp.take(pair_table, pair_index, axis=0), (2, 0, 1))
    key_live = (jnp.arange(SEQ) <= PATCHES)[None, None, None, :]

    def attend(block_data):
        return attend_pages(block_data, pair_bias, key_live)
    attended = lax.map(jax.checkpoint(attend), (query_rows, key_rows, value_rows)).reshape(TOKENS, D)
    attended = low(low_back(attended))
    attention_branch = low_back(dense(attended, output_weight)) + output_bias
    middle = entered + attention_scale * attention_branch
    second_low = low(layer_norm(middle, second_gain, second_shift))
    hidden_pre = low_back(dense(second_low, up_weight) + up_bias)
    hidden_low = low(jax.nn.gelu(hidden_pre, approximate=False))
    feed_branch = low_back(dense(hidden_low, down_weight)) + down_bias
    return middle + feed_scale * feed_branch

def reference(patches, page_mask, pair_index, mask_embed, first_gain, first_shift, project_weight, project_bias, pair_table, output_weight, output_bias, attention_scale, second_gain, second_shift, up_weight, up_bias, down_weight, down_bias, feed_scale, cotangent):
    position = jnp.arange(TOKENS) % SEQ
    hidden = (page_mask > 0) & (position >= 1) & (position <= PATCHES)
    floats = tuple((array.astype(jnp.float32) for array in (patches, mask_embed, first_gain, first_shift, project_weight, project_bias, pair_table, output_weight, output_bias, attention_scale, second_gain, second_shift, up_weight, up_bias, down_weight, down_bias, feed_scale)))

    def forward_fn(*params):
        return layer_forward(params, hidden, pair_index)
    layer_output, pull_back = jax.vjp(forward_fn, *floats)
    patch_gradient, embed_gradient, first_gain_gradient, first_shift_gradient, project_weight_gradient, project_bias_gradient, pair_table_gradient, output_weight_gradient, output_bias_gradient, attention_scale_gradient, second_gain_gradient, second_shift_gradient, up_weight_gradient, up_bias_gradient, down_weight_gradient, down_bias_gradient, feed_scale_gradient = pull_back(cotangent.astype(jnp.float32))
    return (layer_output, patch_gradient, embed_gradient, first_gain_gradient, first_shift_gradient, project_weight_gradient, project_bias_gradient, pair_table_gradient, output_weight_gradient, output_bias_gradient, attention_scale_gradient, second_gain_gradient, second_shift_gradient, up_weight_gradient, up_bias_gradient, down_weight_gradient, down_bias_gradient, feed_scale_gradient)
```

```python
import functools

import jax
import jax.numpy as jnp
from jax import lax
from jax.experimental import pallas as pl
from jax.experimental.pallas import tpu as pltpu
from jax.sharding import PartitionSpec as P

SEQ = 200
PATCHES = 196
NUM_REL = 732
PAGES = 3
HEADS = 12
WIDTH = 768
GROUP = 8
SLICE = 96
HALF = 48
MESH = pl.DeviceIdType.MESH


class Place:
    def __init__(self, tp_size):
        self.tp_size = tp_size
        self.dp = lax.axis_index("dp")
        self.t = lax.axis_index("tp")
        self.d = lax.rem(self.dp, GROUP)
        self.core = lax.rem(self.d, 2)
        self.x = lax.rem(self.d // 2, 2)
        self.y = self.d // 4
        self.to_core = (self.dp + 1 - 2 * self.core, self.t)
        self.to_x = (self.dp + 2 - 4 * self.x, self.t)
        self.to_y = (self.dp + 4 - 8 * self.y, self.t)
        self.d_x = self.d + 2 - 4 * self.x
        self.d_y = self.d + 4 - 8 * self.y
        self.d_xy = self.d_x + 4 - 8 * self.y

    def core_of(self, d):
        return d + 1 - 2 * self.core

    def to_z(self, offset):
        return (self.dp, lax.rem(self.t + offset, self.tp_size))

    def from_z(self, offset):
        return lax.rem(self.t + self.tp_size - offset, self.tp_size)


def meet(place):
    barrier = pltpu.get_barrier_semaphore()
    others = [place.to_core, place.to_x, place.to_y]
    others += [place.to_z(offset) for offset in range(1, place.tp_size)]
    for other in others:
        pl.semaphore_signal(barrier, inc=1, device_id=other, device_id_type=MESH)
    pl.semaphore_wait(barrier, len(others))


def send(src, dst, send_sem, recv_sem, device):
    return pltpu.make_async_remote_copy(
        src_ref=src,
        dst_ref=dst,
        send_sem=send_sem,
        recv_sem=recv_sem,
        device_id=device,
        device_id_type=MESH,
    )


def slice_row(kind, t, d):
    if kind == 0:
        row = (d // 2) * 768 + t * 192 + lax.rem(d, 2) * SLICE
    else:
        row = t * 768 + d * SLICE
    return pl.multiple_of(row, 16)


LOW = jnp.bfloat16
F32 = jnp.float32
CHUNKS = ((0, 48), (48, 48), (96, 48), (144, 56))
TILE = 256
NT = (((1,), (1,)), ((), ()))
NN = (((1,), (0,)), ((), ()))
TN = (((0,), (0,)), ((), ()))
EMBED, GAIN_1, SHIFT_1, OUT_BIAS, ATT_SCALE, GAIN_2, SHIFT_2, DOWN_BIAS, FEED_SCALE = range(9)
Q_BIAS, V_BIAS, UP_BIAS = 9, 10, 12


def dot(left, right, dims):
    return lax.dot_general(left, right, dims, preferred_element_type=F32)


def line(ref, index):
    return ref[index : index + 1, :]


def tile(index):
    return slice(index * TILE, index * TILE + TILE)


def fold(values):
    return jnp.sum(values.reshape(values.shape[0] // 8, 8, values.shape[1]), axis=0)


def norm_parts(features):
    center = features - jnp.mean(features, axis=-1, keepdims=True)
    scale = lax.rsqrt(jnp.mean(center * center, axis=-1, keepdims=True) + 1e-6)
    return center * scale, scale


def enter(patches, hide, vec, page, rows):
    features = patches[page, rows, :].astype(F32)
    return jnp.where(hide[page, rows, :] > 0, line(vec, EMBED), features)


def chunks():
    return [slice(start, start + size) for start, size in CHUNKS]


def first_norm(patches, hide, vec, first_low, page):
    for rows in chunks():
        norm, _ = norm_parts(enter(patches, hide, vec, page, rows))
        first_low[page, rows, :] = (norm * line(vec, GAIN_1) + line(vec, SHIFT_1)).astype(LOW)


def lookup(small_all, index_t, pair_bias, head):
    block, place = head // 3, head % 3
    table = small_all[block, place : place + 1, :].astype(F32)
    for half in range(2):
        index = index_t[:, 128 * half : 128 * half + 128]
        low_part, high_part = index & 127, index >> 7
        found = None
        for part in range(6):
            entries = jnp.broadcast_to(table[:, 128 * part : 128 * part + 128], (SEQ, 128))
            got = jnp.take_along_axis(entries, low_part, axis=1)
            found = got if found is None else jnp.where(high_part == part, got, found)
        key = lax.broadcasted_iota(jnp.int32, (SEQ, 128), 0)
        pair_bias[head, :, 128 * half : 128 * half + 128] = jnp.where(key > PATCHES, -1e30, found)


def project(first_low, full_a, bias_rows, heads, part, column):
    weight = full_a[part * WIDTH + column * TILE : part * WIDTH + column * TILE + TILE, :]
    for page in range(PAGES):
        result = dot(first_low[page], weight, NT)
        if part == 0:
            result = (result + bias_rows[0:1, tile(column)]) * 0.125
        elif part == 2:
            result = result + bias_rows[1:2, tile(column)]
        heads[part, page, :, tile(column)] = result.astype(LOW)


def attend(heads, pair_bias, expo, scale, page, pair):
    lanes = slice(pair * 128, pair * 128 + 128)
    query, key, value = (heads[part, page, :, lanes] for part in range(3))
    lane = lax.broadcasted_iota(jnp.int32, (SEQ, 128), 1)
    value_t = value.T
    outs = []
    for which in range(2):
        head = 2 * pair + which
        keep = lane < 64 if which == 0 else lane >= 64
        scores = dot(key, jnp.where(keep, query, jnp.zeros_like(query)), NT)
        scores = scores + pair_bias[head, :, 0:SEQ]
        raised = jnp.exp(scores - jnp.max(scores, axis=0, keepdims=True))
        inverse = 1.0 / jnp.sum(raised, axis=0, keepdims=True)
        raised = raised.astype(LOW)
        expo[page, head] = raised
        scale[page, head : head + 1, :] = inverse
        outs.append(dot(value_t[64 * which : 64 * which + 64], raised, NN) * inverse)
    heads[3, page, :, lanes] = jnp.concatenate(outs, axis=0).T.astype(LOW)


def out_project(heads, full_a, vec, patches, hide, branch, middle, page):
    for column in range(3):
        weight = full_a[3 * WIDTH : 4 * WIDTH, tile(column)]
        branch[page, :, tile(column)] = dot(heads[3, page], weight, NN) + vec[3:4, tile(column)]
    for rows in chunks():
        entered = enter(patches, hide, vec, page, rows)
        middle[page, rows, :] = entered + line(vec, ATT_SCALE) * branch[page, rows, :]


def second_norm(middle, vec, second_low, page):
    for rows in chunks():
        norm, _ = norm_parts(middle[page, rows, :])
        second_low[page, rows, :] = (norm * line(vec, GAIN_2) + line(vec, SHIFT_2)).astype(LOW)


def feed_up(second_low, full_up, up_bias, hidden_low, slope, t, column):
    weight = full_up[t * WIDTH : (t + 1) * WIDTH, tile(column)]
    bias = up_bias[t : t + 1, tile(column)]
    for page in range(PAGES):
        pre = dot(second_low[page], weight, NN) + bias
        portion = 0.5 * (1.0 + lax.erf(pre * 0.7071067811865476))
        hidden_low[t, page, :, tile(column)] = (pre * portion).astype(LOW)
        bell = jnp.exp(-0.5 * pre * pre) * 0.3989422804014327
        slope[t, page, :, tile(column)] = (portion + pre * bell).astype(LOW)


def feed_down(hidden_low, full_down, vec, middle, cot, output, feed_sum, tp_size, page):
    for column in range(3):
        total = None
        for t in range(tp_size):
            weight = full_down[t * WIDTH : (t + 1) * WIDTH, tile(column)]
            term = dot(hidden_low[t, page], weight, NN)
            total = term if total is None else total + term
        branch = total + vec[DOWN_BIAS : DOWN_BIAS + 1, tile(column)]
        scaled = vec[FEED_SCALE : FEED_SCALE + 1, tile(column)] * branch
        output[page, :, tile(column)] = middle[page, :, tile(column)] + scaled
        feed_sum[:, tile(column)] += fold(cot[page, :, tile(column)].astype(F32) * branch)


class Gather:
    def __init__(self, place, blocks, small, full, small_all, sems):
        self.place, self.blocks, self.small = place, blocks, small
        self.full, self.small_all = full, small_all
        self.own_sem, self.z_sem, self.small_sem, self.plane_sem, self.core_sem = sems
        self.offsets = range(1, place.tp_size)
        self.started = []

    def start(self, copy):
        copy.start()
        self.started.append(copy)

    def rows(self, kind, t, d, start=0, size=SLICE):
        row = pl.multiple_of(slice_row(kind, t, d) + start, 16)
        return self.full[kind].at[pl.ds(row, size)]

    def z_copy(self, kind, offset, source):
        place = self.place
        return send(
            self.blocks[kind].at[pl.ds(pl.multiple_of(place.d * SLICE, 16), SLICE)],
            self.rows(kind, source, place.d),
            self.z_sem.at[0, kind, offset - 1],
            self.z_sem.at[1, kind, offset - 1],
            place.to_z(offset),
        )

    def small_copy(self, offset, source):
        return send(
            self.small,
            self.small_all.at[source],
            self.small_sem.at[0, offset - 1],
            self.small_sem.at[1, offset - 1],
            self.place.to_z(offset),
        )

    def plane_copy(self, step, kind, offset, d, device, start=0, size=SLICE):
        rows = self.rows(kind, self.place.from_z(offset), d, start, size)
        return send(
            rows,
            rows,
            self.plane_sem.at[0, step, kind, offset - 1],
            self.plane_sem.at[1, step, kind, offset - 1],
            device,
        )

    def core_copy(self, step, kind, offset, d):
        rows = self.rows(kind, self.place.from_z(offset), d)
        return send(
            rows,
            rows,
            self.core_sem.at[0, step, kind, offset - 1],
            self.core_sem.at[1, step, kind, offset - 1],
            self.place.to_core,
        )

    def own_copy(self, index):
        t, sem = self.place.t, self.own_sem.at[index]
        if index == 0:
            return pltpu.make_async_copy(self.small, self.small_all.at[t], sem)
        if index < 3:
            rows = pl.ds(pl.multiple_of(t * WIDTH, 16), WIDTH)
            return pltpu.make_async_copy(self.blocks[index], self.full[index].at[rows], sem)
        part = index - 3
        rows = pl.ds(pl.multiple_of(part * WIDTH + t * 192, 16), 192)
        block = self.blocks[0].at[pl.ds(part * 192, 192)]
        return pltpu.make_async_copy(block, self.full[0].at[rows], sem)

    def begin(self):
        for offset in self.offsets:
            self.start(self.small_copy(offset, self.place.t))
        for kind in range(3):
            for offset in self.offsets:
                self.start(self.z_copy(kind, offset, self.place.t))
        for index in range(7):
            self.own_copy(index).start()

    def small_ready(self):
        self.own_copy(0).wait()
        for offset in self.offsets:
            self.small_copy(offset, self.place.from_z(offset)).wait_recv()

    def first(self, kind, offset):
        place = self.place
        self.z_copy(kind, offset, place.from_z(offset)).wait_recv()
        self.start(self.plane_copy(0, kind, offset, place.d, place.to_x))
        self.start(self.plane_copy(1, kind, offset, place.d, place.to_y))
        self.start(self.core_copy(0, kind, offset, place.d))

    def second(self, kind, offset):
        place = self.place
        self.plane_copy(0, kind, offset, place.d_x, place.to_x).wait_recv()
        self.start(self.plane_copy(2, kind, offset, place.d_x, place.to_y, HALF, HALF))
        self.start(self.core_copy(1, kind, offset, place.d_x))
        self.plane_copy(1, kind, offset, place.d_y, place.to_y).wait_recv()
        self.start(self.plane_copy(3, kind, offset, place.d_y, place.to_x, 0, HALF))
        self.start(self.core_copy(2, kind, offset, place.d_y))

    def third(self, kind, offset):
        place = self.place
        self.plane_copy(2, kind, offset, place.d_xy, place.to_y, HALF, HALF).wait_recv()
        self.plane_copy(3, kind, offset, place.d_xy, place.to_x, 0, HALF).wait_recv()
        self.start(self.core_copy(3, kind, offset, place.d_xy))

    def last(self, kind):
        place = self.place
        for offset in self.offsets:
            for step, d in enumerate((place.d, place.d_x, place.d_y, place.d_xy)):
                self.core_copy(step, kind, offset, place.core_of(d)).wait_recv()
        for index in range(3, 7) if kind == 0 else (kind,):
            self.own_copy(index).wait()

    def finish(self):
        for copy in self.started:
            copy.wait_send()


GATHER_ORDER = (
    (0, 0, 1), (0, 0, 2), (0, 0, 3), (1, 0, 1), (1, 0, 2), (0, 1, 1),
    (1, 0, 3), (2, 0, 1), (0, 1, 2), (2, 0, 2), (1, 1, 1), (0, 1, 3),
    (2, 0, 3), (1, 1, 2), (0, 2, 1), (2, 1, 1), (1, 1, 3), (0, 2, 2),
    (2, 1, 2), (1, 2, 1), (0, 2, 3), (2, 1, 3), (1, 2, 2), (2, 2, 1),
    (1, 2, 3), (2, 2, 2), (2, 2, 3),
)


def forward_kernel(tp_size, *refs):
    blocks, small = refs[:3], refs[3]
    patches, cot, hide, index_t, vec = refs[4:9]
    saved_full, saved_hidden, saved_slope, saved_heads, saved_expo = refs[9:12], *refs[12:16]
    saved_branch, saved_middle, saved_second, saved_first, output = refs[16:21]
    scale, feed_sum = refs[21:23]
    full, small_all = refs[23:26], refs[26]
    (pair_bias, heads, expo, branch, middle, first_low, second_low, second_t) = refs[27:35]
    (hidden_low, slope, result, bias_rows, up_bias) = refs[35:40]
    save_sem, sems = refs[40], refs[41:]
    place = Place(tp_size)
    gather = Gather(place, blocks, small, full, small_all, sems)
    saves = []

    def save(src, dst):
        copy = pltpu.make_async_copy(src, dst, save_sem.at[len(saves)])
        copy.start()
        saves.append(copy)

    events = list(GATHER_ORDER)
    steps = (gather.first, gather.second, gather.third)

    def advance(count):
        for _ in range(min(count, len(events))):
            step, kind, offset = events.pop(0)
            steps[step](kind, offset)

    def advance_kind(kind):
        while any(event[1] == kind for event in events):
            advance(1)
        gather.last(kind)
        save(full[kind], saved_full[kind])

    meet(place)
    gather.begin()
    for page in range(PAGES):
        first_norm(patches, hide, vec, first_low, page)
    save(first_low, saved_first)
    feed_sum[...] = jnp.zeros_like(feed_sum)
    gather.small_ready()
    for t in range(tp_size):
        columns = slice(192 * t, 192 * t + 192)
        up_bias[t : t + 1, :] = small_all[t, 3:4, :].astype(F32)
        bias_rows[0:1, columns] = small_all[t, 4:5, 0:192].astype(F32)
        bias_rows[1:2, columns] = small_all[t, 5:6, 0:192].astype(F32)
    for head in range(HEADS):
        lookup(small_all, index_t, pair_bias, head)
        if head % 2 == 1:
            advance(1)
    advance_kind(0)
    for part in range(3):
        for column in range(3):
            project(first_low, full[0], bias_rows, heads, part, column)
        advance(1)
    for page in range(PAGES):
        for pair in range(HEADS // 2):
            attend(heads, pair_bias, expo, scale, page, pair)
            if pair % 3 == 2:
                advance(1)
    save(expo, saved_expo)
    save(heads, saved_heads)
    for page in range(PAGES):
        out_project(heads, full[0], vec, patches, hide, branch, middle, page)
        second_norm(middle, vec, second_low, page)
        advance(1)
    save(branch, saved_branch)
    save(middle, saved_middle)
    advance_kind(1)
    for page in range(PAGES):
        second_t[page] = second_low[page].T
    save(second_t, saved_second)
    for t in range(tp_size):
        for column in range(3):
            feed_up(second_low, full[1], up_bias, hidden_low, slope, t, column)
            advance(1)
        save(hidden_low.at[t], saved_hidden.at[t])
        save(slope.at[t], saved_slope.at[t])
    advance_kind(2)
    for page in range(PAGES):
        feed_down(
            hidden_low, full[2], vec, middle, cot, result, feed_sum, tp_size, page
        )
        save(result.at[page], output.at[page])
    gather.finish()
    for copy in saves:
        copy.wait()


def forward(blocks, small, patches, cot, hide, index_t, vec, tp_size):
    any_space = pl.BlockSpec(memory_space=pl.ANY)
    vmem = pl.BlockSpec(memory_space=pltpu.VMEM)
    dma = pltpu.SemaphoreType.DMA
    page_shape = (PAGES, SEQ, WIDTH)
    full = jax.ShapeDtypeStruct((tp_size * WIDTH, WIDTH), LOW)
    wide = jax.ShapeDtypeStruct((tp_size,) + page_shape, LOW)
    page_low = jax.ShapeDtypeStruct(page_shape, LOW)
    page_full = jax.ShapeDtypeStruct(page_shape, F32)
    expo = jax.ShapeDtypeStruct((PAGES, HEADS, SEQ, SEQ), LOW)
    second = jax.ShapeDtypeStruct((PAGES, WIDTH, SEQ), LOW)
    in_memory = [full, full, full, wide, wide, jax.ShapeDtypeStruct((4,) + page_shape, LOW), expo]
    in_memory += [page_full, page_full, second, page_low, page_full]
    out_shape = in_memory + [
        jax.ShapeDtypeStruct((PAGES, 16, SEQ), F32),
        jax.ShapeDtypeStruct((8, WIDTH), F32),
    ]

    def scratch(shape):
        return pltpu.VMEM(shape.shape, shape.dtype)

    return pl.pallas_call(
        functools.partial(forward_kernel, tp_size),
        out_shape=out_shape,
        in_specs=[any_space] * 4 + [vmem] * 5,
        out_specs=[any_space] * len(in_memory) + [vmem] * 2,
        scratch_shapes=[scratch(full)] * 3
        + [
            pltpu.VMEM((tp_size,) + small.shape, LOW),
            pltpu.VMEM((HEADS, SEQ, TILE), F32),
            pltpu.VMEM((4,) + page_shape, LOW),
            scratch(expo),
            scratch(page_full),
            scratch(page_full),
            scratch(page_low),
            scratch(page_low),
            scratch(second),
            scratch(wide),
            scratch(wide),
            scratch(page_full),
            pltpu.VMEM((8, WIDTH), F32),
            pltpu.VMEM((8, WIDTH), F32),
            dma((32,)),
            dma((7,)),
            dma((2, 3, tp_size - 1)),
            dma((2, tp_size - 1)),
            dma((2, 4, 3, tp_size - 1)),
            dma((2, 4, 3, tp_size - 1)),
        ],
        compiler_params=pltpu.CompilerParams(
            collective_id=0, has_side_effects=True, vmem_limit_bytes=60 << 20
        ),
    )(*blocks, small, patches, cot, hide, index_t, vec)


DOWN, UP, FIRST = 0, 1, 2


class Reduce:
    def __init__(self, place, parts, bufs, outs, sems):
        self.place, self.parts, self.outs = place, parts, outs
        self.core_in, self.one_in, self.two_in, self.z_in = bufs
        self.core_sem, self.one_sem, self.two_sem, self.z_sem, self.plane_sem, self.back_sem = sems
        self.offsets = range(1, place.tp_size)
        self.mine = place.y * 2 + place.x
        self.other_x, self.other_y = 1 - place.x, 1 - place.y
        self.started = {DOWN: [], UP: [], FIRST: [], "out": []}

    def start(self, kind, copy):
        copy.start()
        self.started[kind].append(copy)

    def sent(self, kind):
        for copy in self.started[kind]:
            copy.wait_send()
        self.started[kind] = []

    def part(self, kind):
        return self.parts.at[1 if kind == UP else 0]

    def block(self, group):
        return lax.rem(self.place.t + group, self.place.tp_size)

    def core_copy(self, kind, group):
        return send(
            self.part(kind).at[1 - self.place.core, :, :, self.block(group)],
            self.core_in.at[kind, group],
            self.core_sem.at[0, kind, group],
            self.core_sem.at[1, kind, group],
            self.place.to_core,
        )

    def own(self, kind):
        return self.part(kind).at[self.place.core]

    def one_copy(self, kind, group, which):
        t = self.block(group)
        if which < 2:
            src = self.own(kind).at[0, which * 2 + self.other_x, t]
            dst, device = self.one_in.at[kind, group, 0, which], self.place.to_x
        else:
            src = self.own(kind).at[1, self.other_y * 2 + which - 2, t]
            dst, device = self.one_in.at[kind, group, 1, which - 2], self.place.to_y
        sem = self.one_sem
        return send(src, dst, sem.at[0, kind, group, which], sem.at[1, kind, group, which], device)

    def two_copy(self, kind, group, which):
        t, place = self.block(group), self.place
        cell = self.other_y * 2 + place.x if which == 0 else place.y * 2 + self.other_x
        return send(
            self.own(kind).at[which, cell, t],
            self.two_in.at[kind, group, which],
            self.two_sem.at[0, kind, group, which],
            self.two_sem.at[1, kind, group, which],
            place.to_y if which == 0 else place.to_x,
        )

    def z_copy(self, kind, group):
        return send(
            self.own(kind).at[:, self.mine, self.block(group)],
            self.z_in.at[kind, group - 1],
            self.z_sem.at[0, kind, group - 1],
            self.z_sem.at[1, kind, group - 1],
            self.place.to_z(group),
        )

    def rows(self, kind, d, begin=0, size=SLICE):
        return self.outs[kind].at[pl.ds(pl.multiple_of(d * SLICE + begin, 16), size)]

    def plane_copy(self, step, kind, d, device, begin=0, size=SLICE):
        rows = self.rows(kind, d, begin, size)
        sem = self.plane_sem
        return send(rows, rows, sem.at[0, step, kind], sem.at[1, step, kind], device)

    def back_copy(self, step, kind, d):
        rows, sem = self.rows(kind, d), self.back_sem
        return send(rows, rows, sem.at[0, step, kind], sem.at[1, step, kind], self.place.to_core)

    def add(self, kind, half, cell, t, addend):
        ref = self.own(kind).at[half, cell, t]
        ref[...] = (ref[...].astype(F32) + addend.astype(F32)).astype(LOW)

    def cross(self, kind, group):
        self.start(kind, self.core_copy(kind, group))

    def one(self, kind, group):
        self.core_copy(kind, group).wait_recv()
        t = self.block(group)
        for half in range(2):
            for cell in range(4):
                self.add(kind, half, cell, t, self.core_in[kind, group, half, cell])
        for which in range(4):
            self.start(kind, self.one_copy(kind, group, which))

    def two(self, kind, group):
        for which in range(4):
            self.one_copy(kind, group, which).wait_recv()
        t, place = self.block(group), self.place
        for index in range(2):
            self.add(kind, 0, index * 2 + place.x, t, self.one_in[kind, group, 0, index])
            self.add(kind, 1, place.y * 2 + index, t, self.one_in[kind, group, 1, index])
        for which in range(2):
            self.start(kind, self.two_copy(kind, group, which))

    def three(self, kind, group):
        for which in range(2):
            self.two_copy(kind, group, which).wait_recv()
            self.add(kind, which, self.mine, self.block(group), self.two_in[kind, group, which])
        if group:
            self.start(kind, self.z_copy(kind, group))

    def final(self, kind):
        place = self.place
        for offset in self.offsets:
            self.z_copy(kind, offset).wait_recv()
        for half in range(2):
            total = self.own(kind)[half, self.mine, place.t].astype(F32)
            for offset in self.offsets:
                total = total + self.z_in[kind, offset - 1, half].astype(F32)
            self.rows(kind, place.d, half * HALF, HALF)[...] = total.astype(LOW)
        self.start("out", self.plane_copy(0, kind, place.d, place.to_x))
        self.start("out", self.plane_copy(1, kind, place.d, place.to_y))
        self.start("out", self.back_copy(0, kind, place.d))

    def relay(self, kind):
        place = self.place
        self.plane_copy(0, kind, place.d_x, place.to_x).wait_recv()
        self.start("out", self.plane_copy(2, kind, place.d_x, place.to_y, HALF, HALF))
        self.start("out", self.back_copy(1, kind, place.d_x))
        self.plane_copy(1, kind, place.d_y, place.to_y).wait_recv()
        self.start("out", self.plane_copy(3, kind, place.d_y, place.to_x, 0, HALF))
        self.start("out", self.back_copy(2, kind, place.d_y))

    def back(self, kind):
        place = self.place
        self.plane_copy(2, kind, place.d_xy, place.to_y, HALF, HALF).wait_recv()
        self.plane_copy(3, kind, place.d_xy, place.to_x, 0, HALF).wait_recv()
        self.start("out", self.back_copy(3, kind, place.d_xy))

    def last(self, kind):
        place = self.place
        for step, d in enumerate((place.d, place.d_x, place.d_y, place.d_xy)):
            self.back_copy(step, kind, place.core_of(d)).wait_recv()


class Total:
    def __init__(self, place, stages, arrived, line_up, sems):
        self.place, self.stages, self.arrived, self.line_up = place, stages, arrived, line_up
        self.pair_sem, self.z_sem = sems
        self.started = []

    def pair_copy(self, step):
        device = (self.place.to_core, self.place.to_x, self.place.to_y)[step]
        sem = self.pair_sem
        return send(
            self.stages.at[step], self.arrived.at[step], sem.at[0, step], sem.at[1, step], device
        )

    def z_copy(self, offset, source):
        sem = self.z_sem
        return send(
            self.stages.at[3],
            self.line_up.at[source],
            sem.at[0, offset - 1],
            sem.at[1, offset - 1],
            self.place.to_z(offset),
        )

    def start(self, copy):
        copy.start()
        self.started.append(copy)

    def begin(self):
        self.start(self.pair_copy(0))

    def step(self, index):
        self.pair_copy(index).wait_recv()
        self.stages[index + 1] = self.stages[index] + self.arrived[index]
        if index < 2:
            self.start(self.pair_copy(index + 1))
        else:
            for offset in range(1, self.place.tp_size):
                self.start(self.z_copy(offset, self.place.t))
            self.line_up[self.place.t] = self.stages[3]

    def end(self):
        for offset in range(1, self.place.tp_size):
            self.z_copy(offset, self.place.from_z(offset)).wait_recv()
        total = self.line_up[0]
        for t in range(1, self.place.tp_size):
            total = total + self.line_up[t]
        return total

    def finish(self):
        for copy in self.started:
            copy.wait_send()


def store_part(part, base, values, t):
    for piece in range(values.shape[0] // 16):
        d, inner = divmod(base + piece * 16, SLICE)
        rows = pl.ds(inner % HALF, 16)
        lines = values[piece * 16 : piece * 16 + 16].astype(LOW)
        part[d % 2, inner // HALF, d // 2, t, rows, :] = lines


def store_first(part, section, base, values):
    for piece in range(values.shape[0] // 16):
        t, inner = divmod(base + piece * 16, 192)
        core, inner = divmod(inner, SLICE)
        rows = pl.ds(inner % HALF, 16)
        lines = values[piece * 16 : piece * 16 + 16].astype(LOW)
        part[core, inner // HALF, section, t, rows, :] = lines


def total_of(terms):
    result = None
    for term in terms:
        result = term if result is None else result + term
    return result


def feed_cot(cot, vec, feed_low, sums, page):
    for rows in chunks():
        values = cot[page, rows, :].astype(F32) * line(vec, FEED_SCALE)
        sums[DOWN_BIAS] += fold(values)
        feed_low[page, rows, :] = values.astype(LOW)


def down_back(feed_low, full_down, hidden_low, slope, sums, part, t, column):
    row = pl.multiple_of(t * WIDTH + column * TILE, TILE)
    weight = full_down[pl.ds(row, TILE), :]
    grads, folds = [], []
    for page in range(PAGES):
        grads.append(dot(hidden_low[t, page, :, tile(column)], feed_low[page], TN))
        pre_cot = dot(feed_low[page], weight, NT) * slope[t, page, :, tile(column)].astype(F32)
        folds.append(fold(pre_cot))
        slope[t, page, :, tile(column)] = pre_cot.astype(LOW)
    sums[UP_BIAS + t, :, tile(column)] = total_of(folds)
    store_part(part, column * TILE, total_of(grads), t)


def up_back(second_t, pre_cot, part, t, column):
    grads = [dot(second_t[page, tile(column), :], pre_cot[t, page], NN) for page in range(PAGES)]
    store_part(part, column * TILE, total_of(grads), t)


def second_cot(pre_cot, full_up, result, tp_size, page):
    for column in range(3):
        terms = []
        for t in range(tp_size):
            rows = slice(t * WIDTH + column * TILE, t * WIDTH + column * TILE + TILE)
            terms.append(dot(pre_cot[t, page], full_up[rows, :], NT))
        result[page, :, tile(column)] = total_of(terms)


def norm_back(features, cot, gain, sums, gain_row, shift_row):
    norm, scale = norm_parts(features)
    sums[gain_row] += fold(cot * norm)
    sums[shift_row] += fold(cot)
    cot = cot * gain
    mean = jnp.mean(cot, axis=-1, keepdims=True)
    along = jnp.mean(cot * norm, axis=-1, keepdims=True)
    return scale * (cot - mean - norm * along)


def second_back(middle, result, cot, branch, vec, sums, branch_low, page):
    for rows in chunks():
        part = norm_back(
            middle[page, rows, :], result[page, rows, :], line(vec, GAIN_2), sums, GAIN_2, SHIFT_2
        )
        middle_cot = cot[page, rows, :].astype(F32) + part
        middle[page, rows, :] = middle_cot
        sums[ATT_SCALE] += fold(middle_cot * branch[page, rows, :])
        branch_cot = middle_cot * line(vec, ATT_SCALE)
        sums[OUT_BIAS] += fold(branch_cot)
        branch_low[page, rows, :] = branch_cot.astype(LOW)


def attended_back(branch_low, full_a, attended_cot, page):
    for column in range(3):
        rows = slice(3 * WIDTH + column * TILE, 3 * WIDTH + column * TILE + TILE)
        result = dot(branch_low[page], full_a[rows, :], NT)
        attended_cot[page, :, tile(column)] = result.astype(LOW)


def attend_back(heads, expo, scale, attended_cot, scores, page, pair):
    lanes = slice(pair * 128, pair * 128 + 128)
    query, key, value = (heads[part, page, :, lanes] for part in range(3))
    cot = attended_cot[page, :, lanes]
    lane = lax.broadcasted_iota(jnp.int32, (SEQ, 128), 1)
    zero = jnp.zeros_like(query)
    key_t = key.T
    query_cots, key_cots, value_cots = [], [], []
    for which in range(2):
        head = 2 * pair + which
        keep = lane < 64 if which == 0 else lane >= 64
        head_query, head_cot = jnp.where(keep, query, zero), jnp.where(keep, cot, zero)
        prob_cot = dot(value, head_cot, NT)
        probs = expo[page, head].astype(F32) * scale[page, head : head + 1, :]
        product = probs * prob_cot
        score_cot = product - probs * jnp.sum(product, axis=0, keepdims=True)
        for half, width in ((0, 128), (1, SEQ - 128)):
            rows = slice((half * HEADS + head) * SEQ, (half * HEADS + head + 1) * SEQ)
            scores[rows, 0:width] += score_cot[:, half * 128 : half * 128 + width]
        score_cot = score_cot.astype(LOW)
        value_cots.append(dot(probs.astype(LOW), head_cot, NN))
        key_cots.append(dot(score_cot, head_query, NN))
        query_cots.append(dot(key_t[64 * which : 64 * which + 64], score_cot, NN))
    heads[0, page, :, lanes] = (jnp.concatenate(query_cots, axis=0).T * 0.125).astype(LOW)
    heads[1, page, :, lanes] = total_of(key_cots).astype(LOW)
    heads[2, page, :, lanes] = total_of(value_cots).astype(LOW)


def section_back(heads, right, part, sums, section, column):
    pieces = [heads[section, page, :, tile(column)] for page in range(PAGES)]
    grads = [dot(pieces[page], right[page], TN) for page in range(PAGES)]
    if section in (0, 2):
        index = Q_BIAS if section == 0 else V_BIAS
        sums[index, :, tile(column)] = total_of([fold(piece.astype(F32)) for piece in pieces])
    store_first(part, section, column * TILE, total_of(grads))


def first_cot(heads, full_a, result, page):
    for column in range(3):
        terms = [
            dot(heads[part, page], full_a[part * WIDTH : (part + 1) * WIDTH, tile(column)], NN)
            for part in range(3)
        ]
        result[page, :, tile(column)] = total_of(terms)


def first_back(patches, hide, vec, result, middle, sums, page):
    for rows in chunks():
        features = enter(patches, hide, vec, page, rows)
        part = norm_back(
            features, result[page, rows, :], line(vec, GAIN_1), sums, GAIN_1, SHIFT_1
        )
        entered_cot = middle[page, rows, :] + part
        hidden = hide[page, rows, :] > 0
        result[page, rows, :] = jnp.where(hidden, 0.0, entered_cot)
        sums[EMBED] += fold(jnp.where(hidden, entered_cot, 0.0))


def table_back(scores, index_t, packed):
    row = lax.broadcasted_iota(jnp.int32, (128, TILE), 0)
    unroll = 20

    def step(index, total):
        lefts, rights = [], []
        for inner in range(unroll):
            key = index * unroll + inner
            halves = [
                scores[pl.ds(half * HEADS * SEQ + key, HEADS, stride=SEQ), :] for half in range(2)
            ]
            terms = jnp.concatenate(halves, axis=1)
            terms = jnp.concatenate([terms, jnp.zeros((4, TILE), F32)], axis=0)
            entry = index_t[pl.ds(key, 1), :]
            low_part, high_part = entry & 127, entry >> 7
            match = jnp.broadcast_to(low_part, (128, TILE)) == row
            rights.append(jnp.where(match, 1.0, 0.0).astype(LOW))
            picked = [jnp.where(high_part == part, terms, 0.0).astype(LOW) for part in range(6)]
            lefts.append(jnp.concatenate(picked, axis=0))
        return total + dot(jnp.concatenate(lefts, axis=1), jnp.concatenate(rights, axis=1), NT)

    total = lax.fori_loop(0, SEQ // unroll, step, jnp.zeros((96, 128), F32))
    for part in range(6):
        packed[16:32, part * 128 : part * 128 + 128] = total[part * 16 : part * 16 + 16]


def backward_kernel(tp_size, *refs):
    from_full, from_hidden, from_slope, from_heads, from_expo = refs[:3], *refs[3:7]
    from_branch, from_middle, from_second, from_first = refs[7:11]
    scale, feed_sum, patches, cot, hide, index_t, vec = refs[11:18]
    outs, patch_out, vectors, bias_out, table_out, up_out = refs[18:21], *refs[21:26]
    weights, wide, slope, expo, parts = refs[26:31]
    bufs = refs[31:35]
    scores, branch, middle, result, second_t, first_low, feed_low, attended_cot = refs[35:43]
    sums, stages, arrived, line_up = refs[43:47]
    load_sem, wide_sem, reduce_sems, total_sems = refs[47], refs[48], refs[49:55], refs[55:57]
    place = Place(tp_size)
    reduce = Reduce(place, parts, bufs, outs, reduce_sems)
    total = Total(place, stages, arrived, line_up, total_sems)

    def load(index, src, dst):
        return pltpu.make_async_copy(src, dst, load_sem.at[index])

    def load_wide(group):
        t = reduce.block(group)
        rows = pl.ds(pl.multiple_of(t * WIDTH, 16), WIDTH)
        pairs = (
            (from_full[2].at[rows], weights.at[0, rows]),
            (from_hidden.at[t], wide.at[t]),
            (from_slope.at[t], slope.at[t]),
        )
        return [
            pltpu.make_async_copy(src, dst, wide_sem.at[group, index])
            for index, (src, dst) in enumerate(pairs)
        ]

    order = tuple(range(1, tp_size)) + (0,)
    for group in order:
        for copy in load_wide(group):
            copy.start()
    early = [
        load(0, from_second, second_t),
        load(1, from_full[1], weights.at[1]),
        load(2, from_middle, middle),
        load(3, from_branch, branch),
        load(4, from_expo, expo),
        load(5, from_first, first_low),
    ]
    for copy in early:
        copy.start()
    sums[...] = jnp.zeros_like(sums)
    sums[FEED_SCALE] = feed_sum[...]
    scores[...] = jnp.zeros_like(scores)
    for page in range(PAGES):
        feed_cot(cot, vec, feed_low, sums, page)
    meet(place)

    def run(*events):
        for step, kind, group in events:
            step(kind, group)

    def whole(step):
        return lambda kind, group: step(kind)

    cross, one, two, three = reduce.cross, reduce.one, reduce.two, reduce.three
    final, relay, back = whole(reduce.final), whole(reduce.relay), whole(reduce.back)
    last = whole(reduce.last)

    after_down = {
        1: ((cross, DOWN, 1),),
        2: ((cross, DOWN, 2), (one, DOWN, 1)),
        3: ((cross, DOWN, 3), (one, DOWN, 2)),
        0: ((cross, DOWN, 0), (one, DOWN, 3)),
    }
    for group in order:
        for copy in load_wide(group):
            copy.wait()
        for column in range(3):
            down_back(
                feed_low, weights.at[0], wide, slope, sums, reduce.part(DOWN),
                reduce.block(group), column,
            )
        run(*after_down[group])
    late = [load(6, from_full[0], weights.at[0]), load(7, from_heads, wide)]
    for copy in late:
        copy.start()
    early[0].wait()
    after_up = {
        1: ((cross, UP, 1), (one, DOWN, 0), (two, DOWN, 1)),
        2: ((cross, UP, 2), (one, UP, 1)),
        3: ((cross, UP, 3), (one, UP, 2), (two, DOWN, 2)),
        0: ((cross, UP, 0), (one, UP, 3), (three, DOWN, 1)),
    }
    for group in order:
        for column in range(3):
            up_back(second_t, slope, reduce.part(UP), reduce.block(group), column)
        run(*after_up[group])
    early[1].wait()
    after_second = (
        ((one, UP, 0), (two, DOWN, 3)),
        ((three, DOWN, 2),),
        ((two, DOWN, 0),),
    )
    for page in range(PAGES):
        second_cot(slope, weights.at[1], result, tp_size, page)
        run(*after_second[page])
    for copy in early[2:4]:
        copy.wait()
    for page in range(PAGES):
        second_back(middle, result, cot, branch, vec, sums, feed_low, page)
    run((three, DOWN, 3), (two, UP, 1))
    for copy in late + early[4:]:
        copy.wait()
    for page in range(PAGES):
        attended_back(feed_low, weights.at[0], attended_cot, page)
    run((three, DOWN, 0))
    after_attend = (
        ((two, UP, 2),),
        ((three, UP, 1), (final, DOWN, 0)),
        ((two, UP, 3),),
        ((three, UP, 2), (relay, DOWN, 0)),
        ((two, UP, 0),),
        ((three, UP, 3), (back, DOWN, 0)),
    )
    for page in range(PAGES):
        for pair in range(HEADS // 2):
            attend_back(wide, expo, scale, attended_cot, scores, page, pair)
            if pair % 3 == 2:
                run(*after_attend[page * 2 + pair // 3])
    reduce.sent(DOWN)
    for section in (3, 0, 1, 2):
        right = feed_low if section == 3 else first_low
        for column in range(3):
            section_back(wide, right, reduce.part(FIRST), sums, section, column)
    run(*((cross, FIRST, group) for group in order))
    first_cot(wide, weights.at[0], result, 0)
    run((three, UP, 0), (one, FIRST, 1), (one, FIRST, 2))
    first_cot(wide, weights.at[0], result, 1)
    run((one, FIRST, 3), (one, FIRST, 0))
    first_cot(wide, weights.at[0], result, 2)
    run((final, UP, 0))
    for page in range(PAGES):
        first_back(patches, hide, vec, result, middle, sums, page)
    run((two, FIRST, 1), (relay, UP, 0))
    patch_copy = load(8, result, patch_out)
    patch_copy.start()
    table_back(scores, index_t, stages.at[0])
    stages[0, 0:16, :] = jnp.sum(sums[...], axis=1)
    total.begin()
    run((two, FIRST, 2), (back, UP, 0))
    total.step(0)
    run((two, FIRST, 3), (three, FIRST, 1))
    total.step(1)
    run((two, FIRST, 0), (three, FIRST, 2))
    total.step(2)
    run((three, FIRST, 3), (three, FIRST, 0))
    arrived[0] = total.end()
    vectors[...] = arrived[0, 0:16, :]
    for t in range(tp_size):

        @pl.when(place.t == t)
        def _():
            bias_out[...] = arrived[0, Q_BIAS : Q_BIAS + 2, 192 * t : 192 * t + 192]
            table_out[...] = arrived[0, 16 + 3 * t : 19 + 3 * t, 0:NUM_REL]
            up_out[...] = arrived[0, UP_BIAS + t : UP_BIAS + t + 1, :]

    run((final, FIRST, 0), (relay, FIRST, 0), (back, FIRST, 0))
    run((last, DOWN, 0), (last, UP, 0), (last, FIRST, 0))
    patch_copy.wait()
    for kind in (UP, FIRST, "out"):
        reduce.sent(kind)
    total.finish()


def backward(saved, patches, cot, hide, index_t, vec, tp_size):
    any_space = pl.BlockSpec(memory_space=pl.ANY)
    vmem = pl.BlockSpec(memory_space=pltpu.VMEM)
    dma = pltpu.SemaphoreType.DMA
    page_shape = (PAGES, SEQ, WIDTH)
    shape = jax.ShapeDtypeStruct
    block = (2, 4, HALF, WIDTH)
    return pl.pallas_call(
        functools.partial(backward_kernel, tp_size),
        out_shape=[shape((WIDTH, WIDTH), LOW)] * 3
        + [
            shape(page_shape, F32),
            shape((16, WIDTH), F32),
            shape((2, 192), F32),
            shape((3, NUM_REL), F32),
            shape((1, WIDTH), F32),
        ],
        in_specs=[any_space] * 11 + [vmem] * 7,
        out_specs=[vmem] * 3 + [any_space] + [vmem] * 4,
        scratch_shapes=[
            pltpu.VMEM((2, tp_size * WIDTH, WIDTH), LOW),
            pltpu.VMEM((4,) + page_shape, LOW),
            pltpu.VMEM((tp_size,) + page_shape, LOW),
            pltpu.VMEM((PAGES, HEADS, SEQ, SEQ), LOW),
            pltpu.VMEM((2, 2, 2, 4, tp_size, HALF, WIDTH), LOW),
            pltpu.VMEM((3, tp_size) + block, LOW),
            pltpu.VMEM((3, tp_size, 2, 2, HALF, WIDTH), LOW),
            pltpu.VMEM((3, tp_size, 2, HALF, WIDTH), LOW),
            pltpu.VMEM((3, tp_size - 1, 2, HALF, WIDTH), LOW),
            pltpu.VMEM((2 * HEADS * SEQ, 128), F32),
            pltpu.VMEM(page_shape, F32),
            pltpu.VMEM(page_shape, F32),
            pltpu.VMEM(page_shape, F32),
            pltpu.VMEM((PAGES, WIDTH, SEQ), LOW),
            pltpu.VMEM(page_shape, LOW),
            pltpu.VMEM(page_shape, LOW),
            pltpu.VMEM(page_shape, LOW),
            pltpu.VMEM((16, 8, WIDTH), F32),
            pltpu.VMEM((4, 32, WIDTH), F32),
            pltpu.VMEM((3, 32, WIDTH), F32),
            pltpu.VMEM((tp_size, 32, WIDTH), F32),
            dma((9,)),
            dma((tp_size, 3)),
            dma((2, 3, tp_size)),
            dma((2, 3, tp_size, 4)),
            dma((2, 3, tp_size, 2)),
            dma((2, 3, tp_size - 1)),
            dma((2, 4, 3)),
            dma((2, 4, 3)),
            dma((2, 3)),
            dma((2, tp_size - 1)),
        ],
        compiler_params=pltpu.CompilerParams(
            collective_id=1, has_side_effects=True, vmem_limit_bytes=63 << 20
        ),
    )(*saved, patches, cot, hide, index_t, vec)


def body(tp_size, dp_size, *args):
    (
        patches, page_mask, pair_index, mask_embed, first_gain, first_shift, project_weight,
        project_bias, pair_table, output_weight, output_bias, attention_scale, second_gain,
        second_shift, up_weight, up_bias, down_weight, down_bias, feed_scale, cotangent,
    ) = args
    block_a = jnp.concatenate(
        [jnp.transpose(project_weight, (1, 2, 0)).reshape(576, WIDTH), output_weight], axis=0
    )
    small = jnp.concatenate(
        [
            jnp.pad(jnp.transpose(pair_table), ((0, 0), (0, WIDTH - NUM_REL))),
            up_bias[None],
            jnp.pad(project_bias, ((0, 0), (0, WIDTH - 192))),
            jnp.zeros((10, WIDTH), LOW),
        ],
        axis=0,
    )
    row_count = patches.shape[0]
    position = jnp.arange(row_count) % SEQ
    hidden = (page_mask > 0) & (position >= 1) & (position <= PATCHES)
    hide = hidden.astype(F32).reshape(PAGES, SEQ, 1)
    vec = jnp.stack(
        [
            mask_embed, first_gain, first_shift, output_bias, attention_scale, second_gain,
            second_shift, down_bias, feed_scale,
        ]
    )
    vec = jnp.pad(vec, ((0, 7), (0, 0)))
    index_t = jnp.pad(jnp.transpose(pair_index), ((0, 0), (0, TILE - SEQ)))
    patches = patches.reshape(PAGES, SEQ, WIDTH)
    cot = cotangent.reshape(PAGES, SEQ, WIDTH)
    blocks = (block_a, up_weight, down_weight)
    saved = forward(blocks, small, patches, cot, hide, index_t, vec, tp_size)
    layer_output = saved[11].reshape(row_count, WIDTH)
    results = backward(
        saved[:11] + saved[12:], patches, cot, hide, index_t, vec, tp_size
    )
    down_sum, up_sum, first_sum = (value.astype(F32) for value in results[:3])
    patch_gradient = results[3].reshape(row_count, WIDTH)
    sums = (down_sum, up_sum, first_sum) + tuple(results[4:])
    if dp_size > GROUP:
        groups = [[i + GROUP * j for j in range(dp_size // GROUP)] for i in range(GROUP)]
        sums = lax.psum(sums, "dp", axis_index_groups=groups)
    down_sum, up_sum, first_sum, vectors, bias_sum, table_sum, up_bias_sum = sums
    return (
        layer_output,
        patch_gradient,
        vectors[EMBED],
        vectors[GAIN_1],
        vectors[SHIFT_1],
        jnp.transpose(first_sum[:576].reshape(3, 192, WIDTH), (2, 0, 1)),
        bias_sum,
        jnp.transpose(table_sum),
        first_sum[576:],
        vectors[OUT_BIAS],
        vectors[ATT_SCALE],
        vectors[GAIN_2],
        vectors[SHIFT_2],
        up_sum,
        up_bias_sum[0],
        down_sum,
        vectors[DOWN_BIAS],
        vectors[FEED_SCALE],
    )


def solution(mesh):
    rows, heads = P(("dp", "tp"), None), P(None, "tp")
    in_specs = (
        rows, P(("dp", "tp")), P(), P(), P(), P(), P(None, None, "tp"), heads, heads,
        P("tp", None), P(), P(), P(), P(), heads, P("tp"), P("tp", None), P(), P(), rows,
    )
    out_specs = (
        rows, rows, P(), P(), P(), P(None, None, "tp"), heads, heads, P("tp", None), P(), P(),
        P(), P(), heads, P("tp"), P("tp", None), P(), P(),
    )
    step = functools.partial(body, mesh.shape["tp"], mesh.shape["dp"])
    return jax.shard_map(step, mesh=mesh, in_specs=in_specs, out_specs=out_specs, check_vma=False)
```

```python
import functools

import jax
import jax.numpy as jnp
from jax import lax
from jax.experimental import pallas as pl
from jax.experimental.pallas import tpu as pltpu
from jax.sharding import PartitionSpec as P

SEQ = 200
PATCHES = 196
NUM_REL = 732
PAGES = 3
HEADS = 12
WIDTH = 768
GROUP = 8
SLICE = 96
HALF = 48
MESH = pl.DeviceIdType.MESH


class Place:
    def __init__(self, tp_size):
        self.tp_size = tp_size
        self.dp = lax.axis_index("dp")
        self.t = lax.axis_index("tp")
        self.d = lax.rem(self.dp, GROUP)
        self.core = lax.rem(self.d, 2)
        self.x = lax.rem(self.d // 2, 2)
        self.y = self.d // 4
        self.to_core = (self.dp + 1 - 2 * self.core, self.t)
        self.to_x = (self.dp + 2 - 4 * self.x, self.t)
        self.to_y = (self.dp + 4 - 8 * self.y, self.t)
        self.d_x = self.d + 2 - 4 * self.x
        self.d_y = self.d + 4 - 8 * self.y
        self.d_xy = self.d_x + 4 - 8 * self.y

    def core_of(self, d):
        return d + 1 - 2 * self.core

    def to_z(self, offset):
        return (self.dp, lax.rem(self.t + offset, self.tp_size))

    def from_z(self, offset):
        return lax.rem(self.t + self.tp_size - offset, self.tp_size)


def meet(place):
    barrier = pltpu.get_barrier_semaphore()
    others = [place.to_core, place.to_x, place.to_y]
    others += [place.to_z(offset) for offset in range(1, place.tp_size)]
    for other in others:
        pl.semaphore_signal(barrier, inc=1, device_id=other, device_id_type=MESH)
    pl.semaphore_wait(barrier, len(others))


def send(src, dst, send_sem, recv_sem, device):
    return pltpu.make_async_remote_copy(
        src_ref=src,
        dst_ref=dst,
        send_sem=send_sem,
        recv_sem=recv_sem,
        device_id=device,
        device_id_type=MESH,
    )


def slice_row(kind, t, d):
    if kind == 0:
        row = (d // 2) * 768 + t * 192 + lax.rem(d, 2) * SLICE
    else:
        row = t * 768 + d * SLICE
    return pl.multiple_of(row, 16)


LOW = jnp.bfloat16
F32 = jnp.float32
CHUNKS = ((0, 48), (48, 48), (96, 48), (144, 56))
TILE = 256
NT = (((1,), (1,)), ((), ()))
NN = (((1,), (0,)), ((), ()))
TN = (((0,), (0,)), ((), ()))
EMBED, GAIN_1, SHIFT_1, OUT_BIAS, ATT_SCALE, GAIN_2, SHIFT_2, DOWN_BIAS, FEED_SCALE = range(9)
Q_BIAS, V_BIAS, UP_BIAS = 9, 10, 12


def dot(left, right, dims):
    return lax.dot_general(left, right, dims, preferred_element_type=F32)


def line(ref, index):
    return ref[index : index + 1, :]


def tile(index):
    return slice(index * TILE, index * TILE + TILE)


def fold(values):
    return jnp.sum(values.reshape(values.shape[0] // 8, 8, values.shape[1]), axis=0)


def norm_parts(features):
    center = features - jnp.mean(features, axis=-1, keepdims=True)
    scale = lax.rsqrt(jnp.mean(center * center, axis=-1, keepdims=True) + 1e-6)
    return center * scale, scale


def enter(patches, hide, vec, page, rows):
    features = patches[page, rows, :].astype(F32)
    return jnp.where(hide[rows, page : page + 1] > 0, line(vec, EMBED), features)


def chunks():
    return [slice(start, start + size) for start, size in CHUNKS]


def first_norm(patches, hide, vec, first_low, page):
    for rows in chunks():
        norm, _ = norm_parts(enter(patches, hide, vec, page, rows))
        first_low[page, rows, :] = (norm * line(vec, GAIN_1) + line(vec, SHIFT_1)).astype(LOW)


def lookup(small_all, index_t, pair_bias, head):
    block, place = head // 3, head % 3
    table = small_all[block, place : place + 1, :]
    for half in range(2):
        index = index_t[:, 128 * half : 128 * half + 128]
        low_part, high_part = index & 127, index >> 7
        found = None
        for part in range(6):
            entries = jnp.broadcast_to(table[:, 128 * part : 128 * part + 128], (SEQ, 128))
            got = jnp.take_along_axis(entries, low_part, axis=1)
            found = got if found is None else jnp.where(high_part == part, got, found)
        key = lax.broadcasted_iota(jnp.int32, (SEQ, 128), 0)
        rows = slice((half * HEADS + head) * SEQ, (half * HEADS + head + 1) * SEQ)
        pair_bias[rows, :] = jnp.where(key > PATCHES, -1e30, found)


def project(first_low, full_a, bias_rows, heads, part, column):
    weight = full_a[part * WIDTH + column * TILE : part * WIDTH + column * TILE + TILE, :]
    for page in range(PAGES):
        result = dot(first_low[page], weight, NT)
        if part == 0:
            result = (result + bias_rows[0:1, tile(column)]) * 0.125
        elif part == 2:
            result = result + bias_rows[1:2, tile(column)]
        heads[part, page, :, tile(column)] = result.astype(LOW)


def attend(heads, pair_bias, expo, scale, page, pair):
    lanes = slice(pair * 128, pair * 128 + 128)
    query, key, value = (heads[part, page, :, lanes] for part in range(3))
    lane = lax.broadcasted_iota(jnp.int32, (SEQ, 128), 1)
    value_t = value.T
    outs = []
    for which in range(2):
        head = 2 * pair + which
        keep = lane < 64 if which == 0 else lane >= 64
        scores = dot(key, jnp.where(keep, query, jnp.zeros_like(query)), NT)
        left = pair_bias[head * SEQ : (head + 1) * SEQ, :]
        right = pair_bias[(HEADS + head) * SEQ : (HEADS + head + 1) * SEQ, :]
        scores = scores + jnp.concatenate([left, right], axis=1)[:, 0:SEQ]
        raised = jnp.exp(scores - jnp.max(scores, axis=0, keepdims=True))
        inverse = 1.0 / jnp.sum(raised, axis=0, keepdims=True)
        raised = raised.astype(LOW)
        expo[head // 3, page, :, (head % 3) * TILE : (head % 3) * TILE + SEQ] = raised
        scale[page, head : head + 1, :] = inverse
        outs.append(dot(value_t[64 * which : 64 * which + 64], raised, NN) * inverse)
    heads[3, page, :, lanes] = jnp.concatenate(outs, axis=0).T.astype(LOW)


def out_project(heads, full_a, vec, patches, hide, branch, middle, page):
    for column in range(3):
        weight = full_a[3 * WIDTH : 4 * WIDTH, tile(column)]
        branch[page, :, tile(column)] = dot(heads[3, page], weight, NN) + vec[3:4, tile(column)]
    for rows in chunks():
        entered = enter(patches, hide, vec, page, rows)
        middle[page, rows, :] = entered + line(vec, ATT_SCALE) * branch[page, rows, :]


def second_norm(middle, vec, second_low, page):
    for rows in chunks():
        norm, _ = norm_parts(middle[page, rows, :])
        second_low[page, rows, :] = (norm * line(vec, GAIN_2) + line(vec, SHIFT_2)).astype(LOW)


def feed_up(second_low, full_up, up_bias, hidden_low, slope, t, column):
    weight = full_up[t * WIDTH : (t + 1) * WIDTH, tile(column)]
    bias = up_bias[t : t + 1, tile(column)]
    for page in range(PAGES):
        pre = dot(second_low[page], weight, NN) + bias
        portion = 0.5 * (1.0 + lax.erf(pre * 0.7071067811865476))
        hidden_low[t, page, :, tile(column)] = (pre * portion).astype(LOW)
        bell = jnp.exp(-0.5 * pre * pre) * 0.3989422804014327
        slope[t, page, :, tile(column)] = (portion + pre * bell).astype(LOW)


def feed_down(hidden_low, full_down, vec, middle, cot, output, sums, tp_size, page):
    for column in range(3):
        total = None
        for t in range(tp_size):
            weight = full_down[t * WIDTH : (t + 1) * WIDTH, tile(column)]
            term = dot(hidden_low[t, page], weight, NN)
            total = term if total is None else total + term
        branch = total + vec[DOWN_BIAS : DOWN_BIAS + 1, tile(column)]
        scaled = vec[FEED_SCALE : FEED_SCALE + 1, tile(column)] * branch
        output[page, :, tile(column)] = middle[page, :, tile(column)] + scaled
        sums[FEED_SCALE, :, tile(column)] += fold(cot[page, :, tile(column)].astype(F32) * branch)


class Gather:
    def __init__(self, place, blocks, small, full, small_all, sems):
        self.place, self.blocks, self.small = place, blocks, small
        self.full, self.small_all = full, small_all
        self.own_sem, self.z_sem, self.small_sem, self.plane_sem, self.core_sem = sems
        self.offsets = range(1, place.tp_size)
        self.started = {0: [], 1: [], 2: [], "small": []}
        self.waiting = [(kind, offset) for kind in range(3) for offset in (1, 3, 2)]
        order = tuple(self.waiting)
        self.events = [
            (step,) + order[tick - step]
            for tick in range(len(order) + 2)
            for step in range(3)
            if 0 <= tick - step < len(order)
        ]

    def start(self, kind, copy):
        copy.start()
        self.started[kind].append(copy)

    def sent(self, kind):
        for copy in self.started[kind]:
            copy.wait_send()
        self.started[kind] = []

    def rows(self, kind, t, d, start=0, size=SLICE):
        row = pl.multiple_of(slice_row(kind, t, d) + start, 16)
        return self.full[kind].at[pl.ds(row, size)]

    def z_copy(self, kind, offset, source, block=None):
        place = self.place
        if block is None:
            block = self.blocks[kind + 1].at[pl.ds(pl.multiple_of(place.d * SLICE, 16), SLICE)]
        return send(
            block,
            self.rows(kind, source, place.d),
            self.z_sem.at[0, kind, offset - 1],
            self.z_sem.at[1, kind, offset - 1],
            place.to_z(offset),
        )

    def z_start(self, count):
        place = self.place
        for kind, offset in self.waiting[:count]:
            if kind:
                self.start(kind, self.z_copy(kind, offset, place.t))
                continue

            @pl.when(place.d < 6)
            def _():
                rows = pl.ds(pl.multiple_of(place.d * SLICE, 16), SLICE)
                self.z_copy(0, offset, place.t, self.blocks[0].at[rows]).start()

            @pl.when(place.d >= 6)
            def _():
                rows = pl.ds(pl.multiple_of((place.d - 6) * SLICE, 16), SLICE)
                self.z_copy(0, offset, place.t, self.blocks[1].at[rows]).start()

            rows = pl.ds(0, SLICE)
            self.started[0].append(self.z_copy(0, offset, place.t, self.blocks[1].at[rows]))
        self.waiting = self.waiting[count:]

    def small_copy(self, offset, source):
        return send(
            self.small,
            self.small_all.at[source],
            self.small_sem.at[0, offset - 1],
            self.small_sem.at[1, offset - 1],
            self.place.to_z(offset),
        )

    def plane_copy(self, step, kind, offset, d, device, start=0, size=SLICE):
        rows = self.rows(kind, self.place.from_z(offset), d, start, size)
        return send(
            rows,
            rows,
            self.plane_sem.at[0, step, kind, offset - 1],
            self.plane_sem.at[1, step, kind, offset - 1],
            device,
        )

    def core_copy(self, step, kind, offset, d):
        rows = self.rows(kind, self.place.from_z(offset), d)
        return send(
            rows,
            rows,
            self.core_sem.at[0, step, kind, offset - 1],
            self.core_sem.at[1, step, kind, offset - 1],
            self.place.to_core,
        )

    def own_copy(self, index):
        t, sem = self.place.t, self.own_sem.at[index]
        if index == 0:
            return pltpu.make_async_copy(self.small, self.small_all.at[t], sem)
        if index < 3:
            rows = pl.ds(pl.multiple_of(t * WIDTH, 16), WIDTH)
            return pltpu.make_async_copy(self.blocks[index + 1], self.full[index].at[rows], sem)
        part = index - 3
        rows = pl.ds(pl.multiple_of(part * WIDTH + t * 192, 16), 192)
        block = self.blocks[0].at[pl.ds(part * 192, 192)] if part < 3 else self.blocks[1]
        return pltpu.make_async_copy(block, self.full[0].at[rows], sem)

    def begin(self):
        self.z_start(2)
        for index in range(1, 7):
            self.own_copy(index).start()

    def small_start(self):
        self.own_copy(0).start()
        for offset in self.offsets:
            self.start("small", self.small_copy(offset, self.place.t))

    def advance(self, count=1):
        steps = (self.first, self.second, self.third)
        for step, kind, offset in self.events[:count]:
            steps[step](kind, offset)
        self.events = self.events[count:]

    def advance_kind(self, kind):
        while any(event[1] == kind for event in self.events):
            self.advance()
        self.last(kind)

    def small_ready(self):
        self.own_copy(0).wait()
        for offset in self.offsets:
            self.small_copy(offset, self.place.from_z(offset)).wait_recv()

    def first(self, kind, offset):
        place = self.place
        self.z_copy(kind, offset, place.from_z(offset), self.blocks[1].at[0:SLICE]).wait_recv()
        self.start(kind, self.plane_copy(0, kind, offset, place.d, place.to_x))
        self.start(kind, self.plane_copy(1, kind, offset, place.d, place.to_y))
        self.start(kind, self.core_copy(0, kind, offset, place.d))
        self.z_start(1)

    def second(self, kind, offset):
        place = self.place
        self.plane_copy(0, kind, offset, place.d_x, place.to_x).wait_recv()
        self.start(kind, self.plane_copy(2, kind, offset, place.d_x, place.to_y, HALF, HALF))
        self.start(kind, self.core_copy(1, kind, offset, place.d_x))
        self.plane_copy(1, kind, offset, place.d_y, place.to_y).wait_recv()
        self.start(kind, self.plane_copy(3, kind, offset, place.d_y, place.to_x, 0, HALF))
        self.start(kind, self.core_copy(2, kind, offset, place.d_y))

    def third(self, kind, offset):
        place = self.place
        self.plane_copy(2, kind, offset, place.d_xy, place.to_y, HALF, HALF).wait_recv()
        self.plane_copy(3, kind, offset, place.d_xy, place.to_x, 0, HALF).wait_recv()
        self.start(kind, self.core_copy(3, kind, offset, place.d_xy))

    def last(self, kind):
        place = self.place
        for offset in self.offsets:
            for step, d in enumerate((place.d, place.d_x, place.d_y, place.d_xy)):
                self.core_copy(step, kind, offset, place.core_of(d)).wait_recv()
        for index in range(3, 7) if kind == 0 else (kind,):
            self.own_copy(index).wait()


DOWN, UP, FIRST = 0, 1, 2


class Reduce:
    def __init__(self, place, parts, bufs, outs, sems):
        self.place, self.parts, self.outs = place, parts, outs
        (self.core_in, self.one_in, self.near_in, self.far_in, self.two_in, self.z_in) = bufs
        (
            self.core_sem, self.one_sem, self.near_sem, self.far_sem, self.two_sem, self.z_sem,
            self.plane_sem, self.back_sem, self.free_sem,
        ) = sems
        t = place.t
        near, far = t + 1 - 2 * lax.rem(t, 2), t + 2 - 4 * (t // 2)
        self.blocks = (near, far + 1 - 2 * lax.rem(t, 2), far, t)
        self.major = (place.x, place.y)
        self.minor = (place.y, place.x)
        self.to_major = (place.to_x, place.to_y)
        self.to_minor = (place.to_y, place.to_x)
        self.started = {DOWN: [], UP: [], FIRST: [], "out": []}

    def start(self, kind, copy):
        copy.start()
        self.started[kind].append(copy)

    def sent(self, kind):
        for copy in self.started[kind]:
            copy.wait_send()
        self.started[kind] = []

    def line(self, group):
        return (self.place.dp, self.blocks[group])

    def cells(self, kind, core, group, half=None, major=None, minor=None):
        row, size = (core * 4 + self.blocks[group]) * 8, 8
        if half is not None:
            row, size = row + half * 4 + major * 2, 2
        if minor is not None:
            row, size = row + minor, 1
        return self.parts[kind].at[pl.ds(pl.multiple_of(row * HALF, 16), size * HALF)]

    def own(self, kind, group, half, major=None, minor=None):
        major = self.major[half] if major is None else major
        return self.cells(kind, self.place.core, group, half, major, minor)

    def copy(self, sem, index, src, dst, device):
        return send(src, dst, sem.at[(0,) + index], sem.at[(1,) + index], device)

    def core_copy(self, kind, group):
        src = self.cells(kind, 1 - self.place.core, group)
        dst = self.core_in.at[1 if kind == UP else 0, group]
        return self.copy(self.core_sem, (kind, group), src, dst, self.place.to_core)

    def one_copy(self, kind, group, half):
        src = self.own(kind, group, half, 1 - self.major[half])
        dst = self.one_in.at[kind, group, half]
        return self.copy(self.one_sem, (kind, group, half), src, dst, self.to_major[half])

    def near_copy(self, kind, group, half):
        src, dst = self.own(kind, group, half), self.near_in.at[kind, group, half]
        return self.copy(self.near_sem, (kind, group, half), src, dst, self.line(0))

    def far_copy(self, kind, half):
        src, dst = self.own(kind, 2, half), self.far_in.at[kind, half]
        return self.copy(self.far_sem, (kind, half), src, dst, self.line(2))

    def two_copy(self, kind, group, half):
        src = self.own(kind, group, half, None, 1 - self.minor[half])
        dst = self.two_in.at[kind, group, half]
        return self.copy(self.two_sem, (kind, group, half), src, dst, self.to_minor[half])

    def z_copy(self, group, half):
        src = self.own(FIRST, group, half, None, self.minor[half])
        dst = self.z_in.at[group, half]
        return self.copy(self.z_sem, (group, half), src, dst, self.line(group))

    def rows(self, kind, d, begin=0, size=SLICE):
        return self.outs[kind].at[pl.ds(pl.multiple_of(d * SLICE + begin, 16), size)]

    def plane_copy(self, step, kind, d, device, begin=0, size=SLICE):
        rows = self.rows(kind, d, begin, size)
        return self.copy(self.plane_sem, (step, kind), rows, rows, device)

    def back_copy(self, step, kind, d):
        rows = self.rows(kind, d)
        return self.copy(self.back_sem, (step, kind), rows, rows, self.place.to_core)

    def add(self, ref, addend):
        ref[...] = (ref[...].astype(F32) + addend.astype(F32)).astype(LOW)

    def cross(self, kind, group):
        if kind == FIRST and group == 0:
            pl.semaphore_wait(self.free_sem, 1)
        self.start(kind, self.core_copy(kind, group))

    def one(self, kind, group):
        self.core_copy(kind, group).wait_recv()
        for half in range(2):
            for major in range(2):
                rows = self.own(kind, group, half, major)
                slot, begin = 1 if kind == UP else 0, (half * 2 + major) * SLICE
                self.add(rows, self.core_in[slot, group, begin : begin + SLICE, :])
        for half in range(2):
            self.start(kind, self.one_copy(kind, group, half))
        if kind == DOWN and group == 3:
            pl.semaphore_signal(
                self.free_sem, inc=1, device_id=self.place.to_core, device_id_type=MESH
            )

    def two(self, kind, group):
        for half in range(2):
            self.one_copy(kind, group, half).wait_recv()
            self.add(self.own(kind, group, half), self.one_in[kind, group, half])
            if kind == FIRST:
                self.start(kind, self.two_copy(kind, group, half))
            elif group < 2:
                self.start(kind, self.near_copy(kind, group, half))

    def three(self, kind, group):
        for half in range(2):
            self.two_copy(kind, group, half).wait_recv()
            rows = self.own(kind, group, half, None, self.minor[half])
            self.add(rows, self.two_in[kind, group, half])
            if group < 3:
                self.start(kind, self.z_copy(group, half))

    def keep(self, kind, _):
        for half in range(2):
            self.near_copy(kind, 1, half).wait_recv()
            self.add(self.own(kind, 2, half), self.near_in[kind, 1, half])
            self.start(kind, self.far_copy(kind, half))

    def mine(self, kind, _):
        for half in range(2):
            self.near_copy(kind, 0, half).wait_recv()
            self.far_copy(kind, half).wait_recv()
            rows = self.own(kind, 3, half)
            total = rows[...].astype(F32) + self.near_in[kind, 0, half].astype(F32)
            rows[...] = (total + self.far_in[kind, half].astype(F32)).astype(LOW)
            self.start(kind, self.two_copy(kind, 3, half))

    def final(self, kind, _):
        place = self.place
        for half in range(2):
            total = self.own(kind, 3, half, None, self.minor[half])[...].astype(F32)
            if kind == FIRST:
                for group in range(3):
                    self.z_copy(group, half).wait_recv()
                    total = total + self.z_in[group, half].astype(F32)
            else:
                self.two_copy(kind, 3, half).wait_recv()
                total = total + self.two_in[kind, 3, half].astype(F32)
            self.rows(kind, place.d, half * HALF, HALF)[...] = total.astype(LOW)
        self.start("out", self.plane_copy(0, kind, place.d, place.to_x))
        self.start("out", self.plane_copy(1, kind, place.d, place.to_y))
        self.start("out", self.back_copy(0, kind, place.d))

    def relay(self, kind, _):
        place = self.place
        self.plane_copy(0, kind, place.d_x, place.to_x).wait_recv()
        self.start("out", self.plane_copy(2, kind, place.d_x, place.to_y, HALF, HALF))
        self.start("out", self.back_copy(1, kind, place.d_x))
        self.plane_copy(1, kind, place.d_y, place.to_y).wait_recv()
        self.start("out", self.plane_copy(3, kind, place.d_y, place.to_x, 0, HALF))
        self.start("out", self.back_copy(2, kind, place.d_y))

    def back(self, kind, _):
        place = self.place
        self.plane_copy(2, kind, place.d_xy, place.to_y, HALF, HALF).wait_recv()
        self.plane_copy(3, kind, place.d_xy, place.to_x, 0, HALF).wait_recv()
        self.start("out", self.back_copy(3, kind, place.d_xy))

    def last(self, kind, _):
        place = self.place
        for step, d in enumerate((place.d, place.d_x, place.d_y, place.d_xy)):
            self.back_copy(step, kind, place.core_of(d)).wait_recv()


class Total:
    def __init__(self, place, stages, arrived, line_up, sems):
        self.place, self.stages, self.arrived, self.line_up = place, stages, arrived, line_up
        self.pair_sem, self.z_sem = sems
        self.started = []

    def pair_copy(self, step):
        device = (self.place.to_core, self.place.to_x, self.place.to_y)[step]
        sem = self.pair_sem
        return send(
            self.stages.at[step], self.arrived.at[step], sem.at[0, step], sem.at[1, step], device
        )

    def z_copy(self, offset, source):
        sem = self.z_sem
        return send(
            self.stages.at[3],
            self.line_up.at[source],
            sem.at[0, offset - 1],
            sem.at[1, offset - 1],
            self.place.to_z(offset),
        )

    def start(self, copy):
        copy.start()
        self.started.append(copy)

    def begin(self):
        self.start(self.pair_copy(0))

    def step(self, index):
        self.pair_copy(index).wait_recv()
        self.stages[index + 1] = self.stages[index] + self.arrived[index]
        if index < 2:
            self.start(self.pair_copy(index + 1))
        else:
            for offset in range(1, self.place.tp_size):
                self.start(self.z_copy(offset, self.place.t))
            self.line_up[self.place.t] = self.stages[3]

    def end(self):
        for offset in range(1, self.place.tp_size):
            self.z_copy(offset, self.place.from_z(offset)).wait_recv()
        total = self.line_up[0]
        for t in range(1, self.place.tp_size):
            total = total + self.line_up[t]
        return total

    def finish(self):
        for copy in self.started:
            copy.wait_send()


def part_row(core, t, half, y, x):
    cell = x * 2 + y if half == 0 else y * 2 + x
    return (((core * 4 + t) * 2 + half) * 4 + cell) * HALF


def store_rows(part, core, t, half, cell, begin, values):
    row = pl.multiple_of(part_row(core, t, half, cell // 2, cell % 2) + begin, 16)
    part[pl.ds(row, 16), :] = values.astype(LOW)


def store_part(part, base, values, t):
    for piece in range(values.shape[0] // 16):
        d, inner = divmod(base + piece * 16, SLICE)
        half, begin = divmod(inner, HALF)
        store_rows(part, d % 2, t, half, d // 2, begin, values[piece * 16 : piece * 16 + 16])


def store_first(part, section, base, values):
    for piece in range(values.shape[0] // 16):
        t, inner = divmod(base + piece * 16, 192)
        core, inner = divmod(inner, SLICE)
        half, begin = divmod(inner, HALF)
        store_rows(part, core, t, half, section, begin, values[piece * 16 : piece * 16 + 16])


def total_of(terms):
    result = None
    for term in terms:
        result = term if result is None else result + term
    return result


def feed_cot(cot, vec, feed_low, sums, page):
    for rows in chunks():
        values = cot[page, rows, :].astype(F32) * line(vec, FEED_SCALE)
        sums[DOWN_BIAS] += fold(values)
        feed_low[page, rows, :] = values.astype(LOW)


def down_grad(feed_low, hidden_low, part, t, column):
    grads = [
        dot(hidden_low[t, page, :, tile(column)], feed_low[page], TN) for page in range(PAGES)
    ]
    store_part(part, column * TILE, total_of(grads), t)


def pre_back(feed_low, full_down, slope, sums, t, column):
    row = pl.multiple_of(t * WIDTH + column * TILE, TILE)
    weight = full_down[pl.ds(row, TILE), :]
    folds = []
    for page in range(PAGES):
        pre_cot = dot(feed_low[page], weight, NT) * slope[t, page, :, tile(column)].astype(F32)
        folds.append(fold(pre_cot))
        slope[t, page, :, tile(column)] = pre_cot.astype(LOW)
    sums[UP_BIAS + t, :, tile(column)] = total_of(folds)


def up_back(second_t, pre_cot, part, t, column):
    grads = [dot(second_t[page, tile(column), :], pre_cot[t, page], NN) for page in range(PAGES)]
    store_part(part, column * TILE, total_of(grads), t)


def second_cot(pre_cot, full_up, result, tp_size, page):
    for column in range(3):
        terms = []
        for t in range(tp_size):
            rows = slice(t * WIDTH + column * TILE, t * WIDTH + column * TILE + TILE)
            terms.append(dot(pre_cot[t, page], full_up[rows, :], NT))
        result[page, :, tile(column)] = total_of(terms)


def norm_back(features, cot, gain, sums, gain_row, shift_row):
    norm, scale = norm_parts(features)
    sums[gain_row] += fold(cot * norm)
    sums[shift_row] += fold(cot)
    cot = cot * gain
    mean = jnp.mean(cot, axis=-1, keepdims=True)
    along = jnp.mean(cot * norm, axis=-1, keepdims=True)
    return scale * (cot - mean - norm * along)


def second_back(middle, result, cot, branch, vec, sums, branch_low, page):
    for rows in chunks():
        part = norm_back(
            middle[page, rows, :], result[page, rows, :], line(vec, GAIN_2), sums, GAIN_2, SHIFT_2
        )
        middle_cot = cot[page, rows, :].astype(F32) + part
        middle[page, rows, :] = middle_cot
        sums[ATT_SCALE] += fold(middle_cot * branch[page, rows, :])
        branch_cot = middle_cot * line(vec, ATT_SCALE)
        sums[OUT_BIAS] += fold(branch_cot)
        branch_low[page, rows, :] = branch_cot.astype(LOW)


def attended_back(branch_low, full_a, attended_cot, page):
    for column in range(3):
        rows = slice(3 * WIDTH + column * TILE, 3 * WIDTH + column * TILE + TILE)
        result = dot(branch_low[page], full_a[rows, :], NT)
        attended_cot[page, :, tile(column)] = result.astype(LOW)


def attend_back(heads, expo, scale, attended_cot, scores, page, pair):
    lanes = slice(pair * 128, pair * 128 + 128)
    query, key, value = (heads[part, page, :, lanes] for part in range(3))
    cot = attended_cot[page, :, lanes]
    lane = lax.broadcasted_iota(jnp.int32, (SEQ, 128), 1)
    zero = jnp.zeros_like(query)
    key_t = key.T
    query_cots, key_cots, value_cots = [], [], []
    for which in range(2):
        head = 2 * pair + which
        keep = lane < 64 if which == 0 else lane >= 64
        head_query, head_cot = jnp.where(keep, query, zero), jnp.where(keep, cot, zero)
        prob_cot = dot(value, head_cot, NT)
        columns = slice((head % 3) * TILE, (head % 3) * TILE + SEQ)
        probs = expo[head // 3, page, :, columns].astype(F32) * scale[page, head : head + 1, :]
        product = probs * prob_cot
        score_cot = product - probs * jnp.sum(product, axis=0, keepdims=True)
        for half, width in ((0, 128), (1, SEQ - 128)):
            rows = slice((half * HEADS + head) * SEQ, (half * HEADS + head + 1) * SEQ)
            scores[rows, 0:width] += score_cot[:, half * 128 : half * 128 + width]
        score_cot = score_cot.astype(LOW)
        value_cots.append(dot(probs.astype(LOW), head_cot, NN))
        key_cots.append(dot(score_cot, head_query, NN))
        query_cots.append(dot(key_t[64 * which : 64 * which + 64], score_cot, NN))
    heads[0, page, :, lanes] = (jnp.concatenate(query_cots, axis=0).T * 0.125).astype(LOW)
    heads[1, page, :, lanes] = total_of(key_cots).astype(LOW)
    heads[2, page, :, lanes] = total_of(value_cots).astype(LOW)


def section_back(heads, right, part, sums, section, column):
    pieces = [heads[section, page, :, tile(column)] for page in range(PAGES)]
    grads = [dot(pieces[page], right[page], TN) for page in range(PAGES)]
    if section in (0, 2):
        index = Q_BIAS if section == 0 else V_BIAS
        sums[index, :, tile(column)] = total_of([fold(piece.astype(F32)) for piece in pieces])
    store_first(part, section, column * TILE, total_of(grads))


def first_cot(heads, full_a, result, page):
    for column in range(3):
        terms = [
            dot(heads[part, page], full_a[part * WIDTH : (part + 1) * WIDTH, tile(column)], NN)
            for part in range(3)
        ]
        result[page, :, tile(column)] = total_of(terms)


def first_back(patches, hide, vec, result, middle, sums, page):
    for rows in chunks():
        features = enter(patches, hide, vec, page, rows)
        part = norm_back(
            features, result[page, rows, :], line(vec, GAIN_1), sums, GAIN_1, SHIFT_1
        )
        entered_cot = middle[page, rows, :] + part
        hidden = hide[rows, page : page + 1] > 0
        result[page, rows, :] = jnp.where(hidden, 0.0, entered_cot)
        sums[EMBED] += fold(jnp.where(hidden, entered_cot, 0.0))


def table_back(scores, index_t, packed):
    row = lax.broadcasted_iota(jnp.int32, (128, TILE), 0)
    unroll = 20

    def step(index, total):
        lefts, rights = [], []
        for inner in range(unroll):
            key = index * unroll + inner
            halves = [
                scores[pl.ds(half * HEADS * SEQ + key, HEADS, stride=SEQ), :] for half in range(2)
            ]
            terms = jnp.concatenate(halves, axis=1)
            terms = jnp.concatenate([terms, jnp.zeros((4, TILE), F32)], axis=0)
            entry = index_t[pl.ds(key, 1), :]
            low_part, high_part = entry & 127, entry >> 7
            match = jnp.broadcast_to(low_part, (128, TILE)) == row
            rights.append(jnp.where(match, 1.0, 0.0).astype(LOW))
            picked = [jnp.where(high_part == part, terms, 0.0).astype(LOW) for part in range(6)]
            lefts.append(jnp.concatenate(picked, axis=0))
        return total + dot(jnp.concatenate(lefts, axis=1), jnp.concatenate(rights, axis=1), NT)

    total = lax.fori_loop(0, SEQ // unroll, step, jnp.zeros((96, 128), F32))
    for part in range(6):
        packed[16:32, part * 128 : part * 128 + 128] = total[part * 16 : part * 16 + 16]


def layer_kernel(tp_size, *refs):
    blocks = refs[:4]
    patches, cot, mask, index, table, bias_up, bias_qv = refs[4:11]
    vec_in = refs[11:20]
    sums_out, total_out = refs[20:23], refs[23]
    output, patch_out, expo_out, heads_out = refs[24:28]
    outs, refs = refs[28:31], refs[31:]
    full, small_all, small = refs[0:3], refs[3], refs[4]
    wide, inner, parts = refs[5:8]
    bufs = refs[8:14]
    scores_t, branch, middle, result, second_t, first_low, second_low, feed_low = refs[14:22]
    sums, stages, arrived, line_up = refs[22:26]
    vec, hide, index_t, scale, bias_rows, up_bias = refs[26:32]
    local_sem = refs[32]
    gather_sems, reduce_sems, total_sems = refs[33:38], refs[38:47], refs[47:49]
    place = Place(tp_size)
    gather = Gather(place, blocks, small, full, small_all, gather_sems)
    reduce = Reduce(place, (parts.at[0], parts.at[1], full[1]), bufs, outs, reduce_sems)
    total = Total(place, stages, arrived, line_up, total_sems)
    pair_bias = scores = scores_t

    def local(index, src, dst):
        return pltpu.make_async_copy(src, dst, local_sem.at[index])

    meet(place)
    gather.begin()
    small[0:3, 0:NUM_REL] = table[...].astype(F32)
    small[3:4, :] = bias_up[...].astype(F32).reshape(1, WIDTH)
    small[4:6, 0:192] = bias_qv[...].astype(F32)
    gather.small_start()
    for row, values in enumerate(vec_in):
        vec[row : row + 1, :] = values[...].reshape(1, WIDTH)
    place_in_page = lax.broadcasted_iota(jnp.int32, (PAGES, SEQ), 1)
    patch = (place_in_page >= 1) & (place_in_page <= PATCHES)
    pages = [mask[pl.ds(SEQ * page, SEQ)].reshape(1, SEQ) for page in range(PAGES)]
    hidden = jnp.where((jnp.concatenate(pages, axis=0) > 0) & patch, 1.0, 0.0)
    hide[...] = jnp.concatenate([hidden, jnp.zeros((8 - PAGES, SEQ), F32)], axis=0).T
    index_t[...] = jnp.zeros_like(index_t)
    index_t[:, 0:SEQ] = index[...].astype(F32).T.astype(jnp.int32)
    sums[...] = jnp.zeros_like(sums)
    for page in range(PAGES):
        first_norm(patches, hide, vec, first_low, page)
    gather.small_ready()
    for t in range(tp_size):
        columns = slice(192 * t, 192 * t + 192)
        up_bias[t : t + 1, :] = small_all[t, 3:4, :]
        bias_rows[0:1, columns] = small_all[t, 4:5, 0:192]
        bias_rows[1:2, columns] = small_all[t, 5:6, 0:192]
    for head in range(HEADS):
        lookup(small_all, index_t, pair_bias, head)
        if head % 2 == 1:
            gather.advance()
    gather.advance_kind(0)
    for part in range(3):
        for column in range(3):
            project(first_low, full[0], bias_rows, inner, part, column)
        gather.advance(part % 2)
    for page in range(PAGES):
        for pair in range(HEADS // 2):
            attend(inner, pair_bias, wide, scale, page, pair)
        gather.advance()
    saves = [local(0, wide, expo_out), local(1, inner, heads_out)]
    for copy in saves:
        copy.start()
    for page in range(PAGES):
        out_project(inner, full[0], vec, patches, hide, branch, middle, page)
        second_norm(middle, vec, second_low, page)
        second_t[page] = second_low[page].T
        feed_cot(cot, vec, feed_low, sums, page)
    for copy in saves:
        copy.wait()
    scores[...] = jnp.zeros_like(scores)
    gather.advance_kind(1)
    for t in range(tp_size):
        for column in range(3):
            feed_up(second_low, full[1], up_bias, wide, inner, t, column)
        gather.advance(t % 2)
    for group in range(4):
        for column in range(3):
            down_grad(feed_low, wide, parts.at[DOWN], reduce.blocks[group], column)
        reduce.cross(DOWN, group)
        gather.advance(group % 2)
    gather.advance(len(gather.events))
    reduce.one(DOWN, 0)
    reduce.one(DOWN, 1)
    gather.last(2)
    reduce.one(DOWN, 2)
    reduce.one(DOWN, 3)

    def run(*events):
        for step, kind, group in events:
            step(kind, group)

    cross, one, two, three = reduce.cross, reduce.one, reduce.two, reduce.three
    keep, mine, final = reduce.keep, reduce.mine, reduce.final
    relay, back, last = reduce.relay, reduce.back, reduce.last

    after_up = (
        ((cross, UP, 0),),
        ((cross, UP, 1), (one, UP, 0), (two, DOWN, 0)),
        ((cross, UP, 2), (one, UP, 1), (two, DOWN, 1)),
        ((cross, UP, 3), (one, UP, 2), (two, DOWN, 2)),
    )
    for group in range(4):
        t = reduce.blocks[group]
        for column in range(3):
            pre_back(feed_low, full[2], inner, sums, t, column)
        for column in range(3):
            up_back(second_t, inner, parts.at[UP], t, column)
        run(*after_up[group])
    after_feed = (((one, UP, 3),), ((two, DOWN, 3),), ())
    for page in range(PAGES):
        feed_down(wide, full[2], vec, middle, cot, result, sums, tp_size, page)
        run(*after_feed[page])
    output_copy = local(2, result, output)
    output_copy.start()
    loads = [local(3, expo_out, wide), local(4, heads_out, inner)]
    loads[0].start()
    output_copy.wait()
    after_second = ((), (), ((two, UP, 0),))
    for page in range(PAGES):
        second_cot(inner, full[1], result, tp_size, page)
        run(*after_second[page])
    loads[1].start()
    branch_low, attended_cot = feed_low, second_low
    for page in range(PAGES):
        second_back(middle, result, cot, branch, vec, sums, branch_low, page)
    run((keep, DOWN, 0))
    for page in range(PAGES):
        attended_back(branch_low, full[0], attended_cot, page)
    run((two, UP, 1))
    for copy in loads:
        copy.wait()
    after_attend = (((two, UP, 2),), ((two, UP, 3),), ())
    for page in range(PAGES):
        for pair in range(HEADS // 2):
            attend_back(inner, wide, scale, attended_cot, scores, page, pair)
        run(*after_attend[page])
    gather.sent(1)
    for section in (3, 0, 1, 2):
        right = branch_low if section == 3 else first_low
        for column in range(3):
            section_back(inner, right, full[1], sums, section, column)
    run(*((cross, FIRST, group) for group in range(4)))
    first_cot(inner, full[0], result, 0)
    run((mine, DOWN, 0), (one, FIRST, 0), (one, FIRST, 1))
    first_cot(inner, full[0], result, 1)
    run((one, FIRST, 2), (one, FIRST, 3))
    first_cot(inner, full[0], result, 2)
    run((keep, UP, 0), (final, DOWN, 0))
    for page in range(PAGES):
        first_back(patches, hide, vec, result, middle, sums, page)
    patch_copy = local(5, result, patch_out)
    patch_copy.start()
    run((two, FIRST, 0))
    table_back(scores, index_t, stages.at[0])
    stages[0, 0:16, :] = jnp.sum(sums[...], axis=1)
    total.begin()
    run((relay, DOWN, 0), (two, FIRST, 1), (three, FIRST, 0), (mine, UP, 0))
    total.step(0)
    run((two, FIRST, 2), (three, FIRST, 1), (back, DOWN, 0), (final, UP, 0))
    total.step(1)
    run((two, FIRST, 3), (three, FIRST, 2), (relay, UP, 0))
    total.step(2)
    run((three, FIRST, 3), (last, DOWN, 0), (back, UP, 0))
    total_out[...] = total.end()
    run((final, FIRST, 0), (relay, FIRST, 0), (back, FIRST, 0))
    run((last, UP, 0), (last, FIRST, 0))
    sum_copies = [local(6 + kind, outs[kind], sums_out[kind]) for kind in range(3)]
    for copy in sum_copies:
        copy.start()
    patch_copy.wait()
    for kind in (DOWN, UP, FIRST, "out"):
        reduce.sent(kind)
    for kind in (0, 2, "small"):
        gather.sent(kind)
    total.finish()
    for copy in sum_copies:
        copy.wait()


ANY = pl.BlockSpec(memory_space=pl.ANY)
VMEM = pl.BlockSpec(memory_space=pltpu.VMEM)


def layer(blocks, local_args, vec_rows, tp_size):
    dma, regular = pltpu.SemaphoreType.DMA, pltpu.SemaphoreType.REGULAR
    shape, scratch = jax.ShapeDtypeStruct, pltpu.VMEM
    page_shape = (PAGES, SEQ, WIDTH)
    quarter = (SLICE, WIDTH)
    return pl.pallas_call(
        functools.partial(layer_kernel, tp_size),
        out_shape=[shape((WIDTH, WIDTH), LOW)] * 3
        + [
            shape((32, WIDTH), F32),
            shape(page_shape, F32),
            shape(page_shape, F32),
            shape((4,) + page_shape, LOW),
            shape((4,) + page_shape, LOW),
        ],
        in_specs=[ANY] * 4 + [VMEM] * 16,
        out_specs=[ANY] * 3 + [VMEM] + [ANY] * 4,
        scratch_shapes=[scratch((WIDTH, WIDTH), LOW)] * 3
        + [scratch((tp_size * WIDTH, WIDTH), LOW)] * 3
        + [
            scratch((tp_size, 8, WIDTH), F32),
            scratch((8, WIDTH), F32),
            scratch((4,) + page_shape, LOW),
            scratch((4,) + page_shape, LOW),
            scratch((2, 32 * SLICE, WIDTH), LOW),
            scratch((2, 4, 4 * SLICE, WIDTH), LOW),
            scratch((3, 4, 2) + quarter, LOW),
            scratch((2, 2, 2) + quarter, LOW),
            scratch((2, 2) + quarter, LOW),
            scratch((3, 4, 2, HALF, WIDTH), LOW),
            scratch((3, 2, HALF, WIDTH), LOW),
            scratch((2 * HEADS * SEQ, 128), F32),
            scratch(page_shape, F32),
            scratch(page_shape, F32),
            scratch(page_shape, F32),
            scratch((PAGES, WIDTH, SEQ), LOW),
            scratch(page_shape, LOW),
            scratch(page_shape, LOW),
            scratch(page_shape, LOW),
            scratch((16, 8, WIDTH), F32),
            scratch((4, 32, WIDTH), F32),
            scratch((3, 32, WIDTH), F32),
            scratch((tp_size, 32, WIDTH), F32),
            scratch((16, WIDTH), F32),
            scratch((SEQ, 8), F32),
            scratch((SEQ, TILE), jnp.int32),
            scratch((PAGES, 16, SEQ), F32),
            scratch((8, WIDTH), F32),
            scratch((8, WIDTH), F32),
            dma((9,)),
            dma((7,)),
            dma((2, 3, tp_size - 1)),
            dma((2, tp_size - 1)),
            dma((2, 4, 3, tp_size - 1)),
            dma((2, 4, 3, tp_size - 1)),
            dma((2, 3, 4)),
            dma((2, 3, 4, 2)),
            dma((2, 2, 2, 2)),
            dma((2, 2, 2)),
            dma((2, 3, 4, 2)),
            dma((2, 3, 2)),
            dma((2, 4, 3)),
            dma((2, 4, 3)),
            regular,
            dma((2, 3)),
            dma((2, tp_size - 1)),
        ],
        compiler_params=pltpu.CompilerParams(
            collective_id=0, has_side_effects=True, vmem_limit_bytes=64 * 1024 * 1024 - 65536
        ),
    )(*blocks, *local_args, *vec_rows)


def finish_kernel(tp_size, *refs):
    sums, totals, output, patch = refs[:3], *refs[3:6]
    project_out, output_out, up_out, down_out, layer_out, patch_out = refs[6:12]
    rows_out, bias_out, table_out, bias_up = refs[12:21], *refs[21:24]
    low, wide, total, pages, sem = refs[24:29]
    loads = [pltpu.make_async_copy(totals, total, sem.at[0])]
    for kind in range(3):
        loads.append(pltpu.make_async_copy(sums[kind], low.at[kind], sem.at[1 + kind]))
    loads.append(pltpu.make_async_copy(output, pages.at[0], sem.at[4]))
    loads.append(pltpu.make_async_copy(patch, pages.at[1], sem.at[5]))
    for copy in loads:
        copy.start()
    copies = []
    for kind, target in enumerate((down_out, up_out, None)):
        loads[1 + kind].wait()
        for part in range(4):
            rows = slice(part * 192, part * 192 + 192)
            wide[kind, rows, :] = low[kind, rows, :].astype(F32)
            if kind < FIRST:
                dst = target.at[rows]
            else:
                dst = project_out.at[rows] if part < 3 else output_out
            copies.append(
                pltpu.make_async_copy(wide.at[kind, rows], dst, sem.at[6 + len(copies)])
            )
            copies[-1].start()
    for index, target in enumerate((layer_out, patch_out)):
        loads[4 + index].wait()
        copies.append(
            pltpu.make_async_copy(pages.at[index], target, sem.at[6 + len(copies)])
        )
        copies[-1].start()
    loads[0].wait()
    for row, target in enumerate(rows_out):
        target[...] = total[row : row + 1, :].reshape(WIDTH)
    for t in range(tp_size):

        @pl.when(lax.axis_index("tp") == t)
        def _():
            bias_out[...] = total[Q_BIAS : Q_BIAS + 2, 192 * t : 192 * t + 192]
            table_out[...] = total[16 + 3 * t : 19 + 3 * t, 0:NUM_REL]
            bias_up[...] = total[UP_BIAS + t : UP_BIAS + t + 1, :].reshape(WIDTH)

    for copy in copies:
        copy.wait()


def finish(values, tp_size):
    shape = jax.ShapeDtypeStruct
    page_shape = (PAGES, SEQ, WIDTH)
    return pl.pallas_call(
        functools.partial(finish_kernel, tp_size),
        out_shape=[
            shape((3 * 192, WIDTH), F32),
            shape((192, WIDTH), F32),
            shape((WIDTH, WIDTH), F32),
            shape((WIDTH, WIDTH), F32),
            shape(page_shape, F32),
            shape(page_shape, F32),
        ]
        + [shape((WIDTH,), F32)] * 9
        + [shape((2, 192), F32), shape((3, NUM_REL), F32), shape((WIDTH,), F32)],
        in_specs=[ANY] * 6,
        out_specs=[ANY] * 6 + [VMEM] * 12,
        scratch_shapes=[
            pltpu.VMEM((3, WIDTH, WIDTH), values[0].dtype),
            pltpu.VMEM((3, WIDTH, WIDTH), F32),
            pltpu.VMEM((32, WIDTH), F32),
            pltpu.VMEM((2,) + page_shape, F32),
            pltpu.SemaphoreType.DMA((20,)),
        ],
        compiler_params=pltpu.CompilerParams(vmem_limit_bytes=63 << 20),
    )(*values)


def body(tp_size, dp_size, *args):
    (
        patches, page_mask, pair_index, mask_embed, first_gain, first_shift, project_weight,
        project_bias, pair_table, output_weight, output_bias, attention_scale, second_gain,
        second_shift, up_weight, up_bias, down_weight, down_bias, feed_scale, cotangent,
    ) = args
    row_count = patches.shape[0]
    project_rows = jnp.transpose(project_weight, (1, 2, 0)).reshape(3 * 192, WIDTH)
    vec_rows = (
        mask_embed, first_gain, first_shift, output_bias, attention_scale, second_gain,
        second_shift, down_bias, feed_scale,
    )
    local_args = (
        patches.reshape(PAGES, SEQ, WIDTH),
        cotangent.reshape(PAGES, SEQ, WIDTH),
        page_mask,
        pair_index,
        jnp.transpose(pair_table),
        up_bias,
        project_bias,
    )
    values = layer(
        (project_rows, output_weight, up_weight, down_weight),
        local_args,
        vec_rows,
        tp_size,
    )[:6]
    if dp_size > GROUP:
        groups = [[i + GROUP * j for j in range(dp_size // GROUP)] for i in range(GROUP)]
        sums = [value.astype(F32) for value in values[:4]]
        values = list(lax.psum(sums, "dp", axis_index_groups=groups)) + list(values[4:])
    results = finish(values, tp_size)
    project_sum, output_sum, up_sum, down_sum, layer_output, patch_gradient = results[:6]
    rows = results[6:15]
    bias_sum, table_sum, up_bias_sum = results[15:]
    return (
        layer_output.reshape(row_count, WIDTH),
        patch_gradient.reshape(row_count, WIDTH),
        rows[EMBED],
        rows[GAIN_1],
        rows[SHIFT_1],
        jnp.transpose(project_sum.reshape(3, 192, WIDTH), (2, 0, 1)),
        bias_sum,
        jnp.transpose(table_sum),
        output_sum,
        rows[OUT_BIAS],
        rows[ATT_SCALE],
        rows[GAIN_2],
        rows[SHIFT_2],
        up_sum,
        up_bias_sum,
        down_sum,
        rows[DOWN_BIAS],
        rows[FEED_SCALE],
    )


def solution(mesh):
    rows, heads = P(("dp", "tp"), None), P(None, "tp")
    in_specs = (
        rows, P(("dp", "tp")), P(), P(), P(), P(), P(None, None, "tp"), heads, heads,
        P("tp", None), P(), P(), P(), P(), heads, P("tp"), P("tp", None), P(), P(), rows,
    )
    out_specs = (
        rows, rows, P(), P(), P(), P(None, None, "tp"), heads, heads, P("tp", None), P(), P(),
        P(), P(), heads, P("tp"), P("tp", None), P(), P(),
    )
    step = functools.partial(body, mesh.shape["tp"], mesh.shape["dp"])
    return jax.shard_map(step, mesh=mesh, in_specs=in_specs, out_specs=out_specs, check_vma=False)
```

```python
import functools

import jax
import jax.numpy as jnp
from jax import lax
from jax.experimental import pallas as pl
from jax.experimental.pallas import tpu as pltpu
from jax.sharding import PartitionSpec as P

SEQ = 200
PATCHES = 196
NUM_REL = 732
PAGES = 3
HEADS = 12
WIDTH = 768
GROUP = 8
SLICE = 96
HALF = 48
MESH = pl.DeviceIdType.MESH


class Place:
    def __init__(self, tp_size):
        self.tp_size = tp_size
        self.dp = lax.axis_index("dp")
        self.t = lax.axis_index("tp")
        self.d = lax.rem(self.dp, GROUP)
        self.core = lax.rem(self.d, 2)
        self.x = lax.rem(self.d // 2, 2)
        self.y = self.d // 4
        self.to_core = (self.dp + 1 - 2 * self.core, self.t)
        self.to_x = (self.dp + 2 - 4 * self.x, self.t)
        self.to_y = (self.dp + 4 - 8 * self.y, self.t)
        self.d_x = self.d + 2 - 4 * self.x
        self.d_y = self.d + 4 - 8 * self.y
        self.d_xy = self.d_x + 4 - 8 * self.y

    def core_of(self, d):
        return d + 1 - 2 * self.core

    def to_z(self, offset):
        return (self.dp, lax.rem(self.t + offset, self.tp_size))

    def from_z(self, offset):
        return lax.rem(self.t + self.tp_size - offset, self.tp_size)


def partners(place):
    others = [place.to_core, place.to_x, place.to_y]
    return others + [place.to_z(offset) for offset in range(1, place.tp_size)]


def greet(place):
    barrier = pltpu.get_barrier_semaphore()
    for other in partners(place):
        pl.semaphore_signal(barrier, inc=1, device_id=other, device_id_type=MESH)


def meet(place):
    pl.semaphore_wait(pltpu.get_barrier_semaphore(), len(partners(place)))


def send(src, dst, send_sem, recv_sem, device):
    return pltpu.make_async_remote_copy(
        src_ref=src,
        dst_ref=dst,
        send_sem=send_sem,
        recv_sem=recv_sem,
        device_id=device,
        device_id_type=MESH,
    )


def slice_row(kind, t, d):
    if kind == 0:
        row = (d // 2) * 768 + t * 192 + lax.rem(d, 2) * SLICE
    else:
        row = t * 768 + d * SLICE
    return pl.multiple_of(row, 16)


LOW = jnp.bfloat16
F32 = jnp.float32
CHUNKS = ((0, 48), (48, 48), (96, 48), (144, 56))
TILE = 256
NT = (((1,), (1,)), ((), ()))
NN = (((1,), (0,)), ((), ()))
TN = (((0,), (0,)), ((), ()))
EMBED, GAIN_1, SHIFT_1, OUT_BIAS, ATT_SCALE, GAIN_2, SHIFT_2, DOWN_BIAS, FEED_SCALE = range(9)
Q_BIAS, V_BIAS, UP_BIAS = 9, 10, 12


def dot(left, right, dims):
    return lax.dot_general(left, right, dims, preferred_element_type=F32)


def line(ref, index):
    return ref[index : index + 1, :]


def tile(index):
    return slice(index * TILE, index * TILE + TILE)


def fold(values):
    return jnp.sum(values.reshape(values.shape[0] // 8, 8, values.shape[1]), axis=0)


def norm_parts(features):
    center = features - jnp.mean(features, axis=-1, keepdims=True)
    scale = lax.rsqrt(jnp.mean(center * center, axis=-1, keepdims=True) + 1e-6)
    return center * scale, scale


def enter(patches, hide, vec, page, rows):
    features = patches[page, rows, :].astype(F32)
    return jnp.where(hide[rows, page : page + 1] > 0, line(vec, EMBED), features)


def chunks():
    return [slice(start, start + size) for start, size in CHUNKS]


def first_norm(patches, hide, vec, first_low, page):
    for rows in chunks():
        norm, _ = norm_parts(enter(patches, hide, vec, page, rows))
        first_low[page, rows, :] = (norm * line(vec, GAIN_1) + line(vec, SHIFT_1)).astype(LOW)


def lookup(small_all, index_t, pair_bias, head):
    block, place = head // 3, head % 3
    table = small_all[block, place : place + 1, :]
    for half in range(2):
        index = index_t[:, 128 * half : 128 * half + 128]
        low_part, high_part = index & 127, index >> 7
        found = None
        for part in range(6):
            entries = jnp.broadcast_to(table[:, 128 * part : 128 * part + 128], (SEQ, 128))
            got = jnp.take_along_axis(entries, low_part, axis=1)
            found = got if found is None else jnp.where(high_part == part, got, found)
        key = lax.broadcasted_iota(jnp.int32, (SEQ, 128), 0)
        rows = slice((half * HEADS + head) * SEQ, (half * HEADS + head + 1) * SEQ)
        pair_bias[rows, :] = jnp.where(key > PATCHES, -1e30, found)


def project(first_low, full_a, bias_rows, heads, part, column):
    weight = full_a[part * WIDTH + column * TILE : part * WIDTH + column * TILE + TILE, :]
    for page in range(PAGES):
        result = dot(first_low[page], weight, NT)
        if part == 0:
            result = (result + bias_rows[0:1, tile(column)]) * 0.125
        elif part == 2:
            result = result + bias_rows[1:2, tile(column)]
        heads[part, page, :, tile(column)] = result.astype(LOW)


def attend(heads, pair_bias, expo, scale, page, pair):
    lanes = slice(pair * 128, pair * 128 + 128)
    query, key, value = (heads[part, page, :, lanes] for part in range(3))
    lane = lax.broadcasted_iota(jnp.int32, (SEQ, 128), 1)
    value_t = value.T
    outs = []
    for which in range(2):
        head = 2 * pair + which
        keep = lane < 64 if which == 0 else lane >= 64
        scores = dot(key, jnp.where(keep, query, jnp.zeros_like(query)), NT)
        left = pair_bias[head * SEQ : (head + 1) * SEQ, :]
        right = pair_bias[(HEADS + head) * SEQ : (HEADS + head + 1) * SEQ, :]
        scores = scores + jnp.concatenate([left, right], axis=1)[:, 0:SEQ]
        raised = jnp.exp(scores - jnp.max(scores, axis=0, keepdims=True))
        inverse = 1.0 / jnp.sum(raised, axis=0, keepdims=True)
        raised = raised.astype(LOW)
        expo[head // 3, page, :, (head % 3) * TILE : (head % 3) * TILE + SEQ] = raised
        scale[page, head : head + 1, :] = inverse
        outs.append(dot(value_t[64 * which : 64 * which + 64], raised, NN) * inverse)
    heads[3, page, :, lanes] = jnp.concatenate(outs, axis=0).T.astype(LOW)


def out_project(heads, full_a, vec, patches, hide, branch, middle, page):
    for column in range(3):
        weight = full_a[3 * WIDTH : 4 * WIDTH, tile(column)]
        branch[page, :, tile(column)] = dot(heads[3, page], weight, NN) + vec[3:4, tile(column)]
    for rows in chunks():
        entered = enter(patches, hide, vec, page, rows)
        middle[page, rows, :] = entered + line(vec, ATT_SCALE) * branch[page, rows, :]


def second_norm(middle, vec, second_low, page):
    for rows in chunks():
        norm, _ = norm_parts(middle[page, rows, :])
        second_low[page, rows, :] = (norm * line(vec, GAIN_2) + line(vec, SHIFT_2)).astype(LOW)


def feed_up(second_low, full_up, up_bias, hidden_low, slope, t, column):
    weight = full_up[t * WIDTH : (t + 1) * WIDTH, tile(column)]
    bias = up_bias[t : t + 1, tile(column)]
    for page in range(PAGES):
        pre = dot(second_low[page], weight, NN) + bias
        portion = 0.5 * (1.0 + lax.erf(pre * 0.7071067811865476))
        hidden_low[t, page, :, tile(column)] = (pre * portion).astype(LOW)
        bell = jnp.exp(-0.5 * pre * pre) * 0.3989422804014327
        slope[t, page, :, tile(column)] = (portion + pre * bell).astype(LOW)


def feed_down(hidden_low, full_down, vec, patches, hide, cot, branch, sums, tp_size, page):
    for column in range(3):
        columns = tile(column)
        total = None
        for t in range(tp_size):
            weight = full_down[t * WIDTH : (t + 1) * WIDTH, columns]
            term = dot(hidden_low[t, page], weight, NN)
            total = term if total is None else total + term
        total = total + vec[DOWN_BIAS : DOWN_BIAS + 1, columns]
        entered = patches[page, :, columns].astype(F32)
        entered = jnp.where(hide[:, page : page + 1] > 0, vec[EMBED : EMBED + 1, columns], entered)
        middle = entered + vec[ATT_SCALE : ATT_SCALE + 1, columns] * branch[page, :, columns]
        branch[page, :, columns] = middle + vec[FEED_SCALE : FEED_SCALE + 1, columns] * total
        sums[FEED_SCALE, :, columns] += fold(cot[page, :, columns].astype(F32) * total)


FIRST_DUE, TICK = 5.0, 5.0


class Gather:
    def __init__(self, place, blocks, small, full, small_all, sems):
        self.place, self.blocks, self.small = place, blocks, small
        self.full, self.small_all = full, small_all
        self.own_sem, self.z_sem, self.small_sem, self.plane_sem, self.core_sem = sems
        self.offsets = range(1, place.tp_size)
        self.started = {0: [], 1: [], 2: [], "small": []}
        self.waiting = [(kind, offset) for kind in range(3) for offset in (1, 3, 2)]
        order = tuple(self.waiting)
        self.events = [
            (FIRST_DUE + TICK * tick, step) + order[tick - step]
            for tick in range(len(order) + 2)
            for step in range(3)
            if 0 <= tick - step < len(order)
        ]
        self.clock = 0.0

    def start(self, kind, copy):
        copy.start()
        self.started[kind].append(copy)

    def sent(self, kind):
        for copy in self.started[kind]:
            copy.wait_send()
        self.started[kind] = []

    def rows(self, kind, t, d, start=0, size=SLICE):
        row = pl.multiple_of(slice_row(kind, t, d) + start, 16)
        return self.full[kind].at[pl.ds(row, size)]

    def z_copy(self, kind, offset, source, block=None):
        place = self.place
        if block is None:
            block = self.blocks[kind + 1].at[pl.ds(pl.multiple_of(place.d * SLICE, 16), SLICE)]
        return send(
            block,
            self.rows(kind, source, place.d),
            self.z_sem.at[0, kind, offset - 1],
            self.z_sem.at[1, kind, offset - 1],
            place.to_z(offset),
        )

    def z_start(self, count):
        place = self.place
        for kind, offset in self.waiting[:count]:
            if kind:
                self.start(kind, self.z_copy(kind, offset, place.t))
                continue

            @pl.when(place.d < 6)
            def _():
                rows = pl.ds(pl.multiple_of(place.d * SLICE, 16), SLICE)
                self.z_copy(0, offset, place.t, self.blocks[0].at[rows]).start()

            @pl.when(place.d >= 6)
            def _():
                rows = pl.ds(pl.multiple_of((place.d - 6) * SLICE, 16), SLICE)
                self.z_copy(0, offset, place.t, self.blocks[1].at[rows]).start()

            rows = pl.ds(0, SLICE)
            self.started[0].append(self.z_copy(0, offset, place.t, self.blocks[1].at[rows]))
        self.waiting = self.waiting[count:]

    def small_copy(self, offset, source):
        return send(
            self.small,
            self.small_all.at[source],
            self.small_sem.at[0, offset - 1],
            self.small_sem.at[1, offset - 1],
            self.place.to_z(offset),
        )

    def plane_copy(self, step, kind, offset, d, device, start=0, size=SLICE):
        rows = self.rows(kind, self.place.from_z(offset), d, start, size)
        return send(
            rows,
            rows,
            self.plane_sem.at[0, step, kind, offset - 1],
            self.plane_sem.at[1, step, kind, offset - 1],
            device,
        )

    def core_copy(self, step, kind, offset, d):
        rows = self.rows(kind, self.place.from_z(offset), d)
        return send(
            rows,
            rows,
            self.core_sem.at[0, step, kind, offset - 1],
            self.core_sem.at[1, step, kind, offset - 1],
            self.place.to_core,
        )

    def own_copy(self, index):
        t, sem = self.place.t, self.own_sem.at[index]
        if index == 0:
            return pltpu.make_async_copy(self.small, self.small_all.at[t], sem)
        if index < 3:
            rows = pl.ds(pl.multiple_of(t * WIDTH, 16), WIDTH)
            return pltpu.make_async_copy(self.blocks[index + 1], self.full[index].at[rows], sem)
        part = index - 3
        rows = pl.ds(pl.multiple_of(part * WIDTH + t * 192, 16), 192)
        block = self.blocks[0].at[pl.ds(part * 192, 192)] if part < 3 else self.blocks[1]
        return pltpu.make_async_copy(block, self.full[0].at[rows], sem)

    def begin(self):
        self.z_start(2)
        for index in range(1, 7):
            self.own_copy(index).start()

    def small_start(self):
        self.own_copy(0).start()
        for offset in self.offsets:
            self.start("small", self.small_copy(offset, self.place.t))

    def advance(self, count=1):
        steps = (self.first, self.second, self.third)
        for due, step, kind, offset in self.events[:count]:
            self.clock = max(self.clock, due)
            steps[step](kind, offset)
        self.events = self.events[count:]

    def spend(self, duration):
        self.clock += duration
        while self.events and self.events[0][0] <= self.clock:
            self.advance()

    def advance_kind(self, kind, offset=None):
        while any(event[2] == kind and offset in (None, event[3]) for event in self.events):
            self.advance()
        for which in self.offsets if offset is None else (offset,):
            self.last(kind, which)

    def small_ready(self):
        self.own_copy(0).wait()
        for offset in self.offsets:
            self.small_copy(offset, self.place.from_z(offset)).wait_recv()

    def first(self, kind, offset):
        place = self.place
        self.z_copy(kind, offset, place.from_z(offset), self.blocks[1].at[0:SLICE]).wait_recv()
        self.start(kind, self.plane_copy(0, kind, offset, place.d, place.to_x))
        self.start(kind, self.plane_copy(1, kind, offset, place.d, place.to_y))
        self.start(kind, self.core_copy(0, kind, offset, place.d))
        self.z_start(1)

    def second(self, kind, offset):
        place = self.place
        self.plane_copy(0, kind, offset, place.d_x, place.to_x).wait_recv()
        self.start(kind, self.plane_copy(2, kind, offset, place.d_x, place.to_y, HALF, HALF))
        self.start(kind, self.core_copy(1, kind, offset, place.d_x))
        self.plane_copy(1, kind, offset, place.d_y, place.to_y).wait_recv()
        self.start(kind, self.plane_copy(3, kind, offset, place.d_y, place.to_x, 0, HALF))
        self.start(kind, self.core_copy(2, kind, offset, place.d_y))

    def third(self, kind, offset):
        place = self.place
        self.plane_copy(2, kind, offset, place.d_xy, place.to_y, HALF, HALF).wait_recv()
        self.plane_copy(3, kind, offset, place.d_xy, place.to_x, 0, HALF).wait_recv()
        self.start(kind, self.core_copy(3, kind, offset, place.d_xy))

    def last(self, kind, offset):
        place = self.place
        for step, d in enumerate((place.d, place.d_x, place.d_y, place.d_xy)):
            self.core_copy(step, kind, offset, place.core_of(d)).wait_recv()

    def own_ready(self, kind):
        for index in range(3, 7) if kind == 0 else (kind,):
            self.own_copy(index).wait()


DOWN, UP, FIRST = 0, 1, 2
STRAIGHT = (UP, FIRST)


class Reduce:
    def __init__(self, place, parts, bufs, outs, sems):
        self.place, self.parts, self.outs = place, parts, outs
        (self.core_in, self.one_in, self.near_in, self.far_in, self.two_in, self.z_in) = bufs
        (
            self.core_sem, self.one_sem, self.near_sem, self.far_sem, self.two_sem, self.z_sem,
            self.plane_sem, self.back_sem, self.free_sem,
        ) = sems
        t = place.t
        near, far = t + 1 - 2 * lax.rem(t, 2), t + 2 - 4 * (t // 2)
        self.blocks = (near, far + 1 - 2 * lax.rem(t, 2), far, t)
        self.major = (place.x, place.y)
        self.minor = (place.y, place.x)
        self.to_major = (place.to_x, place.to_y)
        self.to_minor = (place.to_y, place.to_x)
        self.started = {DOWN: [], UP: [], FIRST: [], "out": []}

    def start(self, kind, copy):
        copy.start()
        self.started[kind].append(copy)

    def sent(self, kind):
        for copy in self.started[kind]:
            copy.wait_send()
        self.started[kind] = []
        if kind in STRAIGHT:
            for slot in range(3):
                for half in range(2):
                    self.z_copy(kind, slot, half).wait_send()

    def line(self, t):
        return (self.place.dp, t)

    def block(self, kind, group):
        return group if kind == FIRST else self.blocks[group]

    def cells(self, kind, core, group, half=None, major=None, minor=None):
        row, size = (core * 4 + self.block(kind, group)) * 8, 8
        if half is not None:
            row, size = row + half * 4 + major * 2, 2
        if minor is not None:
            row, size = row + minor, 1
        return self.parts[kind].at[pl.ds(pl.multiple_of(row * HALF, 16), size * HALF)]

    def own(self, kind, group, half, major=None, minor=None):
        major = self.major[half] if major is None else major
        return self.cells(kind, self.place.core, group, half, major, minor)

    def copy(self, sem, index, src, dst, device):
        return send(src, dst, sem.at[(0,) + index], sem.at[(1,) + index], device)

    def core_copy(self, kind, group):
        src = self.cells(kind, 1 - self.place.core, group)
        dst = self.core_in.at[1 if kind == UP else 0, group]
        return self.copy(self.core_sem, (kind, group), src, dst, self.place.to_core)

    def one_copy(self, kind, group, half):
        src = self.own(kind, group, half, 1 - self.major[half])
        dst = self.one_in.at[kind, group, half]
        return self.copy(self.one_sem, (kind, group, half), src, dst, self.to_major[half])

    def near_copy(self, kind, group, half):
        src, dst = self.own(kind, group, half), self.near_in.at[kind, group, half]
        return self.copy(self.near_sem, (kind, group, half), src, dst, self.line(self.blocks[0]))

    def far_copy(self, kind, half):
        src, dst = self.own(kind, 2, half), self.far_in.at[kind, half]
        return self.copy(self.far_sem, (kind, half), src, dst, self.line(self.blocks[2]))

    def two_copy(self, kind, group, half):
        src = self.own(kind, group, half, None, 1 - self.minor[half])
        dst = self.two_in.at[kind, group, half]
        return self.copy(self.two_sem, (kind, group, half), src, dst, self.to_minor[half])

    def z_copy(self, kind, slot, half, group=0):
        src = self.own(kind, group, half, None, self.minor[half])
        dst, device = self.z_in.at[kind, slot, half], self.line(self.block(kind, group))
        return self.copy(self.z_sem, (kind, slot, half), src, dst, device)

    def rows(self, kind, d, begin=0, size=SLICE):
        return self.outs[kind].at[pl.ds(pl.multiple_of(d * SLICE + begin, 16), size)]

    def plane_copy(self, step, kind, d, device, begin=0, size=SLICE):
        rows = self.rows(kind, d, begin, size)
        return self.copy(self.plane_sem, (step, kind), rows, rows, device)

    def back_copy(self, step, kind, d):
        rows = self.rows(kind, d)
        return self.copy(self.back_sem, (step, kind), rows, rows, self.place.to_core)

    def add(self, ref, addend):
        ref[...] = ref[...] + addend

    def cross(self, kind, group):
        if kind == FIRST and group == 0:
            pl.semaphore_wait(self.free_sem, 1)
        self.start(kind, self.core_copy(kind, group))

    def one(self, kind, group):
        self.core_copy(kind, group).wait_recv()
        for half in range(2):
            for major in range(2):
                rows = self.own(kind, group, half, major)
                slot, begin = 1 if kind == UP else 0, (half * 2 + major) * SLICE
                self.add(rows, self.core_in[slot, group, begin : begin + SLICE, :])
        for half in range(2):
            self.start(kind, self.one_copy(kind, group, half))
        if kind == DOWN and group == 3:
            pl.semaphore_signal(
                self.free_sem, inc=1, device_id=self.place.to_core, device_id_type=MESH
            )

    def two(self, kind, group):
        for half in range(2):
            self.one_copy(kind, group, half).wait_recv()
            self.add(self.own(kind, group, half), self.one_in[kind, group, half])
            if kind in STRAIGHT:
                self.start(kind, self.two_copy(kind, group, half))
            elif group < 2:
                self.start(kind, self.near_copy(kind, group, half))

    def three(self, kind, group):
        if kind not in STRAIGHT:
            return
        for half in range(2):
            self.two_copy(kind, group, half).wait_recv()
            rows = self.own(kind, group, half, None, self.minor[half])
            self.add(rows, self.two_in[kind, group, half])
        if kind != FIRST:
            for half in range(2) if group < 3 else ():
                self.z_copy(kind, group, half, group).start()
            return

        @pl.when(self.place.t != group)
        def _():
            slot = lax.rem(group - self.place.t + 4, 4) - 1
            for half in range(2):
                self.z_copy(kind, slot, half, group).start()

    def keep(self, kind, _):
        if kind in STRAIGHT:
            return
        for half in range(2):
            self.near_copy(kind, 1, half).wait_recv()
            self.add(self.own(kind, 2, half), self.near_in[kind, 1, half])
            self.start(kind, self.far_copy(kind, half))

    def mine(self, kind, _):
        if kind in STRAIGHT:
            return
        for half in range(2):
            self.near_copy(kind, 0, half).wait_recv()
            self.far_copy(kind, half).wait_recv()
            rows = self.own(kind, 3, half)
            total = rows[...].astype(F32) + self.near_in[kind, 0, half].astype(F32)
            rows[...] = (total + self.far_in[kind, half].astype(F32)).astype(LOW)
            self.start(kind, self.two_copy(kind, 3, half))

    def final(self, kind, _):
        place = self.place
        for half in range(2):
            mine = place.t if kind == FIRST else 3
            total = self.own(kind, mine, half, None, self.minor[half])[...].astype(F32)
            if kind in STRAIGHT:
                for slot in range(3):
                    self.z_copy(kind, slot, half).wait_recv()
                    total = total + self.z_in[kind, slot, half].astype(F32)
            else:
                self.two_copy(kind, 3, half).wait_recv()
                total = total + self.two_in[kind, 3, half].astype(F32)
            self.rows(kind, place.d, half * HALF, HALF)[...] = total.astype(LOW)
        self.start("out", self.plane_copy(0, kind, place.d, place.to_x))
        self.start("out", self.plane_copy(1, kind, place.d, place.to_y))
        self.start("out", self.back_copy(0, kind, place.d))

    def relay(self, kind, _):
        place = self.place
        self.plane_copy(0, kind, place.d_x, place.to_x).wait_recv()
        self.start("out", self.plane_copy(2, kind, place.d_x, place.to_y, HALF, HALF))
        self.start("out", self.back_copy(1, kind, place.d_x))
        self.plane_copy(1, kind, place.d_y, place.to_y).wait_recv()
        self.start("out", self.plane_copy(3, kind, place.d_y, place.to_x, 0, HALF))
        self.start("out", self.back_copy(2, kind, place.d_y))

    def back(self, kind, _):
        place = self.place
        self.plane_copy(2, kind, place.d_xy, place.to_y, HALF, HALF).wait_recv()
        self.plane_copy(3, kind, place.d_xy, place.to_x, 0, HALF).wait_recv()
        self.start("out", self.back_copy(3, kind, place.d_xy))

    def last(self, kind, _):
        place = self.place
        for step, d in enumerate((place.d, place.d_x, place.d_y, place.d_xy)):
            self.back_copy(step, kind, place.core_of(d)).wait_recv()


class Total:
    def __init__(self, place, stages, arrived, line_up, sems):
        self.place, self.stages, self.arrived, self.line_up = place, stages, arrived, line_up
        self.pair_sem, self.z_sem = sems
        self.started = []

    def pair_copy(self, step):
        device = (self.place.to_core, self.place.to_x, self.place.to_y)[step]
        sem = self.pair_sem
        return send(
            self.stages.at[step], self.arrived.at[step], sem.at[0, step], sem.at[1, step], device
        )

    def z_copy(self, offset, source):
        sem = self.z_sem
        return send(
            self.stages.at[3],
            self.line_up.at[source],
            sem.at[0, offset - 1],
            sem.at[1, offset - 1],
            self.place.to_z(offset),
        )

    def start(self, copy):
        copy.start()
        self.started.append(copy)

    def begin(self):
        self.start(self.pair_copy(0))

    def step(self, index):
        self.pair_copy(index).wait_recv()
        self.stages[index + 1] = self.stages[index] + self.arrived[index]
        if index < 2:
            self.start(self.pair_copy(index + 1))
        else:
            for offset in range(1, self.place.tp_size):
                self.start(self.z_copy(offset, self.place.t))
            self.line_up[self.place.t] = self.stages[3]

    def end(self):
        for offset in range(1, self.place.tp_size):
            self.z_copy(offset, self.place.from_z(offset)).wait_recv()
        total = self.line_up[0]
        for t in range(1, self.place.tp_size):
            total = total + self.line_up[t]
        return total

    def finish(self):
        for copy in self.started:
            copy.wait_send()


def part_row(core, t, half, y, x):
    cell = x * 2 + y if half == 0 else y * 2 + x
    return (((core * 4 + t) * 2 + half) * 4 + cell) * HALF


def store_rows(part, core, t, half, cell, begin, values):
    row = pl.multiple_of(part_row(core, t, half, cell // 2, cell % 2) + begin, 16)
    part[pl.ds(row, 16), :] = values.astype(LOW)


def store_part(part, base, values, t):
    for piece in range(values.shape[0] // 16):
        d, inner = divmod(base + piece * 16, SLICE)
        half, begin = divmod(inner, HALF)
        store_rows(part, d % 2, t, half, d // 2, begin, values[piece * 16 : piece * 16 + 16])


def store_first(part, section, base, values):
    for piece in range(values.shape[0] // 16):
        t, inner = divmod(base + piece * 16, 192)
        core, inner = divmod(inner, SLICE)
        half, begin = divmod(inner, HALF)
        store_rows(part, core, t, half, section, begin, values[piece * 16 : piece * 16 + 16])


def total_of(terms):
    result = None
    for term in terms:
        result = term if result is None else result + term
    return result


def feed_cot(cot, vec, feed_low, sums, page):
    for rows in chunks():
        values = cot[page, rows, :].astype(F32) * line(vec, FEED_SCALE)
        sums[DOWN_BIAS] += fold(values)
        feed_low[page, rows, :] = values.astype(LOW)


def down_grad(feed_low, hidden_low, part, t, column):
    grads = [
        dot(hidden_low[t, page, :, tile(column)], feed_low[page], TN) for page in range(PAGES)
    ]
    store_part(part, column * TILE, total_of(grads), t)


def pre_back(feed_low, full_down, slope, sums, t, column):
    row = pl.multiple_of(t * WIDTH + column * TILE, TILE)
    weight = full_down[pl.ds(row, TILE), :]
    folds = []
    for page in range(PAGES):
        pre_cot = dot(feed_low[page], weight, NT) * slope[t, page, :, tile(column)].astype(F32)
        folds.append(fold(pre_cot))
        slope[t, page, :, tile(column)] = pre_cot.astype(LOW)
    sums[UP_BIAS + t, :, tile(column)] = total_of(folds)


def up_back(second_t, pre_cot, part, t, column):
    grads = [dot(second_t[page, tile(column), :], pre_cot[t, page], NN) for page in range(PAGES)]
    store_part(part, column * TILE, total_of(grads), t)


def second_cot(pre_cot, full_up, result, t, column, fresh):
    row = pl.multiple_of(t * WIDTH + column * TILE, TILE)
    weight = full_up[pl.ds(row, TILE), :]
    for page in range(PAGES):
        term = dot(pre_cot[t, page], weight, NT)
        if fresh:
            result[page, :, tile(column)] = term
        else:
            result[page, :, tile(column)] += term


def norm_back(features, cot, gain, sums, gain_row, shift_row):
    norm, scale = norm_parts(features)
    sums[gain_row] += fold(cot * norm)
    sums[shift_row] += fold(cot)
    cot = cot * gain
    mean = jnp.mean(cot, axis=-1, keepdims=True)
    along = jnp.mean(cot * norm, axis=-1, keepdims=True)
    return scale * (cot - mean - norm * along)


def second_back(middle, result, cot, branch, vec, sums, branch_low, page):
    for rows in chunks():
        part = norm_back(
            middle[page, rows, :], result[page, rows, :], line(vec, GAIN_2), sums, GAIN_2, SHIFT_2
        )
        middle_cot = cot[page, rows, :].astype(F32) + part
        middle[page, rows, :] = middle_cot
        sums[ATT_SCALE] += fold(middle_cot * branch[page, rows, :])
        branch_cot = middle_cot * line(vec, ATT_SCALE)
        sums[OUT_BIAS] += fold(branch_cot)
        branch_low[page, rows, :] = branch_cot.astype(LOW)


def attended_back(branch_low, full_a, attended_cot, page):
    for column in range(3):
        rows = slice(3 * WIDTH + column * TILE, 3 * WIDTH + column * TILE + TILE)
        result = dot(branch_low[page], full_a[rows, :], NT)
        attended_cot[page, :, tile(column)] = result.astype(LOW)


def attend_back(heads, expo, scale, attended_cot, scores, page, pair):
    lanes = slice(pair * 128, pair * 128 + 128)
    query, key, value = (heads[part, page, :, lanes] for part in range(3))
    cot = attended_cot[page, :, lanes]
    lane = lax.broadcasted_iota(jnp.int32, (SEQ, 128), 1)
    zero = jnp.zeros_like(query)
    key_t = key.T
    query_cots, key_cots, value_cots = [], [], []
    for which in range(2):
        head = 2 * pair + which
        keep = lane < 64 if which == 0 else lane >= 64
        head_query, head_cot = jnp.where(keep, query, zero), jnp.where(keep, cot, zero)
        prob_cot = dot(value, head_cot, NT)
        columns = slice((head % 3) * TILE, (head % 3) * TILE + SEQ)
        probs = expo[head // 3, page, :, columns].astype(F32) * scale[page, head : head + 1, :]
        product = probs * prob_cot
        score_cot = product - probs * jnp.sum(product, axis=0, keepdims=True)
        for half, width in ((0, 128), (1, SEQ - 128)):
            rows = slice((half * HEADS + head) * SEQ, (half * HEADS + head + 1) * SEQ)
            scores[rows, 0:width] += score_cot[:, half * 128 : half * 128 + width]
        score_cot = score_cot.astype(LOW)
        value_cots.append(dot(probs.astype(LOW), head_cot, NN))
        key_cots.append(dot(score_cot, head_query, NN))
        query_cots.append(dot(key_t[64 * which : 64 * which + 64], score_cot, NN))
    heads[0, page, :, lanes] = (jnp.concatenate(query_cots, axis=0).T * 0.125).astype(LOW)
    heads[1, page, :, lanes] = total_of(key_cots).astype(LOW)
    heads[2, page, :, lanes] = total_of(value_cots).astype(LOW)


def section_back(heads, right, part, sums, section, half):
    columns = slice(half * 384, half * 384 + 384)
    pieces = [heads[section, page, :, columns] for page in range(PAGES)]
    grads = [dot(pieces[page], right[page], TN) for page in range(PAGES)]
    if section in (0, 2):
        index = Q_BIAS if section == 0 else V_BIAS
        sums[index, :, columns] = total_of([fold(piece.astype(F32)) for piece in pieces])
    store_first(part, section, half * 384, total_of(grads))


def first_cot(heads, full_a, result, page):
    for column in range(3):
        terms = [
            dot(heads[part, page], full_a[part * WIDTH : (part + 1) * WIDTH, tile(column)], NN)
            for part in range(3)
        ]
        result[page, :, tile(column)] = total_of(terms)


def first_back(patches, hide, vec, result, middle, sums, page):
    for rows in chunks():
        features = enter(patches, hide, vec, page, rows)
        part = norm_back(
            features, result[page, rows, :], line(vec, GAIN_1), sums, GAIN_1, SHIFT_1
        )
        entered_cot = middle[page, rows, :] + part
        hidden = hide[rows, page : page + 1] > 0
        result[page, rows, :] = jnp.where(hidden, 0.0, entered_cot)
        sums[EMBED] += fold(jnp.where(hidden, entered_cot, 0.0))


def table_back(scores, index_t, packed, begin, end):
    row = lax.broadcasted_iota(jnp.int32, (128, TILE), 0)
    unroll = 20

    def step(index, total):
        lefts, rights = [], []
        for inner in range(unroll):
            key = index * unroll + inner
            halves = [
                scores[pl.ds(half * HEADS * SEQ + key, HEADS, stride=SEQ), :] for half in range(2)
            ]
            terms = jnp.concatenate(halves, axis=1)
            terms = jnp.concatenate([terms, jnp.zeros((4, TILE), F32)], axis=0)
            entry = index_t[pl.ds(key, 1), :]
            low_part, high_part = entry & 127, entry >> 7
            match = jnp.broadcast_to(low_part, (128, TILE)) == row
            rights.append(jnp.where(match, 1.0, 0.0).astype(LOW))
            picked = [jnp.where(high_part == part, terms, 0.0).astype(LOW) for part in range(6)]
            lefts.append(jnp.concatenate(picked, axis=0))
        return total + dot(jnp.concatenate(lefts, axis=1), jnp.concatenate(rights, axis=1), NT)

    total = lax.fori_loop(begin // unroll, end // unroll, step, jnp.zeros((96, 128), F32))
    for part in range(6):
        columns, rows = slice(part * 128, part * 128 + 128), slice(part * 16, part * 16 + 16)
        if begin:
            packed[16:32, columns] += total[rows]
        else:
            packed[16:32, columns] = total[rows]


def layer_kernel(tp_size, *refs):
    blocks = refs[:4]
    patches, cot, mask, index, table, bias_up, bias_qv = refs[4:11]
    vec_in = refs[11:20]
    sums_out, total_out = refs[20:23], refs[23]
    output, patch_out, expo_out, heads_out, hidden_out = refs[24:29]
    outs, refs = refs[29:32], refs[32:]
    full, small_all, small = refs[0:3], refs[3], refs[4]
    wide, inner, parts = refs[5:8]
    bufs = refs[8:14]
    scores_t, branch, middle, result, second_t, first_low, second_low, feed_low = refs[14:22]
    sums, stages, arrived, line_up = refs[22:26]
    vec, hide, index_t, scale, bias_rows, up_bias = refs[26:32]
    local_sem = refs[32]
    gather_sems, reduce_sems, total_sems = refs[33:38], refs[38:47], refs[47:49]
    place = Place(tp_size)
    gather = Gather(place, blocks, small, full, small_all, gather_sems)
    reduce = Reduce(place, (parts.at[0], parts.at[1], full[1]), bufs, outs, reduce_sems)
    total = Total(place, stages, arrived, line_up, total_sems)
    pair_bias = scores = scores_t

    def local(index, src, dst):
        return pltpu.make_async_copy(src, dst, local_sem.at[index])

    greet(place)
    small[0:3, 0:NUM_REL] = table[...].astype(F32)
    small[3:4, :] = bias_up[...].astype(F32).reshape(1, WIDTH)
    small[4:6, 0:192] = bias_qv[...].astype(F32)
    for row, values in enumerate(vec_in):
        vec[row : row + 1, :] = values[...].reshape(1, WIDTH)
    meet(place)
    gather.begin()
    gather.small_start()
    place_in_page = lax.broadcasted_iota(jnp.int32, (PAGES, SEQ), 1)
    patch = (place_in_page >= 1) & (place_in_page <= PATCHES)
    pages = [mask[pl.ds(SEQ * page, SEQ)].reshape(1, SEQ) for page in range(PAGES)]
    hidden = jnp.where((jnp.concatenate(pages, axis=0) > 0) & patch, 1.0, 0.0)
    hide[...] = jnp.concatenate([hidden, jnp.zeros((8 - PAGES, SEQ), F32)], axis=0).T
    index_t[...] = jnp.zeros_like(index_t)
    index_t[:, 0:SEQ] = index[...].astype(F32).T.astype(jnp.int32)
    sums[...] = jnp.zeros_like(sums)
    for page in range(PAGES):
        first_norm(patches, hide, vec, first_low, page)
    gather.small_ready()
    for t in range(tp_size):
        columns = slice(192 * t, 192 * t + 192)
        up_bias[t : t + 1, :] = small_all[t, 3:4, :]
        bias_rows[0:1, columns] = small_all[t, 4:5, 0:192]
        bias_rows[1:2, columns] = small_all[t, 5:6, 0:192]
    gather.spend(4.0)
    for head in range(HEADS):
        lookup(small_all, index_t, pair_bias, head)
        gather.spend(0.7)
    gather.advance_kind(0)
    gather.own_ready(0)
    for part in range(3):
        for column in range(3):
            project(first_low, full[0], bias_rows, inner, part, column)
            gather.spend(0.4)
    saves = []
    for page in range(PAGES):
        for pair in range(HEADS // 2):
            attend(inner, pair_bias, wide, scale, page, pair)
            if pair % 3 == 2:
                gather.spend(1.4)
        for index, (src, dst) in enumerate(((wide, expo_out), (inner, heads_out))):
            saves.append(local(10 + 2 * page + index, src.at[:, page], dst.at[:, page]))
            saves[-1].start()
    for page in range(PAGES):
        out_project(inner, full[0], vec, patches, hide, branch, middle, page)
        second_norm(middle, vec, second_low, page)
        gather.spend(0.9)
        second_t[page] = second_low[page].T
        feed_cot(cot, vec, feed_low, sums, page)
        gather.spend(0.4)
    for copy in saves:
        copy.wait()
    gather.advance_kind(1)
    gather.own_ready(1)
    for t in range(tp_size):
        for column in range(3):
            feed_up(second_low, full[1], up_bias, wide, inner, t, column)
            gather.spend(0.4)
    hidden_copy = local(2, wide, hidden_out)
    hidden_copy.start()
    for group in range(4):
        for column in range(3):
            down_grad(feed_low, wide, parts.at[DOWN], reduce.blocks[group], column)
            gather.spend(0.35)
        reduce.cross(DOWN, group)
    hidden_copy.wait()
    expo_load = local(3, expo_out, wide)
    expo_load.start()

    def run(*events):
        for step, kind, group in events:
            step(kind, group)

    cross, one, two, three = reduce.cross, reduce.one, reduce.two, reduce.three
    keep, mine, final = reduce.keep, reduce.mine, reduce.final
    relay, back, last = reduce.relay, reduce.back, reduce.last

    def block_back(offset):
        t = place.from_z(offset)
        for column in range(3):
            pre_back(feed_low, full[2], inner, sums, t, column)
        gather.spend(1.2)
        for column in range(3):
            up_back(second_t, inner, parts.at[UP], t, column)
        gather.spend(1.2)
        for column in range(3):
            second_cot(inner, full[1], result, t, column, offset == 0)
        gather.spend(1.2)

    scores[...] = jnp.zeros_like(scores)
    gather.own_ready(2)
    block_back(0)
    run((one, DOWN, 0), (one, DOWN, 1), (one, DOWN, 2), (one, DOWN, 3))
    run((cross, UP, 3),)
    gather.advance_kind(2, 1)
    block_back(1)
    gather.advance_kind(2, 3)
    block_back(3)
    run((cross, UP, 0), (cross, UP, 1))
    gather.advance(len(gather.events))
    gather.advance_kind(2, 2)
    block_back(2)
    run((cross, UP, 2), (one, UP, 0), (one, UP, 1))
    heads_loads = [
        local((0, 1, 4)[page], heads_out.at[:, page], inner.at[:, page]) for page in range(PAGES)
    ]
    for copy in heads_loads:
        copy.start()
    branch_low, attended_cot = feed_low, second_low
    for page in range(PAGES):
        second_back(middle, result, cot, branch, vec, sums, branch_low, page)
    run((one, UP, 2), (one, UP, 3))
    for page in range(PAGES):
        attended_back(branch_low, full[0], attended_cot, page)
    gather.sent(1)
    expo_load.wait()
    after_attend = (
        (),
        ((two, DOWN, 0),),
        ((two, DOWN, 1),),
        ((one, FIRST, 0), (two, DOWN, 2)),
        ((one, FIRST, 1), (two, DOWN, 3)),
        (),
    )
    for half in range(2):
        for page in range(PAGES):
            if half == 0:
                heads_loads[page].wait()
            for pair in range(3 * half, 3 * half + 3):
                attend_back(inner, wide, scale, attended_cot, scores, page, pair)
            run(*after_attend[3 * half + page])
        for section in (3, 0, 1, 2):
            right = branch_low if section == 3 else first_low
            section_back(inner, right, full[1], sums, section, half)
        run((cross, FIRST, 2 * half), (cross, FIRST, 2 * half + 1))
    hidden_load = local(2, hidden_out, wide)
    hidden_load.start()
    after_cot = (
        ((one, FIRST, 2), (two, UP, 0)),
        ((one, FIRST, 3), (two, UP, 1)),
        ((keep, DOWN, 0),),
    )
    for page in range(PAGES):
        first_cot(inner, full[0], result, page)
        run(*after_cot[page])
    after_first = (((three, UP, 0),), ((two, UP, 2), (three, UP, 1)), ((two, UP, 3),))
    for page in range(PAGES):
        first_back(patches, hide, vec, result, middle, sums, page)
        run(*after_first[page])
    patch_copy = local(5, result, patch_out)
    patch_copy.start()
    hidden_load.wait()
    after_feed = (((three, UP, 2),), ((three, UP, 3),), ((two, FIRST, 0),))
    for page in range(PAGES):
        feed_down(wide, full[2], vec, patches, hide, cot, branch, sums, tp_size, page)
        run(*after_feed[page])
    output_copy = local(9, branch, output)
    output_copy.start()
    table_back(scores, index_t, stages.at[0], 0, 100)
    run((mine, DOWN, 0), (two, FIRST, 1), (three, FIRST, 0))
    table_back(scores, index_t, stages.at[0], 100, 200)
    stages[0, 0:16, :] = jnp.sum(sums[...], axis=1)
    total.begin()
    run((two, FIRST, 2), (three, FIRST, 1), (final, DOWN, 0))
    total.step(0)
    run((two, FIRST, 3), (three, FIRST, 2), (relay, DOWN, 0), (final, UP, 0))
    total.step(1)
    run((three, FIRST, 3), (back, DOWN, 0), (relay, UP, 0))
    total.step(2)
    run((final, FIRST, 0), (back, UP, 0), (last, DOWN, 0))
    total_out[...] = total.end()
    run((relay, FIRST, 0), (last, UP, 0), (back, FIRST, 0), (last, FIRST, 0))
    sum_copies = [local(6 + kind, outs[kind], sums_out[kind]) for kind in range(3)]
    for copy in sum_copies:
        copy.start()
    patch_copy.wait()
    output_copy.wait()
    for kind in (DOWN, UP, FIRST, "out"):
        reduce.sent(kind)
    for kind in (0, 2, "small"):
        gather.sent(kind)
    total.finish()
    for copy in sum_copies:
        copy.wait()


ANY = pl.BlockSpec(memory_space=pl.ANY)
VMEM = pl.BlockSpec(memory_space=pltpu.VMEM)


def layer(blocks, local_args, vec_rows, tp_size):
    dma, regular = pltpu.SemaphoreType.DMA, pltpu.SemaphoreType.REGULAR
    shape, scratch = jax.ShapeDtypeStruct, pltpu.VMEM
    page_shape = (PAGES, SEQ, WIDTH)
    quarter = (SLICE, WIDTH)
    return pl.pallas_call(
        functools.partial(layer_kernel, tp_size),
        out_shape=[shape((WIDTH, WIDTH), LOW)] * 3
        + [
            shape((32, WIDTH), F32),
            shape(page_shape, F32),
            shape(page_shape, F32),
        ]
        + [shape((4,) + page_shape, LOW)] * 3,
        in_specs=[ANY] * 4 + [VMEM] * 16,
        out_specs=[ANY] * 3 + [VMEM] + [ANY] * 5,
        scratch_shapes=[scratch((WIDTH, WIDTH), LOW)] * 3
        + [scratch((tp_size * WIDTH, WIDTH), LOW)] * 3
        + [
            scratch((tp_size, 8, WIDTH), F32),
            scratch((8, WIDTH), F32),
            scratch((4,) + page_shape, LOW),
            scratch((4,) + page_shape, LOW),
            scratch((2, 32 * SLICE, WIDTH), LOW),
            scratch((2, 4, 4 * SLICE, WIDTH), LOW),
            scratch((3, 4, 2) + quarter, LOW),
            scratch((2, 2, 2) + quarter, LOW),
            scratch((2, 2) + quarter, LOW),
            scratch((3, 4, 2, HALF, WIDTH), LOW),
            scratch((3, 3, 2, HALF, WIDTH), LOW),
            scratch((2 * HEADS * SEQ, 128), F32),
            scratch(page_shape, F32),
            scratch(page_shape, F32),
            scratch(page_shape, F32),
            scratch((PAGES, WIDTH, SEQ), LOW),
            scratch(page_shape, LOW),
            scratch(page_shape, LOW),
            scratch(page_shape, LOW),
            scratch((16, 8, WIDTH), F32),
            scratch((4, 32, WIDTH), F32),
            scratch((3, 32, WIDTH), F32),
            scratch((tp_size, 32, WIDTH), F32),
            scratch((16, WIDTH), F32),
            scratch((SEQ, 8), F32),
            scratch((SEQ, TILE), jnp.int32),
            scratch((PAGES, 16, SEQ), F32),
            scratch((8, WIDTH), F32),
            scratch((8, WIDTH), F32),
            dma((16,)),
            dma((7,)),
            dma((2, 3, tp_size - 1)),
            dma((2, tp_size - 1)),
            dma((2, 4, 3, tp_size - 1)),
            dma((2, 4, 3, tp_size - 1)),
            dma((2, 3, 4)),
            dma((2, 3, 4, 2)),
            dma((2, 2, 2, 2)),
            dma((2, 2, 2)),
            dma((2, 3, 4, 2)),
            dma((2, 3, 3, 2)),
            dma((2, 4, 3)),
            dma((2, 4, 3)),
            regular,
            dma((2, 3)),
            dma((2, tp_size - 1)),
        ],
        compiler_params=pltpu.CompilerParams(
            collective_id=0, has_side_effects=True, vmem_limit_bytes=64 * 1024 * 1024 - 65536
        ),
    )(*blocks, *local_args, *vec_rows)


def finish_kernel(tp_size, *refs):
    sums, totals, output, patch = refs[:3], *refs[3:6]
    project_out, output_out, up_out, down_out, layer_out, patch_out = refs[6:12]
    rows_out, bias_out, table_out, bias_up = refs[12:21], *refs[21:24]
    low, wide, total, pages, sem = refs[24:29]
    loads = [pltpu.make_async_copy(totals, total, sem.at[0])]
    for kind in range(3):
        loads.append(pltpu.make_async_copy(sums[kind], low.at[kind], sem.at[1 + kind]))
    loads.append(pltpu.make_async_copy(output, pages.at[0], sem.at[4]))
    loads.append(pltpu.make_async_copy(patch, pages.at[1], sem.at[5]))
    for copy in loads:
        copy.start()
    copies = []
    for kind, target in enumerate((down_out, up_out, None)):
        loads[1 + kind].wait()
        for part in range(4):
            rows = slice(part * 192, part * 192 + 192)
            wide[kind, rows, :] = low[kind, rows, :].astype(F32)
            if kind < FIRST:
                dst = target.at[rows]
            else:
                dst = project_out.at[rows] if part < 3 else output_out
            copies.append(
                pltpu.make_async_copy(wide.at[kind, rows], dst, sem.at[6 + len(copies)])
            )
            copies[-1].start()
    for index, target in enumerate((layer_out, patch_out)):
        loads[4 + index].wait()
        copies.append(
            pltpu.make_async_copy(pages.at[index], target, sem.at[6 + len(copies)])
        )
        copies[-1].start()
    loads[0].wait()
    for row, target in enumerate(rows_out):
        target[...] = total[row : row + 1, :].reshape(WIDTH)
    for t in range(tp_size):

        @pl.when(lax.axis_index("tp") == t)
        def _():
            bias_out[...] = total[Q_BIAS : Q_BIAS + 2, 192 * t : 192 * t + 192]
            table_out[...] = total[16 + 3 * t : 19 + 3 * t, 0:NUM_REL]
            bias_up[...] = total[UP_BIAS + t : UP_BIAS + t + 1, :].reshape(WIDTH)

    for copy in copies:
        copy.wait()


def finish(values, tp_size):
    shape = jax.ShapeDtypeStruct
    page_shape = (PAGES, SEQ, WIDTH)
    return pl.pallas_call(
        functools.partial(finish_kernel, tp_size),
        out_shape=[
            shape((3 * 192, WIDTH), F32),
            shape((192, WIDTH), F32),
            shape((WIDTH, WIDTH), F32),
            shape((WIDTH, WIDTH), F32),
            shape(page_shape, F32),
            shape(page_shape, F32),
        ]
        + [shape((WIDTH,), F32)] * 9
        + [shape((2, 192), F32), shape((3, NUM_REL), F32), shape((WIDTH,), F32)],
        in_specs=[ANY] * 6,
        out_specs=[ANY] * 6 + [VMEM] * 12,
        scratch_shapes=[
            pltpu.VMEM((3, WIDTH, WIDTH), values[0].dtype),
            pltpu.VMEM((3, WIDTH, WIDTH), F32),
            pltpu.VMEM((32, WIDTH), F32),
            pltpu.VMEM((2,) + page_shape, F32),
            pltpu.SemaphoreType.DMA((20,)),
        ],
        compiler_params=pltpu.CompilerParams(vmem_limit_bytes=63 << 20),
    )(*values)


def body(tp_size, dp_size, *args):
    (
        patches, page_mask, pair_index, mask_embed, first_gain, first_shift, project_weight,
        project_bias, pair_table, output_weight, output_bias, attention_scale, second_gain,
        second_shift, up_weight, up_bias, down_weight, down_bias, feed_scale, cotangent,
    ) = args
    row_count = patches.shape[0]
    project_rows = jnp.transpose(project_weight, (1, 2, 0)).reshape(3 * 192, WIDTH)
    vec_rows = (
        mask_embed, first_gain, first_shift, output_bias, attention_scale, second_gain,
        second_shift, down_bias, feed_scale,
    )
    local_args = (
        patches.reshape(PAGES, SEQ, WIDTH),
        cotangent.reshape(PAGES, SEQ, WIDTH),
        page_mask,
        pair_index,
        jnp.transpose(pair_table),
        up_bias,
        project_bias,
    )
    values = layer(
        (project_rows, output_weight, up_weight, down_weight),
        local_args,
        vec_rows,
        tp_size,
    )[:6]
    if dp_size > GROUP:
        groups = [[i + GROUP * j for j in range(dp_size // GROUP)] for i in range(GROUP)]
        sums = [value.astype(F32) for value in values[:4]]
        values = list(lax.psum(sums, "dp", axis_index_groups=groups)) + list(values[4:])
    results = finish(values, tp_size)
    project_sum, output_sum, up_sum, down_sum, layer_output, patch_gradient = results[:6]
    rows = results[6:15]
    bias_sum, table_sum, up_bias_sum = results[15:]
    return (
        layer_output.reshape(row_count, WIDTH),
        patch_gradient.reshape(row_count, WIDTH),
        rows[EMBED],
        rows[GAIN_1],
        rows[SHIFT_1],
        jnp.transpose(project_sum.reshape(3, 192, WIDTH), (2, 0, 1)),
        bias_sum,
        jnp.transpose(table_sum),
        output_sum,
        rows[OUT_BIAS],
        rows[ATT_SCALE],
        rows[GAIN_2],
        rows[SHIFT_2],
        up_sum,
        up_bias_sum,
        down_sum,
        rows[DOWN_BIAS],
        rows[FEED_SCALE],
    )


def solution(mesh):
    rows, heads = P(("dp", "tp"), None), P(None, "tp")
    in_specs = (
        rows, P(("dp", "tp")), P(), P(), P(), P(), P(None, None, "tp"), heads, heads,
        P("tp", None), P(), P(), P(), P(), heads, P("tp"), P("tp", None), P(), P(), rows,
    )
    out_specs = (
        rows, rows, P(), P(), P(), P(None, None, "tp"), heads, heads, P("tp", None), P(), P(),
        P(), P(), heads, P("tp"), P("tp", None), P(), P(),
    )
    step = functools.partial(body, mesh.shape["tp"], mesh.shape["dp"])
    return jax.shard_map(step, mesh=mesh, in_specs=in_specs, out_specs=out_specs, check_vma=False)
```

```python
import functools

import jax
import jax.numpy as jnp
from jax import lax
from jax.experimental import pallas as pl
from jax.experimental.pallas import tpu as pltpu
from jax.sharding import PartitionSpec as P

SEQ = 200
PATCHES = 196
NUM_REL = 732
PAGES = 3
HEADS = 12
WIDTH = 768
GROUP = 8
SLICE = 96
HALF = 48
MESH = pl.DeviceIdType.MESH


class Place:
    def __init__(self, tp_size):
        self.tp_size = tp_size
        self.dp = lax.axis_index("dp")
        self.t = lax.axis_index("tp")
        self.d = lax.rem(self.dp, GROUP)
        self.core = lax.rem(self.d, 2)
        self.x = lax.rem(self.d // 2, 2)
        self.y = self.d // 4
        self.to_core = (self.dp + 1 - 2 * self.core, self.t)
        self.to_x = (self.dp + 2 - 4 * self.x, self.t)
        self.to_y = (self.dp + 4 - 8 * self.y, self.t)
        self.d_x = self.d + 2 - 4 * self.x
        self.d_y = self.d + 4 - 8 * self.y
        self.d_xy = self.d_x + 4 - 8 * self.y

    def core_of(self, d):
        return d + 1 - 2 * self.core

    def to_z(self, offset):
        return (self.dp, lax.rem(self.t + offset, self.tp_size))

    def from_z(self, offset):
        return lax.rem(self.t + self.tp_size - offset, self.tp_size)


def partners(place):
    others = [place.to_core, place.to_x, place.to_y]
    return others + [place.to_z(offset) for offset in range(1, place.tp_size)]


def greet(place):
    barrier = pltpu.get_barrier_semaphore()
    for other in partners(place):
        pl.semaphore_signal(barrier, inc=1, device_id=other, device_id_type=MESH)


def meet(place):
    pl.semaphore_wait(pltpu.get_barrier_semaphore(), len(partners(place)))


def send(src, dst, send_sem, recv_sem, device):
    return pltpu.make_async_remote_copy(
        src_ref=src,
        dst_ref=dst,
        send_sem=send_sem,
        recv_sem=recv_sem,
        device_id=device,
        device_id_type=MESH,
    )


def slice_row(kind, t, d):
    if kind == 0:
        row = (d // 2) * 768 + t * 192 + lax.rem(d, 2) * SLICE
    else:
        row = t * 768 + d * SLICE
    return pl.multiple_of(row, 16)


LOW = jnp.bfloat16
F32 = jnp.float32
CHUNKS = ((0, 48), (48, 48), (96, 48), (144, 56))
TILE = 256
NT = (((1,), (1,)), ((), ()))
NN = (((1,), (0,)), ((), ()))
TN = (((0,), (0,)), ((), ()))
EMBED, GAIN_1, SHIFT_1, OUT_BIAS, ATT_SCALE, GAIN_2, SHIFT_2, DOWN_BIAS, FEED_SCALE = range(9)
Q_BIAS, V_BIAS, UP_BIAS = 9, 10, 12


def dot(left, right, dims):
    return lax.dot_general(left, right, dims, preferred_element_type=F32)


def line(ref, index):
    return ref[index : index + 1, :]


def tile(index):
    return slice(index * TILE, index * TILE + TILE)


def fold(values):
    return jnp.sum(values.reshape(values.shape[0] // 8, 8, values.shape[1]), axis=0)


def norm_parts(features):
    center = features - jnp.mean(features, axis=-1, keepdims=True)
    scale = lax.rsqrt(jnp.mean(center * center, axis=-1, keepdims=True) + 1e-6)
    return center * scale, scale


def enter(patches, hide, vec, page, rows):
    features = patches[page, rows, :].astype(F32)
    return jnp.where(hide[rows, page : page + 1] > 0, line(vec, EMBED), features)


def chunks():
    return [slice(start, start + size) for start, size in CHUNKS]


def first_norm(patches, hide, vec, first_low, page):
    for rows in chunks():
        norm, _ = norm_parts(enter(patches, hide, vec, page, rows))
        first_low[page, rows, :] = (norm * line(vec, GAIN_1) + line(vec, SHIFT_1)).astype(LOW)


def lookup(small_all, index_t, pair_bias, head):
    block, place = head // 3, head % 3
    table = small_all[block, place : place + 1, :]
    for half in range(2):
        index = index_t[:, 128 * half : 128 * half + 128]
        low_part, high_part = index & 127, index >> 7
        found = None
        for part in range(6):
            entries = jnp.broadcast_to(table[:, 128 * part : 128 * part + 128], (SEQ, 128))
            got = jnp.take_along_axis(entries, low_part, axis=1)
            found = got if found is None else jnp.where(high_part == part, got, found)
        key = lax.broadcasted_iota(jnp.int32, (SEQ, 128), 0)
        rows = slice((half * HEADS + head) * SEQ, (half * HEADS + head + 1) * SEQ)
        pair_bias[rows, :] = jnp.where(key > PATCHES, -1e30, found)


def project(first_low, full_a, bias_rows, heads, part, column):
    weight = full_a[part * WIDTH + column * TILE : part * WIDTH + column * TILE + TILE, :]
    for page in range(PAGES):
        result = dot(first_low[page], weight, NT)
        if part == 0:
            result = (result + bias_rows[0:1, tile(column)]) * 0.125
        elif part == 2:
            result = result + bias_rows[1:2, tile(column)]
        heads[part, page, :, tile(column)] = result.astype(LOW)


def attend(heads, pair_bias, expo, scale, page, pair):
    lanes = slice(pair * 128, pair * 128 + 128)
    query, key, value = (heads[part, page, :, lanes] for part in range(3))
    lane = lax.broadcasted_iota(jnp.int32, (SEQ, 128), 1)
    value_t = value.T
    outs = []
    for which in range(2):
        head = 2 * pair + which
        keep = lane < 64 if which == 0 else lane >= 64
        scores = dot(key, jnp.where(keep, query, jnp.zeros_like(query)), NT)
        left = pair_bias[head * SEQ : (head + 1) * SEQ, :]
        right = pair_bias[(HEADS + head) * SEQ : (HEADS + head + 1) * SEQ, :]
        scores = scores + jnp.concatenate([left, right], axis=1)[:, 0:SEQ]
        raised = jnp.exp(scores - jnp.max(scores, axis=0, keepdims=True))
        inverse = 1.0 / jnp.sum(raised, axis=0, keepdims=True)
        raised = raised.astype(LOW)
        expo[head // 3, page, :, (head % 3) * TILE : (head % 3) * TILE + SEQ] = raised
        scale[page, head : head + 1, :] = inverse
        outs.append(dot(value_t[64 * which : 64 * which + 64], raised, NN) * inverse)
    heads[3, page, :, lanes] = jnp.concatenate(outs, axis=0).T.astype(LOW)


def out_project(heads, full_a, vec, patches, hide, branch, middle, page):
    for column in range(3):
        weight = full_a[3 * WIDTH : 4 * WIDTH, tile(column)]
        branch[page, :, tile(column)] = dot(heads[3, page], weight, NN) + vec[3:4, tile(column)]
    for rows in chunks():
        entered = enter(patches, hide, vec, page, rows)
        middle[page, rows, :] = entered + line(vec, ATT_SCALE) * branch[page, rows, :]


def second_norm(middle, vec, second_low, page):
    for rows in chunks():
        norm, _ = norm_parts(middle[page, rows, :])
        second_low[page, rows, :] = (norm * line(vec, GAIN_2) + line(vec, SHIFT_2)).astype(LOW)


def feed_up(second_low, full_up, up_bias, hidden_low, slope, t, column):
    weight = full_up[t * WIDTH : (t + 1) * WIDTH, tile(column)]
    bias = up_bias[t : t + 1, tile(column)]
    for page in range(PAGES):
        pre = dot(second_low[page], weight, NN) + bias
        portion = 0.5 * (1.0 + lax.erf(pre * 0.7071067811865476))
        hidden_low[t, page, :, tile(column)] = (pre * portion).astype(LOW)
        bell = jnp.exp(-0.5 * pre * pre) * 0.3989422804014327
        slope[t, page, :, tile(column)] = (portion + pre * bell).astype(LOW)


def feed_down(hidden_low, full_down, vec, patches, hide, cot, branch, sums, tp_size, page):
    for column in range(3):
        columns = tile(column)
        total = None
        for t in range(tp_size):
            weight = full_down[t * WIDTH : (t + 1) * WIDTH, columns]
            term = dot(hidden_low[t, page], weight, NN)
            total = term if total is None else total + term
        total = total + vec[DOWN_BIAS : DOWN_BIAS + 1, columns]
        entered = patches[page, :, columns].astype(F32)
        entered = jnp.where(hide[:, page : page + 1] > 0, vec[EMBED : EMBED + 1, columns], entered)
        middle = entered + vec[ATT_SCALE : ATT_SCALE + 1, columns] * branch[page, :, columns]
        branch[page, :, columns] = middle + vec[FEED_SCALE : FEED_SCALE + 1, columns] * total
        sums[FEED_SCALE, :, columns] += fold(cot[page, :, columns].astype(F32) * total)


FIRST_DUE, TICK = 5.0, 5.0


class Gather:
    def __init__(self, place, blocks, small, full, small_all, sems):
        self.place, self.blocks, self.small = place, blocks, small
        self.full, self.small_all = full, small_all
        self.own_sem, self.z_sem, self.small_sem, self.plane_sem, self.core_sem = sems
        self.offsets = range(1, place.tp_size)
        self.started = {0: [], 1: [], 2: [], "small": []}
        self.waiting = [(kind, offset) for kind in range(3) for offset in (1, 3, 2)]
        order = tuple(self.waiting)
        self.events = [
            (FIRST_DUE + TICK * tick, step) + order[tick - step]
            for tick in range(len(order) + 2)
            for step in range(3)
            if 0 <= tick - step < len(order)
        ]
        self.clock = 0.0

    def start(self, kind, copy):
        copy.start()
        self.started[kind].append(copy)

    def sent(self, kind):
        for copy in self.started[kind]:
            copy.wait_send()
        self.started[kind] = []

    def rows(self, kind, t, d, start=0, size=SLICE):
        row = pl.multiple_of(slice_row(kind, t, d) + start, 16)
        return self.full[kind].at[pl.ds(row, size)]

    def z_copy(self, kind, offset, source, block=None):
        place = self.place
        if block is None:
            block = self.blocks[kind + 1].at[pl.ds(pl.multiple_of(place.d * SLICE, 16), SLICE)]
        return send(
            block,
            self.rows(kind, source, place.d),
            self.z_sem.at[0, kind, offset - 1],
            self.z_sem.at[1, kind, offset - 1],
            place.to_z(offset),
        )

    def z_start(self, count):
        place = self.place
        for kind, offset in self.waiting[:count]:
            if kind:
                self.start(kind, self.z_copy(kind, offset, place.t))
                continue

            @pl.when(place.d < 6)
            def _():
                rows = pl.ds(pl.multiple_of(place.d * SLICE, 16), SLICE)
                self.z_copy(0, offset, place.t, self.blocks[0].at[rows]).start()

            @pl.when(place.d >= 6)
            def _():
                rows = pl.ds(pl.multiple_of((place.d - 6) * SLICE, 16), SLICE)
                self.z_copy(0, offset, place.t, self.blocks[1].at[rows]).start()

            rows = pl.ds(0, SLICE)
            self.started[0].append(self.z_copy(0, offset, place.t, self.blocks[1].at[rows]))
        self.waiting = self.waiting[count:]

    def small_copy(self, offset, source):
        return send(
            self.small,
            self.small_all.at[source],
            self.small_sem.at[0, offset - 1],
            self.small_sem.at[1, offset - 1],
            self.place.to_z(offset),
        )

    def plane_copy(self, step, kind, offset, d, device, start=0, size=SLICE):
        rows = self.rows(kind, self.place.from_z(offset), d, start, size)
        return send(
            rows,
            rows,
            self.plane_sem.at[0, step, kind, offset - 1],
            self.plane_sem.at[1, step, kind, offset - 1],
            device,
        )

    def core_copy(self, step, kind, offset, d):
        rows = self.rows(kind, self.place.from_z(offset), d)
        return send(
            rows,
            rows,
            self.core_sem.at[0, step, kind, offset - 1],
            self.core_sem.at[1, step, kind, offset - 1],
            self.place.to_core,
        )

    def own_copy(self, index):
        t, sem = self.place.t, self.own_sem.at[index]
        if index == 0:
            return pltpu.make_async_copy(self.small, self.small_all.at[t], sem)
        if index < 3:
            rows = pl.ds(pl.multiple_of(t * WIDTH, 16), WIDTH)
            return pltpu.make_async_copy(self.blocks[index + 1], self.full[index].at[rows], sem)
        part = index - 3
        rows = pl.ds(pl.multiple_of(part * WIDTH + t * 192, 16), 192)
        block = self.blocks[0].at[pl.ds(part * 192, 192)] if part < 3 else self.blocks[1]
        return pltpu.make_async_copy(block, self.full[0].at[rows], sem)

    def begin(self):
        self.z_start(2)
        for index in range(1, 7):
            self.own_copy(index).start()

    def small_start(self):
        self.own_copy(0).start()
        for offset in self.offsets:
            self.start("small", self.small_copy(offset, self.place.t))

    def advance(self, count=1):
        steps = (self.first, self.second, self.third)
        for due, step, kind, offset in self.events[:count]:
            self.clock = max(self.clock, due)
            steps[step](kind, offset)
        self.events = self.events[count:]

    def spend(self, duration):
        self.clock += duration
        while self.events and self.events[0][0] <= self.clock:
            self.advance()

    def advance_kind(self, kind, offset=None):
        while any(event[2] == kind and offset in (None, event[3]) for event in self.events):
            self.advance()
        for which in self.offsets if offset is None else (offset,):
            self.last(kind, which)

    def small_ready(self):
        self.own_copy(0).wait()
        for offset in self.offsets:
            self.small_copy(offset, self.place.from_z(offset)).wait_recv()

    def first(self, kind, offset):
        place = self.place
        self.z_copy(kind, offset, place.from_z(offset), self.blocks[1].at[0:SLICE]).wait_recv()
        self.start(kind, self.plane_copy(0, kind, offset, place.d, place.to_x))
        self.start(kind, self.plane_copy(1, kind, offset, place.d, place.to_y))
        self.start(kind, self.core_copy(0, kind, offset, place.d))
        self.z_start(1)

    def second(self, kind, offset):
        place = self.place
        self.plane_copy(0, kind, offset, place.d_x, place.to_x).wait_recv()
        self.start(kind, self.plane_copy(2, kind, offset, place.d_x, place.to_y, HALF, HALF))
        self.start(kind, self.core_copy(1, kind, offset, place.d_x))
        self.plane_copy(1, kind, offset, place.d_y, place.to_y).wait_recv()
        self.start(kind, self.plane_copy(3, kind, offset, place.d_y, place.to_x, 0, HALF))
        self.start(kind, self.core_copy(2, kind, offset, place.d_y))

    def third(self, kind, offset):
        place = self.place
        self.plane_copy(2, kind, offset, place.d_xy, place.to_y, HALF, HALF).wait_recv()
        self.plane_copy(3, kind, offset, place.d_xy, place.to_x, 0, HALF).wait_recv()
        self.start(kind, self.core_copy(3, kind, offset, place.d_xy))

    def last(self, kind, offset):
        place = self.place
        for step, d in enumerate((place.d, place.d_x, place.d_y, place.d_xy)):
            self.core_copy(step, kind, offset, place.core_of(d)).wait_recv()

    def own_ready(self, kind):
        for index in range(3, 7) if kind == 0 else (kind,):
            self.own_copy(index).wait()


DOWN, UP, FIRST = 0, 1, 2
STRAIGHT = (UP, FIRST)


class Reduce:
    def __init__(self, place, parts, bufs, outs, sems):
        self.place, self.parts, self.outs = place, parts, outs
        (self.core_in, self.one_in, self.near_in, self.far_in, self.two_in, self.z_in) = bufs
        (
            self.core_sem, self.one_sem, self.near_sem, self.far_sem, self.two_sem, self.z_sem,
            self.plane_sem, self.back_sem, self.free_sem,
        ) = sems
        t = place.t
        near, far = t + 1 - 2 * lax.rem(t, 2), t + 2 - 4 * (t // 2)
        self.blocks = (near, far + 1 - 2 * lax.rem(t, 2), far, t)
        self.major = (place.x, place.y)
        self.minor = (place.y, place.x)
        self.to_major = (place.to_x, place.to_y)
        self.to_minor = (place.to_y, place.to_x)
        self.started = {DOWN: [], UP: [], FIRST: [], "out": []}

    def start(self, kind, copy):
        copy.start()
        self.started[kind].append(copy)

    def sent(self, kind):
        for copy in self.started[kind]:
            copy.wait_send()
        self.started[kind] = []
        if kind in STRAIGHT:
            for slot in range(3):
                for half in range(2):
                    self.z_copy(kind, slot, half).wait_send()

    def line(self, t):
        return (self.place.dp, t)

    def block(self, kind, group):
        return group if kind == FIRST else self.blocks[group]

    def cells(self, kind, core, group, half=None, major=None, minor=None):
        row, size = (core * 4 + self.block(kind, group)) * 8, 8
        if half is not None:
            row, size = row + half * 4 + major * 2, 2
        if minor is not None:
            row, size = row + minor, 1
        return self.parts[kind].at[pl.ds(pl.multiple_of(row * HALF, 16), size * HALF)]

    def own(self, kind, group, half, major=None, minor=None):
        major = self.major[half] if major is None else major
        return self.cells(kind, self.place.core, group, half, major, minor)

    def copy(self, sem, index, src, dst, device):
        return send(src, dst, sem.at[(0,) + index], sem.at[(1,) + index], device)

    def core_copy(self, kind, group):
        src = self.cells(kind, 1 - self.place.core, group)
        dst = self.core_in.at[1 if kind == UP else 0, group]
        return self.copy(self.core_sem, (kind, group), src, dst, self.place.to_core)

    def one_copy(self, kind, group, half):
        src = self.own(kind, group, half, 1 - self.major[half])
        dst = self.one_in.at[kind, group, half]
        return self.copy(self.one_sem, (kind, group, half), src, dst, self.to_major[half])

    def near_copy(self, kind, group, half):
        src, dst = self.own(kind, group, half), self.near_in.at[kind, group, half]
        return self.copy(self.near_sem, (kind, group, half), src, dst, self.line(self.blocks[0]))

    def far_copy(self, kind, half):
        src, dst = self.own(kind, 2, half), self.far_in.at[kind, half]
        return self.copy(self.far_sem, (kind, half), src, dst, self.line(self.blocks[2]))

    def two_copy(self, kind, group, half):
        src = self.own(kind, group, half, None, 1 - self.minor[half])
        dst = self.two_in.at[kind, group, half]
        return self.copy(self.two_sem, (kind, group, half), src, dst, self.to_minor[half])

    def z_copy(self, kind, slot, half, group=0):
        src = self.own(kind, group, half, None, self.minor[half])
        dst, device = self.z_in.at[kind, slot, half], self.line(self.block(kind, group))
        return self.copy(self.z_sem, (kind, slot, half), src, dst, device)

    def rows(self, kind, d, begin=0, size=SLICE):
        return self.outs[kind].at[pl.ds(pl.multiple_of(d * SLICE + begin, 16), size)]

    def plane_copy(self, step, kind, d, device, begin=0, size=SLICE):
        rows = self.rows(kind, d, begin, size)
        return self.copy(self.plane_sem, (step, kind), rows, rows, device)

    def back_copy(self, step, kind, d):
        rows = self.rows(kind, d)
        return self.copy(self.back_sem, (step, kind), rows, rows, self.place.to_core)

    def add(self, ref, addend):
        ref[...] = ref[...] + addend

    def cross(self, kind, group):
        if kind == FIRST and group == 0:
            pl.semaphore_wait(self.free_sem, 1)
        self.start(kind, self.core_copy(kind, group))

    def one(self, kind, group):
        self.core_copy(kind, group).wait_recv()
        for half in range(2):
            for major in range(2):
                rows = self.own(kind, group, half, major)
                slot, begin = 1 if kind == UP else 0, (half * 2 + major) * SLICE
                self.add(rows, self.core_in[slot, group, begin : begin + SLICE, :])
        for half in range(2):
            self.start(kind, self.one_copy(kind, group, half))
        if kind == DOWN and group == 3:
            pl.semaphore_signal(
                self.free_sem, inc=1, device_id=self.place.to_core, device_id_type=MESH
            )

    def two(self, kind, group):
        for half in range(2):
            self.one_copy(kind, group, half).wait_recv()
            self.add(self.own(kind, group, half), self.one_in[kind, group, half])
            if kind in STRAIGHT:
                self.start(kind, self.two_copy(kind, group, half))
            elif group < 2:
                self.start(kind, self.near_copy(kind, group, half))

    def three(self, kind, group):
        if kind not in STRAIGHT:
            return
        for half in range(2):
            self.two_copy(kind, group, half).wait_recv()
            rows = self.own(kind, group, half, None, self.minor[half])
            self.add(rows, self.two_in[kind, group, half])
        if kind != FIRST:
            for half in range(2) if group < 3 else ():
                self.z_copy(kind, group, half, group).start()
            return

        @pl.when(self.place.t != group)
        def _():
            slot = lax.rem(group - self.place.t + 4, 4) - 1
            for half in range(2):
                self.z_copy(kind, slot, half, group).start()

    def keep(self, kind, _):
        if kind in STRAIGHT:
            return
        for half in range(2):
            self.near_copy(kind, 1, half).wait_recv()
            self.add(self.own(kind, 2, half), self.near_in[kind, 1, half])
            self.start(kind, self.far_copy(kind, half))

    def mine(self, kind, _):
        if kind in STRAIGHT:
            return
        for half in range(2):
            self.near_copy(kind, 0, half).wait_recv()
            self.far_copy(kind, half).wait_recv()
            rows = self.own(kind, 3, half)
            total = rows[...].astype(F32) + self.near_in[kind, 0, half].astype(F32)
            rows[...] = (total + self.far_in[kind, half].astype(F32)).astype(LOW)
            self.start(kind, self.two_copy(kind, 3, half))

    def final(self, kind, _):
        place = self.place
        for half in range(2):
            mine = place.t if kind == FIRST else 3
            total = self.own(kind, mine, half, None, self.minor[half])[...].astype(F32)
            if kind in STRAIGHT:
                for slot in range(3):
                    self.z_copy(kind, slot, half).wait_recv()
                    total = total + self.z_in[kind, slot, half].astype(F32)
            else:
                self.two_copy(kind, 3, half).wait_recv()
                total = total + self.two_in[kind, 3, half].astype(F32)
            self.rows(kind, place.d, half * HALF, HALF)[...] = total.astype(LOW)
        self.start("out", self.plane_copy(0, kind, place.d, place.to_x))
        self.start("out", self.plane_copy(1, kind, place.d, place.to_y))
        self.start("out", self.back_copy(0, kind, place.d))

    def relay(self, kind, _):
        place = self.place
        self.plane_copy(0, kind, place.d_x, place.to_x).wait_recv()
        self.start("out", self.plane_copy(2, kind, place.d_x, place.to_y, HALF, HALF))
        self.start("out", self.back_copy(1, kind, place.d_x))
        self.plane_copy(1, kind, place.d_y, place.to_y).wait_recv()
        self.start("out", self.plane_copy(3, kind, place.d_y, place.to_x, 0, HALF))
        self.start("out", self.back_copy(2, kind, place.d_y))

    def back(self, kind, _):
        place = self.place
        self.plane_copy(2, kind, place.d_xy, place.to_y, HALF, HALF).wait_recv()
        self.plane_copy(3, kind, place.d_xy, place.to_x, 0, HALF).wait_recv()
        self.start("out", self.back_copy(3, kind, place.d_xy))

    def last(self, kind, _):
        place = self.place
        for step, d in enumerate((place.d, place.d_x, place.d_y, place.d_xy)):
            self.back_copy(step, kind, place.core_of(d)).wait_recv()


class Total:
    def __init__(self, place, stages, arrived, line_up, sems):
        self.place, self.stages, self.arrived, self.line_up = place, stages, arrived, line_up
        self.pair_sem, self.z_sem = sems
        self.started = []

    def pair_copy(self, step):
        device = (self.place.to_core, self.place.to_x, self.place.to_y)[step]
        sem = self.pair_sem
        return send(
            self.stages.at[step], self.arrived.at[step], sem.at[0, step], sem.at[1, step], device
        )

    def z_copy(self, offset, source):
        sem = self.z_sem
        return send(
            self.stages.at[3],
            self.line_up.at[source],
            sem.at[0, offset - 1],
            sem.at[1, offset - 1],
            self.place.to_z(offset),
        )

    def start(self, copy):
        copy.start()
        self.started.append(copy)

    def begin(self):
        self.start(self.pair_copy(0))

    def step(self, index):
        self.pair_copy(index).wait_recv()
        self.stages[index + 1] = self.stages[index] + self.arrived[index]
        if index < 2:
            self.start(self.pair_copy(index + 1))
        else:
            for offset in range(1, self.place.tp_size):
                self.start(self.z_copy(offset, self.place.t))
            self.line_up[self.place.t] = self.stages[3]

    def end(self):
        for offset in range(1, self.place.tp_size):
            self.z_copy(offset, self.place.from_z(offset)).wait_recv()
        total = self.line_up[0]
        for t in range(1, self.place.tp_size):
            total = total + self.line_up[t]
        return total

    def finish(self):
        for copy in self.started:
            copy.wait_send()


def part_row(core, t, half, y, x):
    cell = x * 2 + y if half == 0 else y * 2 + x
    return (((core * 4 + t) * 2 + half) * 4 + cell) * HALF


def store_rows(part, core, t, half, cell, begin, values):
    row = pl.multiple_of(part_row(core, t, half, cell // 2, cell % 2) + begin, 16)
    part[pl.ds(row, 16), :] = values.astype(LOW)


def store_part(part, base, values, t):
    for piece in range(values.shape[0] // 16):
        d, inner = divmod(base + piece * 16, SLICE)
        half, begin = divmod(inner, HALF)
        store_rows(part, d % 2, t, half, d // 2, begin, values[piece * 16 : piece * 16 + 16])


def store_first(part, section, base, values):
    for piece in range(values.shape[0] // 16):
        t, inner = divmod(base + piece * 16, 192)
        core, inner = divmod(inner, SLICE)
        half, begin = divmod(inner, HALF)
        store_rows(part, core, t, half, section, begin, values[piece * 16 : piece * 16 + 16])


def total_of(terms):
    result = None
    for term in terms:
        result = term if result is None else result + term
    return result


def feed_cot(cot, vec, feed_low, sums, page):
    for rows in chunks():
        values = cot[page, rows, :].astype(F32) * line(vec, FEED_SCALE)
        sums[DOWN_BIAS] += fold(values)
        feed_low[page, rows, :] = values.astype(LOW)


def down_grad(feed_low, hidden_low, part, t, column):
    grads = [
        dot(hidden_low[t, page, :, tile(column)], feed_low[page], TN) for page in range(PAGES)
    ]
    store_part(part, column * TILE, total_of(grads), t)


def pre_back(feed_low, full_down, slope, sums, t, column):
    row = pl.multiple_of(t * WIDTH + column * TILE, TILE)
    weight = full_down[pl.ds(row, TILE), :]
    folds = []
    for page in range(PAGES):
        pre_cot = dot(feed_low[page], weight, NT) * slope[t, page, :, tile(column)].astype(F32)
        folds.append(fold(pre_cot))
        slope[t, page, :, tile(column)] = pre_cot.astype(LOW)
    sums[UP_BIAS + t, :, tile(column)] = total_of(folds)


def up_back(second_t, pre_cot, part, t, column):
    grads = [dot(second_t[page, tile(column), :], pre_cot[t, page], NN) for page in range(PAGES)]
    store_part(part, column * TILE, total_of(grads), t)


def second_cot(pre_cot, full_up, result, t, column, fresh):
    row = pl.multiple_of(t * WIDTH + column * TILE, TILE)
    weight = full_up[pl.ds(row, TILE), :]
    for page in range(PAGES):
        term = dot(pre_cot[t, page], weight, NT)
        if fresh:
            result[page, :, tile(column)] = term
        else:
            result[page, :, tile(column)] += term


def norm_back(features, cot, gain, sums, gain_row, shift_row):
    norm, scale = norm_parts(features)
    sums[gain_row] += fold(cot * norm)
    sums[shift_row] += fold(cot)
    cot = cot * gain
    mean = jnp.mean(cot, axis=-1, keepdims=True)
    along = jnp.mean(cot * norm, axis=-1, keepdims=True)
    return scale * (cot - mean - norm * along)


def second_back(middle, result, cot, branch, vec, sums, branch_low, page):
    for rows in chunks():
        part = norm_back(
            middle[page, rows, :], result[page, rows, :], line(vec, GAIN_2), sums, GAIN_2, SHIFT_2
        )
        middle_cot = cot[page, rows, :].astype(F32) + part
        middle[page, rows, :] = middle_cot
        sums[ATT_SCALE] += fold(middle_cot * branch[page, rows, :])
        branch_cot = middle_cot * line(vec, ATT_SCALE)
        sums[OUT_BIAS] += fold(branch_cot)
        branch_low[page, rows, :] = branch_cot.astype(LOW)


def attended_back(branch_low, full_a, attended_cot, page):
    for column in range(3):
        rows = slice(3 * WIDTH + column * TILE, 3 * WIDTH + column * TILE + TILE)
        result = dot(branch_low[page], full_a[rows, :], NT)
        attended_cot[page, :, tile(column)] = result.astype(LOW)


def attend_back(heads, expo, scale, attended_cot, scores, page, pair):
    lanes = slice(pair * 128, pair * 128 + 128)
    query, key, value = (heads[part, page, :, lanes] for part in range(3))
    cot = attended_cot[page, :, lanes]
    lane = lax.broadcasted_iota(jnp.int32, (SEQ, 128), 1)
    zero = jnp.zeros_like(query)
    key_t = key.T
    query_cots, key_cots, value_cots = [], [], []
    for which in range(2):
        head = 2 * pair + which
        keep = lane < 64 if which == 0 else lane >= 64
        head_query, head_cot = jnp.where(keep, query, zero), jnp.where(keep, cot, zero)
        prob_cot = dot(value, head_cot, NT)
        columns = slice((head % 3) * TILE, (head % 3) * TILE + SEQ)
        probs = expo[head // 3, page, :, columns].astype(F32) * scale[page, head : head + 1, :]
        product = probs * prob_cot
        score_cot = product - probs * jnp.sum(product, axis=0, keepdims=True)
        for half, width in ((0, 128), (1, SEQ - 128)):
            rows = slice((half * HEADS + head) * SEQ, (half * HEADS + head + 1) * SEQ)
            scores[rows, 0:width] += score_cot[:, half * 128 : half * 128 + width]
        score_cot = score_cot.astype(LOW)
        value_cots.append(dot(probs.astype(LOW), head_cot, NN))
        key_cots.append(dot(score_cot, head_query, NN))
        query_cots.append(dot(key_t[64 * which : 64 * which + 64], score_cot, NN))
    heads[0, page, :, lanes] = (jnp.concatenate(query_cots, axis=0).T * 0.125).astype(LOW)
    heads[1, page, :, lanes] = total_of(key_cots).astype(LOW)
    heads[2, page, :, lanes] = total_of(value_cots).astype(LOW)


def section_back(heads, right, part, sums, section, half):
    columns = slice(half * 384, half * 384 + 384)
    pieces = [heads[section, page, :, columns] for page in range(PAGES)]
    grads = [dot(pieces[page], right[page], TN) for page in range(PAGES)]
    if section in (0, 2):
        index = Q_BIAS if section == 0 else V_BIAS
        sums[index, :, columns] = total_of([fold(piece.astype(F32)) for piece in pieces])
    store_first(part, section, half * 384, total_of(grads))


def first_cot(heads, full_a, result, page):
    for column in range(3):
        terms = [
            dot(heads[part, page], full_a[part * WIDTH : (part + 1) * WIDTH, tile(column)], NN)
            for part in range(3)
        ]
        result[page, :, tile(column)] = total_of(terms)


def first_back(patches, hide, vec, result, middle, sums, page):
    for rows in chunks():
        features = enter(patches, hide, vec, page, rows)
        part = norm_back(
            features, result[page, rows, :], line(vec, GAIN_1), sums, GAIN_1, SHIFT_1
        )
        entered_cot = middle[page, rows, :] + part
        hidden = hide[rows, page : page + 1] > 0
        result[page, rows, :] = jnp.where(hidden, 0.0, entered_cot)
        sums[EMBED] += fold(jnp.where(hidden, entered_cot, 0.0))


def table_back(scores, index_t, packed, begin, end):
    row = lax.broadcasted_iota(jnp.int32, (128, TILE), 0)
    unroll = 20

    def step(index, total):
        lefts, rights = [], []
        for inner in range(unroll):
            key = index * unroll + inner
            halves = [
                scores[pl.ds(half * HEADS * SEQ + key, HEADS, stride=SEQ), :] for half in range(2)
            ]
            terms = jnp.concatenate(halves, axis=1)
            terms = jnp.concatenate([terms, jnp.zeros((4, TILE), F32)], axis=0)
            entry = index_t[pl.ds(key, 1), :]
            low_part, high_part = entry & 127, entry >> 7
            match = jnp.broadcast_to(low_part, (128, TILE)) == row
            rights.append(jnp.where(match, 1.0, 0.0).astype(LOW))
            picked = [jnp.where(high_part == part, terms, 0.0).astype(LOW) for part in range(6)]
            lefts.append(jnp.concatenate(picked, axis=0))
        return total + dot(jnp.concatenate(lefts, axis=1), jnp.concatenate(rights, axis=1), NT)

    total = lax.fori_loop(begin // unroll, end // unroll, step, jnp.zeros((96, 128), F32))
    for part in range(6):
        columns, rows = slice(part * 128, part * 128 + 128), slice(part * 16, part * 16 + 16)
        if begin:
            packed[16:32, columns] += total[rows]
        else:
            packed[16:32, columns] = total[rows]


def layer_kernel(tp_size, *refs):
    blocks = refs[:4]
    patches, cot, mask, index, table, bias_up, bias_qv = refs[4:11]
    vec_in = refs[11:20]
    sums_out, total_out = refs[20:23], refs[23]
    output, patch_out, expo_out, heads_out, hidden_out = refs[24:29]
    outs, refs = refs[29:32], refs[32:]
    full, small_all, small = refs[0:3], refs[3], refs[4]
    wide, inner, parts = refs[5:8]
    bufs = refs[8:14]
    scores_t, branch, middle, result, second_t, first_low, second_low, feed_low = refs[14:22]
    sums, stages, arrived, line_up = refs[22:26]
    vec, hide, index_t, scale, bias_rows, up_bias = refs[26:32]
    local_sem = refs[32]
    gather_sems, reduce_sems, total_sems = refs[33:38], refs[38:47], refs[47:49]
    place = Place(tp_size)
    gather = Gather(place, blocks, small, full, small_all, gather_sems)
    reduce = Reduce(place, (parts.at[0], parts.at[1], full[1]), bufs, outs, reduce_sems)
    total = Total(place, stages, arrived, line_up, total_sems)
    pair_bias = scores = scores_t

    def local(index, src, dst):
        return pltpu.make_async_copy(src, dst, local_sem.at[index])

    greet(place)
    small[0:3, 0:NUM_REL] = table[...].astype(F32)
    small[3:4, :] = bias_up[...].astype(F32).reshape(1, WIDTH)
    small[4:6, 0:192] = bias_qv[...].astype(F32)
    for row, values in enumerate(vec_in):
        vec[row : row + 1, :] = values[...].reshape(1, WIDTH)
    meet(place)
    gather.begin()
    gather.small_start()
    place_in_page = lax.broadcasted_iota(jnp.int32, (PAGES, SEQ), 1)
    patch = (place_in_page >= 1) & (place_in_page <= PATCHES)
    pages = [mask[pl.ds(SEQ * page, SEQ)].reshape(1, SEQ) for page in range(PAGES)]
    hidden = jnp.where((jnp.concatenate(pages, axis=0) > 0) & patch, 1.0, 0.0)
    hide[...] = jnp.concatenate([hidden, jnp.zeros((8 - PAGES, SEQ), F32)], axis=0).T
    index_t[...] = jnp.zeros_like(index_t)
    index_t[:, 0:SEQ] = index[...].astype(F32).T.astype(jnp.int32)
    sums[...] = jnp.zeros_like(sums)
    for page in range(PAGES):
        first_norm(patches, hide, vec, first_low, page)
    gather.small_ready()
    for t in range(tp_size):
        columns = slice(192 * t, 192 * t + 192)
        up_bias[t : t + 1, :] = small_all[t, 3:4, :]
        bias_rows[0:1, columns] = small_all[t, 4:5, 0:192]
        bias_rows[1:2, columns] = small_all[t, 5:6, 0:192]
    gather.spend(4.0)
    for head in range(HEADS):
        lookup(small_all, index_t, pair_bias, head)
        gather.spend(0.7)
    gather.advance_kind(0)
    gather.own_ready(0)
    for part in range(3):
        for column in range(3):
            project(first_low, full[0], bias_rows, inner, part, column)
            gather.spend(0.4)
    saves = []
    for page in range(PAGES):
        for pair in range(HEADS // 2):
            attend(inner, pair_bias, wide, scale, page, pair)
            if pair % 3 == 2:
                gather.spend(1.4)
        for index, (src, dst) in enumerate(((wide, expo_out), (inner, heads_out))):
            saves.append(local(10 + 2 * page + index, src.at[:, page], dst.at[:, page]))
            saves[-1].start()
    for page in range(PAGES):
        out_project(inner, full[0], vec, patches, hide, branch, middle, page)
        second_norm(middle, vec, second_low, page)
        gather.spend(0.9)
        second_t[page] = second_low[page].T
        feed_cot(cot, vec, feed_low, sums, page)
        gather.spend(0.4)
    for copy in saves:
        copy.wait()
    gather.advance_kind(1)
    gather.own_ready(1)
    for t in range(tp_size):
        for column in range(3):
            feed_up(second_low, full[1], up_bias, wide, inner, t, column)
            gather.spend(0.4)
    hidden_copy = local(2, wide, hidden_out)
    hidden_copy.start()
    for group in range(4):
        for column in range(3):
            down_grad(feed_low, wide, parts.at[DOWN], reduce.blocks[group], column)
            gather.spend(0.35)
        reduce.cross(DOWN, group)
    hidden_copy.wait()
    expo_load = local(3, expo_out, wide)
    expo_load.start()

    def run(*events):
        for step, kind, group in events:
            step(kind, group)

    cross, one, two, three = reduce.cross, reduce.one, reduce.two, reduce.three
    keep, mine, final = reduce.keep, reduce.mine, reduce.final
    relay, back, last = reduce.relay, reduce.back, reduce.last

    def block_back(offset):
        t = place.from_z(offset)
        for column in range(3):
            pre_back(feed_low, full[2], inner, sums, t, column)
        gather.spend(1.2)
        for column in range(3):
            up_back(second_t, inner, parts.at[UP], t, column)
        gather.spend(1.2)
        for column in range(3):
            second_cot(inner, full[1], result, t, column, offset == 0)
        gather.spend(1.2)

    scores[...] = jnp.zeros_like(scores)
    gather.own_ready(2)
    block_back(0)
    run((one, DOWN, 0), (one, DOWN, 1), (one, DOWN, 2), (one, DOWN, 3))
    run((cross, UP, 3),)
    gather.advance_kind(2, 1)
    block_back(1)
    gather.advance_kind(2, 3)
    block_back(3)
    run((cross, UP, 0), (cross, UP, 1))
    gather.advance(len(gather.events))
    gather.advance_kind(2, 2)
    block_back(2)
    run((cross, UP, 2), (one, UP, 0), (one, UP, 1))
    heads_loads = [
        local((0, 1, 4)[page], heads_out.at[:, page], inner.at[:, page]) for page in range(PAGES)
    ]
    for copy in heads_loads:
        copy.start()
    branch_low, attended_cot = feed_low, second_low
    for page in range(PAGES):
        second_back(middle, result, cot, branch, vec, sums, branch_low, page)
    run((one, UP, 2), (one, UP, 3))
    for page in range(PAGES):
        attended_back(branch_low, full[0], attended_cot, page)
    gather.sent(1)
    expo_load.wait()
    after_attend = (
        (),
        ((two, DOWN, 0),),
        ((two, DOWN, 1),),
        ((one, FIRST, 0), (two, DOWN, 2)),
        ((one, FIRST, 1), (two, DOWN, 3)),
        (),
    )
    for half in range(2):
        for page in range(PAGES):
            if half == 0:
                heads_loads[page].wait()
            for pair in range(3 * half, 3 * half + 3):
                attend_back(inner, wide, scale, attended_cot, scores, page, pair)
            run(*after_attend[3 * half + page])
        for section in (3, 0, 1, 2):
            right = branch_low if section == 3 else first_low
            section_back(inner, right, full[1], sums, section, half)
        run((cross, FIRST, 2 * half), (cross, FIRST, 2 * half + 1))
    hidden_load = local(2, hidden_out, wide)
    hidden_load.start()
    after_cot = (
        ((one, FIRST, 2), (two, UP, 0)),
        ((one, FIRST, 3), (two, UP, 1)),
        ((keep, DOWN, 0),),
    )
    for page in range(PAGES):
        first_cot(inner, full[0], result, page)
        run(*after_cot[page])
    after_first = (((three, UP, 0),), ((two, UP, 2), (three, UP, 1)), ((two, UP, 3),))
    for page in range(PAGES):
        first_back(patches, hide, vec, result, middle, sums, page)
        run(*after_first[page])
    patch_copy = local(5, result, patch_out)
    patch_copy.start()
    hidden_load.wait()
    after_feed = (((three, UP, 2),), ((three, UP, 3),), ((two, FIRST, 0),))
    for page in range(PAGES):
        feed_down(wide, full[2], vec, patches, hide, cot, branch, sums, tp_size, page)
        run(*after_feed[page])
    output_copy = local(9, branch, output)
    output_copy.start()
    table_back(scores, index_t, stages.at[0], 0, 100)
    run((mine, DOWN, 0), (two, FIRST, 1), (three, FIRST, 0))
    table_back(scores, index_t, stages.at[0], 100, 200)
    stages[0, 0:16, :] = jnp.sum(sums[...], axis=1)
    total.begin()
    run((two, FIRST, 2), (three, FIRST, 1), (final, DOWN, 0))
    total.step(0)
    run((two, FIRST, 3), (three, FIRST, 2), (relay, DOWN, 0), (final, UP, 0))
    total.step(1)
    run((three, FIRST, 3), (back, DOWN, 0), (relay, UP, 0))
    total.step(2)
    run((final, FIRST, 0), (back, UP, 0), (last, DOWN, 0))
    total_out[...] = total.end()
    run((relay, FIRST, 0), (last, UP, 0), (back, FIRST, 0), (last, FIRST, 0))
    sum_copies = [local(6 + kind, outs[kind], sums_out[kind]) for kind in range(3)]
    for copy in sum_copies:
        copy.start()
    patch_copy.wait()
    output_copy.wait()
    for kind in (DOWN, UP, FIRST, "out"):
        reduce.sent(kind)
    for kind in (0, 2, "small"):
        gather.sent(kind)
    total.finish()
    for copy in sum_copies:
        copy.wait()


ANY = pl.BlockSpec(memory_space=pl.ANY)
VMEM = pl.BlockSpec(memory_space=pltpu.VMEM)


def layer(blocks, local_args, vec_rows, tp_size):
    dma, regular = pltpu.SemaphoreType.DMA, pltpu.SemaphoreType.REGULAR
    shape, scratch = jax.ShapeDtypeStruct, pltpu.VMEM
    page_shape = (PAGES, SEQ, WIDTH)
    quarter = (SLICE, WIDTH)
    return pl.pallas_call(
        functools.partial(layer_kernel, tp_size),
        out_shape=[shape((WIDTH, WIDTH), LOW)] * 3
        + [
            shape((32, WIDTH), F32),
            shape(page_shape, F32),
            shape(page_shape, F32),
        ]
        + [shape((4,) + page_shape, LOW)] * 3,
        in_specs=[ANY] * 4 + [VMEM] * 16,
        out_specs=[ANY] * 3 + [VMEM] + [ANY] * 5,
        scratch_shapes=[scratch((WIDTH, WIDTH), LOW)] * 3
        + [scratch((tp_size * WIDTH, WIDTH), LOW)] * 3
        + [
            scratch((tp_size, 8, WIDTH), F32),
            scratch((8, WIDTH), F32),
            scratch((4,) + page_shape, LOW),
            scratch((4,) + page_shape, LOW),
            scratch((2, 32 * SLICE, WIDTH), LOW),
            scratch((2, 4, 4 * SLICE, WIDTH), LOW),
            scratch((3, 4, 2) + quarter, LOW),
            scratch((2, 2, 2) + quarter, LOW),
            scratch((2, 2) + quarter, LOW),
            scratch((3, 4, 2, HALF, WIDTH), LOW),
            scratch((3, 3, 2, HALF, WIDTH), LOW),
            scratch((2 * HEADS * SEQ, 128), F32),
            scratch(page_shape, F32),
            scratch(page_shape, F32),
            scratch(page_shape, F32),
            scratch((PAGES, WIDTH, SEQ), LOW),
            scratch(page_shape, LOW),
            scratch(page_shape, LOW),
            scratch(page_shape, LOW),
            scratch((16, 8, WIDTH), F32),
            scratch((4, 32, WIDTH), F32),
            scratch((3, 32, WIDTH), F32),
            scratch((tp_size, 32, WIDTH), F32),
            scratch((16, WIDTH), F32),
            scratch((SEQ, 8), F32),
            scratch((SEQ, TILE), jnp.int32),
            scratch((PAGES, 16, SEQ), F32),
            scratch((8, WIDTH), F32),
            scratch((8, WIDTH), F32),
            dma((16,)),
            dma((7,)),
            dma((2, 3, tp_size - 1)),
            dma((2, tp_size - 1)),
            dma((2, 4, 3, tp_size - 1)),
            dma((2, 4, 3, tp_size - 1)),
            dma((2, 3, 4)),
            dma((2, 3, 4, 2)),
            dma((2, 2, 2, 2)),
            dma((2, 2, 2)),
            dma((2, 3, 4, 2)),
            dma((2, 3, 3, 2)),
            dma((2, 4, 3)),
            dma((2, 4, 3)),
            regular,
            dma((2, 3)),
            dma((2, tp_size - 1)),
        ],
        compiler_params=pltpu.CompilerParams(
            collective_id=0, has_side_effects=True, vmem_limit_bytes=64 * 1024 * 1024 - 65536
        ),
    )(*blocks, *local_args, *vec_rows)


def finish_kernel(tp_size, *refs):
    sums, totals, output, patch = refs[:3], *refs[3:6]
    project_out, output_out, up_out, down_out, layer_out, patch_out = refs[6:12]
    rows_out, bias_out, table_out, bias_up = refs[12:21], *refs[21:24]
    low, wide, total, pages, sem = refs[24:29]
    loads = [pltpu.make_async_copy(totals, total, sem.at[0])]
    for kind in range(3):
        loads.append(pltpu.make_async_copy(sums[kind], low.at[kind], sem.at[1 + kind]))
    loads.append(pltpu.make_async_copy(output, pages.at[0], sem.at[4]))
    loads.append(pltpu.make_async_copy(patch, pages.at[1], sem.at[5]))
    for copy in loads[4:] + loads[:4]:
        copy.start()
    copies = []
    for index, target in enumerate((layer_out, patch_out)):
        loads[4 + index].wait()
        copies.append(
            pltpu.make_async_copy(pages.at[index], target, sem.at[6 + len(copies)])
        )
        copies[-1].start()
    for kind, target in enumerate((down_out, up_out, None)):
        loads[1 + kind].wait()
        for part in range(4):
            rows = slice(part * 192, part * 192 + 192)
            wide[kind, rows, :] = low[kind, rows, :].astype(F32)
            if kind < FIRST:
                dst = target.at[rows]
            else:
                dst = project_out.at[rows] if part < 3 else output_out
            copies.append(
                pltpu.make_async_copy(wide.at[kind, rows], dst, sem.at[6 + len(copies)])
            )
            copies[-1].start()
    loads[0].wait()
    for row, target in enumerate(rows_out):
        target[...] = total[row : row + 1, :].reshape(WIDTH)
    for t in range(tp_size):

        @pl.when(lax.axis_index("tp") == t)
        def _():
            bias_out[...] = total[Q_BIAS : Q_BIAS + 2, 192 * t : 192 * t + 192]
            table_out[...] = total[16 + 3 * t : 19 + 3 * t, 0:NUM_REL]
            bias_up[...] = total[UP_BIAS + t : UP_BIAS + t + 1, :].reshape(WIDTH)

    for copy in copies:
        copy.wait()


def finish(values, tp_size):
    shape = jax.ShapeDtypeStruct
    page_shape = (PAGES, SEQ, WIDTH)
    return pl.pallas_call(
        functools.partial(finish_kernel, tp_size),
        out_shape=[
            shape((3 * 192, WIDTH), F32),
            shape((192, WIDTH), F32),
            shape((WIDTH, WIDTH), F32),
            shape((WIDTH, WIDTH), F32),
            shape(page_shape, F32),
            shape(page_shape, F32),
        ]
        + [shape((WIDTH,), F32)] * 9
        + [shape((2, 192), F32), shape((3, NUM_REL), F32), shape((WIDTH,), F32)],
        in_specs=[ANY] * 6,
        out_specs=[ANY] * 6 + [VMEM] * 12,
        scratch_shapes=[
            pltpu.VMEM((3, WIDTH, WIDTH), values[0].dtype),
            pltpu.VMEM((3, WIDTH, WIDTH), F32),
            pltpu.VMEM((32, WIDTH), F32),
            pltpu.VMEM((2,) + page_shape, F32),
            pltpu.SemaphoreType.DMA((20,)),
        ],
        compiler_params=pltpu.CompilerParams(vmem_limit_bytes=63 << 20),
    )(*values)


def body(tp_size, dp_size, *args):
    (
        patches, page_mask, pair_index, mask_embed, first_gain, first_shift, project_weight,
        project_bias, pair_table, output_weight, output_bias, attention_scale, second_gain,
        second_shift, up_weight, up_bias, down_weight, down_bias, feed_scale, cotangent,
    ) = args
    row_count = patches.shape[0]
    project_rows = jnp.transpose(project_weight, (1, 2, 0)).reshape(3 * 192, WIDTH)
    vec_rows = (
        mask_embed, first_gain, first_shift, output_bias, attention_scale, second_gain,
        second_shift, down_bias, feed_scale,
    )
    local_args = (
        patches.reshape(PAGES, SEQ, WIDTH),
        cotangent.reshape(PAGES, SEQ, WIDTH),
        page_mask,
        pair_index,
        jnp.transpose(pair_table),
        up_bias,
        project_bias,
    )
    values = layer(
        (project_rows, output_weight, up_weight, down_weight),
        local_args,
        vec_rows,
        tp_size,
    )[:6]
    if dp_size > GROUP:
        groups = [[i + GROUP * j for j in range(dp_size // GROUP)] for i in range(GROUP)]
        sums = [value.astype(F32) for value in values[:4]]
        values = list(lax.psum(sums, "dp", axis_index_groups=groups)) + list(values[4:])
    results = finish(values, tp_size)
    project_sum, output_sum, up_sum, down_sum, layer_output, patch_gradient = results[:6]
    rows = results[6:15]
    bias_sum, table_sum, up_bias_sum = results[15:]
    return (
        layer_output.reshape(row_count, WIDTH),
        patch_gradient.reshape(row_count, WIDTH),
        rows[EMBED],
        rows[GAIN_1],
        rows[SHIFT_1],
        jnp.transpose(project_sum.reshape(3, 192, WIDTH), (2, 0, 1)),
        bias_sum,
        jnp.transpose(table_sum),
        output_sum,
        rows[OUT_BIAS],
        rows[ATT_SCALE],
        rows[GAIN_2],
        rows[SHIFT_2],
        up_sum,
        up_bias_sum,
        down_sum,
        rows[DOWN_BIAS],
        rows[FEED_SCALE],
    )


def solution(mesh):
    rows, heads = P(("dp", "tp"), None), P(None, "tp")
    in_specs = (
        rows, P(("dp", "tp")), P(), P(), P(), P(), P(None, None, "tp"), heads, heads,
        P("tp", None), P(), P(), P(), P(), heads, P("tp"), P("tp", None), P(), P(), rows,
    )
    out_specs = (
        rows, rows, P(), P(), P(), P(None, None, "tp"), heads, heads, P("tp", None), P(), P(),
        P(), P(), heads, P("tp"), P("tp", None), P(), P(),
    )
    step = functools.partial(body, mesh.shape["tp"], mesh.shape["dp"])
    return jax.shard_map(step, mesh=mesh, in_specs=in_specs, out_specs=out_specs, check_vma=False)
```
